256 devices in a mesh: tm: 128 (over x, z, y), rep: 2 (over core).
Axes of the slice: x: 4, y: 4, z: 8, core: 2. Of those that a mesh axis runs over, the one named last changes fastest.
Arguments:
- table: bfloat16 [2, 32768, 512], P(None, 'tm'), may hold values from -30 to 30
- cotangent: bfloat16 [2, 32768, 512], P(None, 'tm'), may hold values from -6 to 6
- stamps: int32 [2, 32768], P(None, 'tm'), may hold values from 0 to 98304, as said below
- starts: int32 [2, 32768], P(None, 'tm'), may hold values from 0 to 65535, as said below
- w_query: bfloat16 [512, 512], P(None, 'rep'), may hold values from -0.5 to 0.5
- w_key: bfloat16 [512, 512], P(None, 'rep'), may hold values from -0.5 to 0.5
- w_value: bfloat16 [512, 512], P(None, 'rep'), may hold values from -0.25 to 0.25
- w_out: bfloat16 [512, 512], P('rep'), may hold values from -0.25 to 0.25
- decay: float32 [4], P('rep'), may hold values from 0.0002 to 0.02
Outputs:
- mixed: bfloat16 [2, 32768, 512], P(None, 'tm')
- grad_table: bfloat16 [2, 32768, 512], P(None, 'tm')
- grad_query: float32 [512, 512], P(None, 'rep')
- grad_key: float32 [512, 512], P(None, 'rep')
- grad_value: float32 [512, 512], P(None, 'rep')
- grad_out: float32 [512, 512], P('rep')
The draws below stay inside these ranges and needn't reach their ends.
Inputs may be any that keep to these rules, and one draw needn't show every extreme that they name: In time order the stamps never fall, successive rows differ by 0 to 3, the first row has stamp 0 and the last row has stamp 3 * 32768. For the row r in time order, starts lies between max(0, (r // 256 - 2) * 256) and r; the first row of each block reaches the lower end and the last row of each block starts at itself.
All inputs are finite; a program needn't handle non-finite values.
Results may differ from the reference program's by a relative error of at most 0.0045.
The reference program's roundings to bfloat16 on the way count: a program that leaves them out, or rounds other values in their place, can miss the bound.
Values may be sent and summed in bfloat16 or wider, within the bound.
A program may use at most 64 MiB of HBM per device.

```python
import math
import jax
import jax.numpy as jnp
from jax import lax

D = 512
HEADS = 4
HD = 128
BLK = 256
ROWS = 65536


def fold_rows(ordered):
    tail = ordered.shape[1:]
    half = ROWS // (2 * BLK)
    blocks = ordered.reshape((2 * half, BLK) + tail)
    lower = blocks[:half].reshape((half * BLK,) + tail)
    upper = blocks[half:][::-1].reshape((half * BLK,) + tail)
    return jnp.stack([lower, upper])


def draw_table(key, part):
    noise = jax.random.normal(jax.random.fold_in(key, 1), (ROWS, D), jnp.float32)
    noise = jnp.clip(noise, -6.0, 6.0)
    return fold_rows(noise).astype(jnp.bfloat16)


def weight_pair(key):
    base = jax.random.normal(jax.random.fold_in(key, 31), (D, D), jnp.float32) / math.sqrt(D)
    other = jax.random.normal(jax.random.fold_in(key, 32), (D, D), jnp.float32) / math.sqrt(D)
    paired = other
    return (jnp.clip(base, -0.5, 0.5), jnp.clip(paired, -0.5, 0.5))


def draw_w_query(key, part):
    return weight_pair(key)[0].astype(jnp.bfloat16)


def draw_w_key(key, part):
    return weight_pair(key)[1].astype(jnp.bfloat16)


def draw_stamps(key, part):
    pair_count = ROWS // 2 - 1
    firsts = jax.random.randint(jax.random.fold_in(key, 41), (pair_count,), 0, 4, dtype=jnp.int32)
    paired = jnp.stack([firsts, 3 - firsts], 1).reshape(2 * pair_count)
    gaps = jnp.concatenate([jnp.full((1,), 3, jnp.int32), paired, jnp.zeros((1,), jnp.int32)])
    times = jnp.cumsum(gaps).astype(jnp.int32) - gaps
    return fold_rows(times)


def draw_starts(key, part):
    row_ids = jnp.arange(ROWS, dtype=jnp.int32)
    blk_ids = row_ids // BLK
    lowest = jnp.maximum(0, (blk_ids - 2) * BLK)
    span = row_ids - lowest
    modes = jax.random.randint(jax.random.fold_in(key, 51), (ROWS // BLK,), 0, 3, dtype=jnp.int32)[blk_ids]
    raw = jax.random.randint(jax.random.fold_in(key, 52), (ROWS,), 0, 1 << 20, dtype=jnp.int32)
    short = raw % jnp.minimum(span + 1, 48)
    spread = raw % (span + 1)
    back = jnp.where(modes == 0, short, jnp.where(modes == 1, spread, span))
    back = jnp.where(row_ids % BLK == 0, span, back)
    back = jnp.where(row_ids % BLK == BLK - 1, 0, back)
    return fold_rows((row_ids - back).astype(jnp.int32))


def level_of(rng, extent, cuts, least, high):
    loudness = 1.0
    for dim, shards_of in cuts:
        heights = jax.random.uniform(jax.random.fold_in(jax.random.fold_in(rng, 6), dim), (shards_of,), jnp.float32, least / len(cuts), high / len(cuts))
        loudness = loudness * jnp.repeat(jnp.exp(heights), extent[dim] // shards_of).reshape((-1,) + (1,) * (len(extent) - 1 - dim))
    return loudness


def gaussian(stream_key, shape, scale, reach, shards=(), kind=jnp.bfloat16):
    values = scale * jax.random.normal(stream_key, shape, jnp.float32)
    if shards:
        values = values * level_of(stream_key, shape, shards, -0.22, 0.18)
    return jnp.clip(values, -reach, reach).astype(kind)


def setup_inputs(seed: int = 0) -> dict:
    arg_keys = jax.random.split(jax.random.key(seed), 10)
    table = draw_table(jax.random.fold_in(arg_keys[9], 71), 0)
    cotangent = gaussian(arg_keys[1], (2, ROWS // 2, D), 1.0, 6.0, ((1, 128),))
    stamps = draw_stamps(jax.random.fold_in(arg_keys[9], 71), 0)
    starts = draw_starts(jax.random.fold_in(arg_keys[9], 71), 0)
    w_query = draw_w_query(jax.random.fold_in(arg_keys[9], 71), 0)
    w_key = draw_w_key(jax.random.fold_in(arg_keys[9], 71), 0)
    w_value = gaussian(arg_keys[6], (D, D), D ** -0.5, 0.25, ((1, 2),))
    w_out = gaussian(arg_keys[7], (D, D), D ** -0.5, 0.25, ((0, 2),))
    decay = jnp.clip(jnp.exp(math.log(0.02) - 4.6051702 * jax.random.uniform(arg_keys[8], (HEADS,), jnp.float32) ** level_of(arg_keys[8], (HEADS,), ((0, 2),), -0.2, 0.2)), 0.0002, 0.02)
    return {"table": table, "cotangent": cotangent, "stamps": stamps, "starts": starts, "w_query": w_query, "w_key": w_key, "w_value": w_value, "w_out": w_out, "decay": decay}


def unfold(folded):
    tail = folded.shape[2:]
    half = folded.shape[1] // BLK
    lower = folded[0].reshape((half, BLK) + tail)
    upper = folded[1].reshape((half, BLK) + tail)[::-1]
    return jnp.concatenate([lower, upper], 0).reshape((2 * half * BLK,) + tail)

def fold_back(ordered):
    tail = ordered.shape[1:]
    half = ordered.shape[0] // (2 * BLK)
    blocks = ordered.reshape((2 * half, BLK) + tail)
    lower = blocks[:half].reshape((half * BLK,) + tail)
    upper = blocks[half:][::-1].reshape((half * BLK,) + tail)
    return jnp.stack([lower, upper])

def reference(table, cotangent, stamps, starts, w_query, w_key, w_value, w_out, decay):
    rows = unfold(table)
    grad_y = unfold(cotangent)
    times = unfold(stamps)
    firsts = unfold(starts)
    total = rows.shape[0]
    blocks_all = total // BLK
    queries = jnp.dot(rows, w_query, preferred_element_type=jnp.float32).astype(jnp.bfloat16)
    key_rows = jnp.dot(rows, w_key, preferred_element_type=jnp.float32).astype(jnp.bfloat16)
    val_rows = jnp.dot(rows, w_value, preferred_element_type=jnp.float32).astype(jnp.bfloat16)
    grad_attn = jnp.dot(grad_y, w_out.T, preferred_element_type=jnp.float32).astype(jnp.bfloat16)
    inv_scale = 1.0 / math.sqrt(HD)
    margin = 2 * BLK
    key_pad = jnp.pad(key_rows, ((margin, 0), (0, 0)))
    val_pad = jnp.pad(val_rows, ((margin, 0), (0, 0)))
    time_pad = jnp.pad(times, (margin, 0))

    def step(carry, blk_id):
        key_acc, val_acc = carry
        row_zero = blk_id * BLK
        q_heads = lax.dynamic_slice_in_dim(queries, row_zero, BLK, 0).reshape(BLK, HEADS, HD).astype(jnp.float32)
        k_heads = lax.dynamic_slice_in_dim(key_pad, row_zero, 3 * BLK, 0).reshape(3 * BLK, HEADS, HD).astype(jnp.float32)
        v_heads = lax.dynamic_slice_in_dim(val_pad, row_zero, 3 * BLK, 0).reshape(3 * BLK, HEADS, HD).astype(jnp.float32)
        g_heads = lax.dynamic_slice_in_dim(grad_attn, row_zero, BLK, 0).reshape(BLK, HEADS, HD).astype(jnp.float32)
        q_times = lax.dynamic_slice_in_dim(times, row_zero, BLK, 0)
        k_times = lax.dynamic_slice_in_dim(time_pad, row_zero, 3 * BLK, 0)
        q_first = lax.dynamic_slice_in_dim(firsts, row_zero, BLK, 0)
        q_pos = row_zero + jnp.arange(BLK, dtype=jnp.int32)
        k_pos = row_zero - margin + jnp.arange(3 * BLK, dtype=jnp.int32)
        allowed = (k_pos[None, :] >= q_first[:, None]) & (k_pos[None, :] <= q_pos[:, None])
        time_gap = (q_times[:, None] - k_times[None, :]).astype(jnp.float32)
        scores = jnp.einsum('qhd,khd->hqk', q_heads, k_heads) * inv_scale - decay[:, None, None] * time_gap[None]
        scores = jnp.where(allowed[None], scores, -1e+30)
        row_max = lax.optimization_barrier(jnp.max(scores, -1, keepdims=True))
        weights = jnp.where(allowed[None], jnp.exp(scores - row_max), 0.0)
        probs = weights / lax.optimization_barrier(jnp.sum(weights, -1, keepdims=True))
        probs_low = probs.astype(jnp.bfloat16).astype(jnp.float32)
        attn = jnp.einsum('hqk,khd->qhd', probs_low, v_heads).astype(jnp.bfloat16)
        d_probs = jnp.einsum('qhd,khd->hqk', g_heads, v_heads)
        delta = lax.optimization_barrier(jnp.sum(probs * d_probs, -1, keepdims=True))
        d_scores = (probs * (d_probs - delta)).astype(jnp.bfloat16).astype(jnp.float32)
        d_query = (jnp.einsum('hqk,khd->qhd', d_scores, k_heads) * inv_scale).astype(jnp.bfloat16)
        d_key = jnp.einsum('hqk,qhd->khd', d_scores, q_heads) * inv_scale
        d_value = jnp.einsum('hqk,qhd->khd', probs_low, g_heads)
        old_key = lax.dynamic_slice_in_dim(key_acc, row_zero, 3 * BLK, 0)
        key_acc = lax.dynamic_update_slice_in_dim(key_acc, old_key + d_key.reshape(3 * BLK, D), row_zero, 0)
        old_val = lax.dynamic_slice_in_dim(val_acc, row_zero, 3 * BLK, 0)
        val_acc = lax.dynamic_update_slice_in_dim(val_acc, old_val + d_value.reshape(3 * BLK, D), row_zero, 0)
        return ((key_acc, val_acc), (attn.reshape(BLK, D), d_query.reshape(BLK, D)))
    zero_acc = jnp.zeros((total + margin, D), jnp.float32)
    (key_acc, val_acc), (attn_blocks, dq_blocks) = lax.scan(step, (zero_acc, zero_acc), jnp.arange(blocks_all, dtype=jnp.int32))
    attn_all = attn_blocks.reshape(total, D)
    dq_all = dq_blocks.reshape(total, D)
    dk_all = key_acc[margin:].astype(jnp.bfloat16)
    dv_all = val_acc[margin:].astype(jnp.bfloat16)
    mixed = jnp.dot(attn_all, w_out, preferred_element_type=jnp.float32).astype(jnp.bfloat16)
    grad_rows = (jnp.dot(dq_all, w_query.T, preferred_element_type=jnp.float32) + jnp.dot(dk_all, w_key.T, preferred_element_type=jnp.float32) + jnp.dot(dv_all, w_value.T, preferred_element_type=jnp.float32)).astype(jnp.bfloat16)
    grad_scale = 1.0 / math.sqrt(total)
    grad_query = jnp.dot(rows.T, dq_all, preferred_element_type=jnp.float32) * grad_scale
    grad_key = jnp.dot(rows.T, dk_all, preferred_element_type=jnp.float32) * grad_scale
    grad_value = jnp.dot(rows.T, dv_all, preferred_element_type=jnp.float32) * grad_scale
    grad_out = jnp.dot(attn_all.T, grad_y, preferred_element_type=jnp.float32) * grad_scale
    return (fold_back(mixed), fold_back(grad_rows), grad_query, grad_key, grad_value, grad_out)
```

```python
import functools
import math

import jax
import jax.numpy as jnp
from jax import lax
from jax.experimental import pallas as pl
from jax.experimental.pallas import tpu as pltpu
from jax.sharding import PartitionSpec as P

HD = 128
BLK = 256
WIN = 3 * BLK
D = 512
NX, NY, NZ = 4, 4, 8
LOG2E = 1.4426950408889634
MESH = pl.DeviceIdType.MESH
F32 = jnp.float32
BF16 = jnp.bfloat16
ORDERS = (("x", "y", "z"), ("y", "x", "z"))
SIZES = {"x": NX, "y": NY, "z": NZ}


def nt(a, b):
    return lax.dot_general(a, b, (((1,), (1,)), ((), ())), preferred_element_type=F32)


def nn(a, b):
    return jnp.dot(a, b, preferred_element_type=F32)


def kernel(
    tm_size,
    table,
    cot,
    stamps,
    starts,
    wq_in,
    wk_in,
    wv_in,
    wo_in,
    decay,
    mixed_out,
    gt_out,
    red_out,
    xw,
    xT,
    g_s,
    ts_near,
    dec_send,
    dec_recv,
    wq,
    wk,
    wv,
    wo,
    mb,
    brow,
    q_s,
    qT_s,
    k_s,
    v_s,
    do_s,
    doT_s,
    o_s,
    dq_s,
    dkT_s,
    dvT_s,
    pf,
    psend,
    precv,
    b0,
    b1,
    b2,
    rc0,
    rc1,
    rc2,
    red,
    ct_send,
    ct_recv,
    ct_own,
    mix,
    gtb,
    lsem,
    osem,
    hs,
    hr,
    ws,
    wr,
    ps,
    pr,
    rs_s,
    rs_r,
    ag_s,
    ag_r,
    cs,
    cr,
    ms,
    mr,
):
    tm = lax.axis_index("tm")
    c = lax.axis_index("rep")
    blocks = 2 * tm_size
    blk = c * (blocks - 1 - 2 * tm) + tm
    coord = {"x": tm // (NZ * NY), "z": (tm // NY) % NZ, "y": tm % NY}

    def holder(pos):
        side = pos // tm_size
        return (side * (blocks - 1 - 2 * pos) + pos, side)

    def partner(axis, d):
        at = dict(coord)
        at[axis] = (coord[axis] + d) % SIZES[axis]
        return ((at["x"] * NZ + at["z"]) * NY + at["y"], c)

    next1 = holder((blk + 1) % blocks)
    next2 = holder((blk + 2) % blocks)
    pos1 = (blk + blocks - 1) % blocks
    pos2 = (blk + blocks - 2) % blocks
    prev1 = holder(pos1)
    prev2 = holder(pos2)
    sib = (tm, 1 - c)

    loads = [
        pltpu.make_async_copy(src, dst, lsem.at[n])
        for n, (src, dst) in enumerate(
            [
                (table.at[c], xw.at[2]),
                (cot.at[c], g_s),
                (wq_in, wq.at[1]),
                (wk_in, wk.at[1]),
                (wv_in, wv.at[1]),
                (wo_in, wo.at[1]),
            ]
        )
    ]
    for copy in loads:
        copy.start()

    barrier = pltpu.get_barrier_semaphore()
    friends = [next1, next2, prev1, prev2, sib]
    for axis, size in SIZES.items():
        friends += [partner(axis, d) for d in range(1, size)]
    for friend in friends:
        pl.semaphore_signal(barrier, inc=1, device_id=friend, device_id_type=MESH)

    def remote(src, dst, send, recv, to):
        return pltpu.make_async_remote_copy(
            src_ref=src, dst_ref=dst, send_sem=send, recv_sem=recv, device_id=to, device_id_type=MESH
        )

    sub = lax.broadcasted_iota(jnp.int32, (8, 128), 0)
    dec_send[...] = jnp.where(sub == 0, decay[0, 0], decay[0, 1])
    first_row = jnp.where(c == 0, starts[0:1, :], starts[1:2, :]) - (blk - 2) * BLK
    first_col = jnp.transpose(jnp.broadcast_to(first_row.astype(F32), (128, BLK)))
    row_id = lax.broadcasted_iota(jnp.int32, (BLK, 128), 0)
    col_id = lax.broadcasted_iota(jnp.int32, (BLK, 128), 1)
    for n in range(WIN // 128):
        key_id = col_id + n * 128
        ok = (key_id.astype(F32) >= first_col) & (key_id <= row_id + 2 * BLK)
        mb[:, n * 128 : (n + 1) * 128] = jnp.where(ok, 0.0, -1e30)

    pl.semaphore_wait(barrier, len(friends))

    half = BLK // 2
    top, low = pl.ds(0, half), pl.ds(half, half)
    mine = [
        remote(table.at[c, rows], xw.at[1, rows], hs.at[n], hr.at[n], next1)
        for n, rows in enumerate((top, low))
    ]
    onward = [
        remote(xw.at[1, rows], xw.at[0, rows], hs.at[2 + n], hr.at[2 + n], next1)
        for n, rows in enumerate((top, low))
    ]
    times = [
        remote(stamps, ts_near.at[n], hs.at[4 + n], hr.at[4 + n], to)
        for n, to in enumerate((next1, next2))
    ]
    weights = [
        remote(src, dst.at[0], ws.at[n], wr.at[n], sib)
        for n, (src, dst) in enumerate(((wq_in, wq), (wk_in, wk), (wv_in, wv), (wo_in, wo)))
    ]
    decays = remote(dec_send, dec_recv, ws.at[4], wr.at[4], sib)
    for copy in mine + times + [decays] + weights:
        copy.start()

    def put_heads(dst, slot, rows, val):
        val = val.astype(BF16)
        for j in range(2):
            dst[2 * j + slot, rows, :] = val[:, j * HD : (j + 1) * HD]
        return val

    every = pl.ds(0, BLK)

    def own_rows(slot):
        x = xw[2]
        val = put_heads(q_s, slot, every, nn(x, wq[slot]))
        for j in range(2):
            qT_s[2 * j + slot] = jnp.transpose(val[:, j * HD : (j + 1) * HD])
        val = put_heads(do_s, slot, every, nt(g_s[...], wo[slot]))
        for j in range(2):
            doT_s[2 * j + slot] = jnp.transpose(val[:, j * HD : (j + 1) * HD])

    def keys_of(part, slot):
        rows = pl.ds(part * BLK, BLK)
        put_heads(k_s, slot, rows, nn(xw[part], wk[slot]))
        put_heads(v_s, slot, rows, nn(xw[part], wv[slot]))

    for copy in loads:
        copy.wait()
    own_rows(1)
    keys_of(2, 1)
    xT[:, 2 * BLK :] = jnp.transpose(xw[2])
    for n in range(2):
        mine[n].wait_recv()
        onward[n].start()
    keys_of(1, 1)
    xT[:, BLK : 2 * BLK] = jnp.transpose(xw[1])
    for copy in weights:
        copy.wait_recv()
    own_rows(0)
    keys_of(2, 0)
    keys_of(1, 0)
    for copy in times + [decays]:
        copy.wait_recv()
    for copy in onward:
        copy.wait_recv()
    keys_of(0, 0)
    keys_of(0, 1)
    xT[:, :BLK] = jnp.transpose(xw[0])

    def side_row(ref, pos):
        return jnp.where(pos // tm_size == 0, ref[0:1, :], ref[1:2, :])

    own_times = side_row(stamps, blk)
    base = jnp.max(own_times, axis=1, keepdims=True)
    rel = jnp.concatenate(
        [side_row(ts_near.at[1], pos2), side_row(ts_near.at[0], pos1), own_times], axis=1
    )
    rel = (rel - base).astype(F32) * LOG2E
    for j in range(2):
        brow[2 * j] = rel * dec_recv[j : j + 1, 0:1]
        brow[2 * j + 1] = rel * dec_send[j : j + 1, 0:1]

    inv_scale = 1.0 / math.sqrt(HD)
    psends = [
        remote(psend.at[j], precv.at[j], ps.at[j], pr.at[j], sib) for j in range(2)
    ]

    def head(t, carry):
        slot = t % 2
        j = t // 2
        lanes = pl.ds(pl.multiple_of(j * HD, HD), HD)
        s = nt(q_s[t], k_s[t]) * (inv_scale * LOG2E) + (mb[...] + brow[t])
        p = jnp.exp2(s - jnp.max(s, axis=-1, keepdims=True))
        p = p * (1.0 / jnp.sum(p, axis=-1, keepdims=True))
        pb = p.astype(BF16)
        o = nn(pb, v_s[t]).astype(BF16)
        o_s[slot, :, lanes] = o
        dvT = nn(doT_s[t], pb).astype(BF16)
        dvT_s[slot, j] = dvT
        dp = nt(do_s[t], v_s[t])
        delta = jnp.sum(p * dp, axis=-1, keepdims=True)
        ds = (p * (dp - delta)).astype(BF16)
        dq = (nn(ds, k_s[t]) * inv_scale).astype(BF16)
        dq_s[slot, :, lanes] = dq
        dkT = (nn(qT_s[t], ds) * inv_scale).astype(BF16)
        dkT_s[slot, j] = dkT
        pf[0:D, :] = nn(xT[:, 2 * BLK :], dq)
        pf[D : 2 * D, :] = nt(xT[...], dkT)
        pf[2 * D : 3 * D, :] = nt(xT[...], dvT)
        go = nn(jnp.transpose(o), g_s[...])
        for n in range(4):
            pf[3 * D + n * HD : 3 * D + (n + 1) * HD, :] = go[:, n * HD : (n + 1) * HD]

        for jj in range(2):

            @pl.when(t == 2 * jj)
            def _():
                psend[jj] = pf[...].astype(BF16)
                psends[jj].start()

            @pl.when(t == 2 * jj + 1)
            def _():
                psends[jj].wait_recv()
                for n in range(4):
                    total = pf[n * D : (n + 1) * D, :] + precv[jj, n * D : (n + 1) * D, :].astype(F32)
                    at = ((n % 2) * 2 + jj) * D
                    b0[n // 2, at : at + D, :] = total.astype(BF16)

        return carry

    lax.fori_loop(0, 4, head, 0)

    sources = (b0, b1, b2)
    landing = (rc0, rc1, rc2)
    rows_at = (4 * D, D, D // 4)

    def scatter(stage):
        copies = []
        for col in range(2):
            axis = ORDERS[col][stage]
            size = SIZES[axis]
            piece = rows_at[stage] // size
            for d in range(1, size):
                there = (coord[axis] + d) % size
                copies.append(
                    remote(
                        sources[stage].at[col, pl.ds(pl.multiple_of(there * piece, piece), piece)],
                        landing[stage].at[col, d - 1],
                        rs_s.at[stage, col, d - 1],
                        rs_r.at[stage, col, d - 1],
                        partner(axis, d),
                    )
                )
        for copy in copies:
            copy.start()
        return copies

    def gathered(stage, col):
        axis = ORDERS[col][stage]
        size = SIZES[axis]
        piece = rows_at[stage] // size
        own = sources[stage][col, pl.ds(pl.multiple_of(coord[axis] * piece, piece), piece), :]
        total = own.astype(F32)
        for d in range(1, size):
            total = total + landing[stage][col, d - 1].astype(F32)
        return total

    def base_row(stage, col):
        row = 0
        for s in range(stage + 1):
            axis = ORDERS[col][s]
            row = row + coord[axis] * (rows_at[s] // SIZES[axis])
        return row

    def spread(stage):
        copies = []
        for col in range(2):
            axis = ORDERS[col][stage]
            size = SIZES[axis]
            piece = rows_at[stage] // size
            here = pl.ds(pl.multiple_of(base_row(stage, col), piece), piece)
            for d in range(1, size):
                copies.append(
                    remote(
                        red.at[col, here],
                        red.at[col, here],
                        ag_s.at[stage, col, d - 1],
                        ag_r.at[stage, col, d - 1],
                        partner(axis, d),
                    )
                )
        for copy in copies:
            copy.start()
        return copies

    def arrived(copies):
        for copy in copies:
            copy.wait_recv()

    sent = []
    first = scatter(0)
    sent += first

    mix[c] = (nn(o_s[0], wo[0]) + nn(o_s[1], wo[1])).astype(BF16)
    to_sib = [remote(mix.at[c], mix.at[c], ms.at[0], mr.at[0], sib)]
    to_sib[0].start()
    for part in range(3):
        cols = slice(part * BLK, (part + 1) * BLK)
        total = jnp.zeros((D, BLK), F32)
        for slot in range(2):
            total = total + nn(wk[slot], dkT_s[slot, :, :, cols].reshape(BLK, BLK))
            total = total + nn(wv[slot], dvT_s[slot, :, :, cols].reshape(BLK, BLK))
        if part == 2:
            ct_own[...] = total
        else:
            ct_send[part] = total.astype(BF16)
    terms = [
        remote(ct_send.at[n], ct_recv.at[n], cs.at[n], cr.at[n], to)
        for n, to in enumerate((prev2, prev1))
    ]

    arrived(first)
    for col in range(2):
        b1[col] = gathered(0, col).astype(BF16)
    second = scatter(1)
    sent += second
    for copy in terms:
        copy.start()
    gtq = nt(dq_s[0], wq[0]) + nt(dq_s[1], wq[1])
    arrived(second)
    for col in range(2):
        b2[col] = gathered(1, col).astype(BF16)
    third = scatter(2)
    sent += third
    arrived(third)
    scale = 1.0 / math.sqrt(blocks * BLK)
    for col in range(2):
        piece = rows_at[2] // NZ
        here = pl.ds(pl.multiple_of(base_row(2, col), piece), piece)
        red[col, here, :] = (gathered(2, col) * scale).astype(BF16)
    up = spread(2)
    sent += up
    for copy in terms:
        copy.wait_recv()
    ct = ct_own[...] + ct_recv[0].astype(F32) + ct_recv[1].astype(F32)
    gtb[c] = (gtq + jnp.transpose(ct)).astype(BF16)
    to_sib.append(remote(gtb.at[c], gtb.at[c], ms.at[1], mr.at[1], sib))
    to_sib[1].start()
    arrived(up)
    up = spread(1)
    sent += up
    arrived(up)
    up = spread(0)
    sent += up
    arrived(to_sib)
    outs = [
        pltpu.make_async_copy(mix, mixed_out, osem.at[0]),
        pltpu.make_async_copy(gtb, gt_out, osem.at[1]),
    ]
    for copy in outs:
        copy.start()
    arrived(up)
    outs.append(pltpu.make_async_copy(red, red_out, osem.at[2]))
    outs[2].start()
    for copy in mine + onward + times + [decays] + weights + psends + sent + terms + to_sib:
        copy.wait_send()
    for copy in outs:
        copy.wait()


def shards(table, cotangent, stamps, starts, w_query, w_key, w_value, w_out, decay):
    tm_size = lax.axis_size("tm")
    hbm = pl.BlockSpec(memory_space=pl.ANY)
    vmem = pl.BlockSpec(memory_space=pltpu.VMEM)
    dma = pltpu.SemaphoreType.DMA
    V = pltpu.VMEM
    mixed, grad_table, red = pl.pallas_call(
        functools.partial(kernel, tm_size),
        out_shape=(
            jax.ShapeDtypeStruct((2, BLK, D), BF16),
            jax.ShapeDtypeStruct((2, BLK, D), BF16),
            jax.ShapeDtypeStruct((2, 4 * D, 128), BF16),
        ),
        in_specs=[hbm, hbm, vmem, vmem, hbm, hbm, hbm, hbm, pl.BlockSpec(memory_space=pltpu.SMEM)],
        out_specs=(hbm, hbm, hbm),
        scratch_shapes=[
            V((3, BLK, D), BF16),
            V((D, WIN), BF16),
            V((BLK, D), BF16),
            V((2, 2, BLK), jnp.int32),
            V((8, 128), F32),
            V((8, 128), F32),
            V((2, D, BLK), BF16),
            V((2, D, BLK), BF16),
            V((2, D, BLK), BF16),
            V((2, BLK, D), BF16),
            V((BLK, WIN), F32),
            V((4, 1, WIN), F32),
            V((4, BLK, HD), BF16),
            V((4, HD, BLK), BF16),
            V((4, WIN, HD), BF16),
            V((4, WIN, HD), BF16),
            V((4, BLK, HD), BF16),
            V((4, HD, BLK), BF16),
            V((2, BLK, BLK), BF16),
            V((2, BLK, BLK), BF16),
            V((2, 2, HD, WIN), BF16),
            V((2, 2, HD, WIN), BF16),
            V((4 * D, 128), F32),
            V((2, 4 * D, 128), BF16),
            V((2, 4 * D, 128), BF16),
            V((2, 4 * D, 128), BF16),
            V((2, D, 128), BF16),
            V((2, D // 4, 128), BF16),
            V((2, 3, D, 128), BF16),
            V((2, 3, D // 4, 128), BF16),
            V((2, 7, D // 32, 128), BF16),
            V((2, 4 * D, 128), BF16),
            V((2, D, BLK), BF16),
            V((2, D, BLK), BF16),
            V((D, BLK), F32),
            V((2, BLK, D), BF16),
            V((2, BLK, D), BF16),
            dma((6,)),
            dma((3,)),
            dma((6,)),
            dma((6,)),
            dma((5,)),
            dma((5,)),
            dma((2,)),
            dma((2,)),
            dma((3, 2, 7)),
            dma((3, 2, 7)),
            dma((3, 2, 7)),
            dma((3, 2, 7)),
            dma((2,)),
            dma((2,)),
            dma((2,)),
            dma((2,)),
        ],
        compiler_params=pltpu.CompilerParams(
            collective_id=0, has_side_effects=True, vmem_limit_bytes=56 * 1024 * 1024
        ),
        name="history_attention",
    )(table, cotangent, stamps, starts, w_query, w_key, w_value, w_out, decay.reshape(1, 2))
    red = red.reshape(4, 2, D, 128).astype(F32)

    def wide(part):
        return jnp.transpose(part, (1, 0, 2)).reshape(D, 256)

    grad_out = jnp.transpose(red[3].reshape(2, 4, 128, 128), (0, 2, 1, 3)).reshape(256, D)
    return (mixed, grad_table, wide(red[0]), wide(red[1]), wide(red[2]), grad_out)


def solution(mesh):
    return jax.shard_map(
        shards,
        mesh=mesh,
        in_specs=(
            P(None, "tm", None),
            P(None, "tm", None),
            P(None, "tm"),
            P(None, "tm"),
            P(None, "rep"),
            P(None, "rep"),
            P(None, "rep"),
            P("rep", None),
            P("rep"),
        ),
        out_specs=(
            P(None, "tm", None),
            P(None, "tm", None),
            P(None, "rep"),
            P(None, "rep"),
            P(None, "rep"),
            P("rep", None),
        ),
        check_vma=False,
    )
```

```python
import functools
import math

import jax
import jax.numpy as jnp
from jax import lax
from jax.experimental import pallas as pl
from jax.experimental.pallas import tpu as pltpu
from jax.sharding import PartitionSpec as P

HD = 128
BLK = 256
WIN = 3 * BLK
D = 512
NX, NY, NZ = 4, 4, 8
LOG2E = 1.4426950408889634
MESH = pl.DeviceIdType.MESH
F32 = jnp.float32
BF16 = jnp.bfloat16
ORDERS = (("x", "y", "z"), ("y", "x", "z"))
SIZES = {"x": NX, "y": NY, "z": NZ}


def nt(a, b):
    return lax.dot_general(a, b, (((1,), (1,)), ((), ())), preferred_element_type=F32)


def nn(a, b):
    return jnp.dot(a, b, preferred_element_type=F32)


def kernel(
    tm_size,
    table,
    cot,
    stamps,
    starts,
    wq_in,
    wk_in,
    wv_in,
    wo_in,
    decay,
    mix,
    gtb,
    red,
    xw,
    xT,
    g_s,
    ts_own,
    st_own,
    dec_in,
    ts_near,
    dec_send,
    dec_recv,
    wq,
    wk,
    wv,
    wo,
    mb,
    brow,
    q_s,
    qT_s,
    k_s,
    v_s,
    do_s,
    doT_s,
    o_s,
    dq_s,
    dkT_s,
    dvT_s,
    psend,
    precv,
    pown,
    b0,
    b1,
    b2,
    rc0,
    rc1,
    rc2,
    ct_send,
    ct_recv,
    ct_own,
    lsem,
    hs,
    hr,
    ws,
    wr,
    ps,
    pr,
    rs_s,
    rs_r,
    ag_s,
    ag_r,
    cs,
    cr,
    ms,
    mr,
):
    tm = lax.axis_index("tm")
    c = lax.axis_index("rep")
    blocks = 2 * tm_size
    blk = c * (blocks - 1 - 2 * tm) + tm
    coord = {"x": tm // (NZ * NY), "z": (tm // NY) % NZ, "y": tm % NY}

    def holder(pos):
        side = pos // tm_size
        return (side * (blocks - 1 - 2 * pos) + pos, side)

    def partner(axis, d):
        at = dict(coord)
        at[axis] = (coord[axis] + d) % SIZES[axis]
        return ((at["x"] * NZ + at["z"]) * NY + at["y"], c)

    next1 = holder((blk + 1) % blocks)
    next2 = holder((blk + 2) % blocks)
    pos1 = (blk + blocks - 1) % blocks
    pos2 = (blk + blocks - 2) % blocks
    prev1 = holder(pos1)
    prev2 = holder(pos2)
    sib = (tm, 1 - c)

    barrier = pltpu.get_barrier_semaphore()
    friends = [next1, next2, prev1, prev2, sib]
    for axis, size in SIZES.items():
        friends += [partner(axis, d) for d in range(1, size)]
    for friend in friends:
        pl.semaphore_signal(barrier, inc=1, device_id=friend, device_id_type=MESH)

    loads = [
        pltpu.make_async_copy(src, dst, lsem.at[n])
        for n, (src, dst) in enumerate(
            [
                (stamps, ts_own),
                (starts, st_own),
                (decay, dec_in),
                (table.at[c], xw.at[2]),
                (cot.at[c], g_s),
                (wq_in, wq.at[1]),
                (wk_in, wk.at[1]),
                (wv_in, wv.at[1]),
                (wo_in, wo.at[1]),
            ]
        )
    ]
    for copy in loads:
        copy.start()

    def remote(src, dst, send, recv, to):
        return pltpu.make_async_remote_copy(
            src_ref=src, dst_ref=dst, send_sem=send, recv_sem=recv, device_id=to, device_id_type=MESH
        )

    for copy in loads[:3]:
        copy.wait()
    sub = lax.broadcasted_iota(jnp.int32, (8, 128), 0)
    dec_send[...] = jnp.where(sub == 0, dec_in[0, 0], dec_in[0, 1])
    first_row = jnp.where(c == 0, st_own[0:1, :], st_own[1:2, :]) - (blk - 2) * BLK
    first_col = jnp.transpose(jnp.broadcast_to(first_row.astype(F32), (128, BLK)))
    row_id = lax.broadcasted_iota(jnp.int32, (BLK, 128), 0)
    col_id = lax.broadcasted_iota(jnp.int32, (BLK, 128), 1)
    for n in range(WIN // 128):
        key_id = col_id + n * 128
        ok = (key_id.astype(F32) >= first_col) & (key_id <= row_id + 2 * BLK)
        mb[:, n * 128 : (n + 1) * 128] = jnp.where(ok, 0.0, -1e30)

    pl.semaphore_wait(barrier, len(friends))

    half = BLK // 2
    top, low = pl.ds(0, half), pl.ds(half, half)
    mine = [
        remote(table.at[c, rows], xw.at[1, rows], hs.at[n], hr.at[n], next1)
        for n, rows in enumerate((top, low))
    ]
    onward = [
        remote(xw.at[1, rows], xw.at[0, rows], hs.at[2 + n], hr.at[2 + n], next1)
        for n, rows in enumerate((top, low))
    ]
    times = [
        remote(stamps, ts_near.at[n], hs.at[4 + n], hr.at[4 + n], to)
        for n, to in enumerate((next1, next2))
    ]
    weights = [
        remote(src, dst.at[0], ws.at[n], wr.at[n], sib)
        for n, (src, dst) in enumerate(((wq_in, wq), (wk_in, wk), (wv_in, wv), (wo_in, wo)))
    ]
    decays = remote(dec_send, dec_recv, ws.at[4], wr.at[4], sib)
    for copy in mine + times + [decays] + weights:
        copy.start()

    def put_heads(dst, slot, rows, val):
        val = val.astype(BF16)
        for j in range(2):
            dst[2 * j + slot, rows, :] = val[:, j * HD : (j + 1) * HD]
        return val

    every = pl.ds(0, BLK)

    def own_rows(slot):
        x = xw[2]
        val = put_heads(q_s, slot, every, nn(x, wq[slot]))
        for j in range(2):
            qT_s[2 * j + slot] = jnp.transpose(val[:, j * HD : (j + 1) * HD])
        val = put_heads(do_s, slot, every, nt(g_s[...], wo[slot]))
        for j in range(2):
            doT_s[2 * j + slot] = jnp.transpose(val[:, j * HD : (j + 1) * HD])

    def keys_of(part, slot):
        rows = pl.ds(part * BLK, BLK)
        put_heads(k_s, slot, rows, nn(xw[part], wk[slot]))
        put_heads(v_s, slot, rows, nn(xw[part], wv[slot]))

    for copy in loads[3:]:
        copy.wait()
    own_rows(1)
    keys_of(2, 1)
    xT[:, 2 * BLK :] = jnp.transpose(xw[2])
    for n in range(2):
        mine[n].wait_recv()
        onward[n].start()
    keys_of(1, 1)
    xT[:, BLK : 2 * BLK] = jnp.transpose(xw[1])
    for copy in weights:
        copy.wait_recv()
    own_rows(0)
    keys_of(2, 0)
    keys_of(1, 0)
    for copy in times + [decays]:
        copy.wait_recv()
    for copy in onward:
        copy.wait_recv()
    keys_of(0, 0)
    keys_of(0, 1)
    xT[:, :BLK] = jnp.transpose(xw[0])

    def side_row(ref, pos):
        return jnp.where(pos // tm_size == 0, ref[0:1, :], ref[1:2, :])

    own_times = side_row(ts_own, blk)
    base = jnp.max(own_times, axis=1, keepdims=True)
    rel = jnp.concatenate(
        [side_row(ts_near.at[1], pos2), side_row(ts_near.at[0], pos1), own_times], axis=1
    )
    rel = (rel - base).astype(F32) * LOG2E
    for j in range(2):
        brow[2 * j] = rel * dec_recv[j : j + 1, 0:1]
        brow[2 * j + 1] = rel * dec_send[j : j + 1, 0:1]

    inv_scale = 1.0 / math.sqrt(HD)
    psends = [
        remote(psend.at[j], precv.at[j], ps.at[j], pr.at[j], sib) for j in range(2)
    ]

    def head(t, carry):
        slot = t % 2
        j = t // 2
        lanes = pl.ds(pl.multiple_of(j * HD, HD), HD)
        s = nt(q_s[t], k_s[t]) * (inv_scale * LOG2E) + (mb[...] + brow[t])
        p = jnp.exp2(s - jnp.max(s, axis=-1, keepdims=True))
        p = p * (1.0 / jnp.sum(p, axis=-1, keepdims=True))
        pb = p.astype(BF16)
        o = nn(pb, v_s[t]).astype(BF16)
        o_s[slot, :, lanes] = o
        dvT = nn(doT_s[t], pb).astype(BF16)
        dvT_s[slot, j] = dvT
        dp = nt(do_s[t], v_s[t])
        delta = jnp.sum(p * dp, axis=-1, keepdims=True)
        ds = (p * (dp - delta)).astype(BF16)
        dq = (nn(ds, k_s[t]) * inv_scale).astype(BF16)
        dq_s[slot, :, lanes] = dq
        dkT = (nn(qT_s[t], ds) * inv_scale).astype(BF16)
        dkT_s[slot, j] = dkT
        parts = [
            nn(xT[:, 2 * BLK :], dq),
            nt(xT[...], dkT),
            nt(xT[...], dvT),
        ]
        go = nn(jnp.transpose(o), g_s[...])
        for n in range(3):
            pown[n] = parts[n]
        for n in range(4):
            pown[3, n * HD : (n + 1) * HD, :] = go[:, n * HD : (n + 1) * HD]

        for jj in range(2):

            @pl.when(t == 2 * jj)
            def _():
                psend[jj] = pown[...]
                psends[jj].start()

            @pl.when(t == 2 * jj + 1)
            def _():
                psends[jj].wait_recv()
                for n in range(4):
                    b0[jj, n // 2, (n % 2) * D : (n % 2 + 1) * D, :] = (pown[n] + precv[jj, n]).astype(BF16)
                for copy in scatters[jj][0]:
                    copy.start()

        return carry

    sources = (b0, b1, b2)
    landing = (rc0, rc1, rc2)
    rows_at = (2 * D, D // 2, D // 8)

    def place(stage, col):
        axis = ORDERS[col][stage]
        return axis, SIZES[axis], rows_at[stage] // SIZES[axis]

    def scatter(j, stage):
        copies = []
        for col in range(2):
            axis, size, piece = place(stage, col)
            for d in range(1, size):
                there = (coord[axis] + d) % size
                copies.append(
                    remote(
                        sources[stage].at[j, col, pl.ds(pl.multiple_of(there * piece, piece), piece)],
                        landing[stage].at[j, col, d - 1],
                        rs_s.at[j, stage, col, d - 1],
                        rs_r.at[j, stage, col, d - 1],
                        partner(axis, d),
                    )
                )
        return copies

    def gathered(j, stage, col):
        axis, size, piece = place(stage, col)
        total = sources[stage][j, col, pl.ds(pl.multiple_of(coord[axis] * piece, piece), piece), :].astype(F32)
        for d in range(1, size):
            total = total + landing[stage][j, col, d - 1].astype(F32)
        return total

    def first_owner(stage, col):
        owner = 0
        for s in range(stage + 1):
            axis, _, piece = place(s, col)
            owner = owner + coord[axis] * (piece // 8)
        return owner

    def spread(j, stage):
        copies = []
        for col in range(2):
            axis, size, piece = place(stage, col)
            here = pl.ds(first_owner(stage, col), piece // 8)
            for d in range(1, size):
                copies.append(
                    remote(
                        red.at[col, j, here],
                        red.at[col, j, here],
                        ag_s.at[j, stage, col, d - 1],
                        ag_r.at[j, stage, col, d - 1],
                        partner(axis, d),
                    )
                )
        return copies

    scatters = [[scatter(j, stage) for stage in range(3)] for j in range(2)]
    spreads = [[spread(j, stage) for stage in range(3)] for j in range(2)]

    def arrived(copies):
        for copy in copies:
            copy.wait_recv()

    def begin(copies):
        for copy in copies:
            copy.start()

    def next_scatter(j, stage):
        arrived(scatters[j][stage])
        for col in range(2):
            if stage < 2:
                sources[stage + 1][j, col] = gathered(j, stage, col)
            else:
                red[col, j, first_owner(2, col)] = (gathered(j, 2, col) * scale).astype(BF16)
        begin(scatters[j][stage + 1] if stage < 2 else spreads[j][2])

    def next_spread(j, stage):
        arrived(spreads[j][stage])
        begin(spreads[j][stage - 1])

    scale = 1.0 / math.sqrt(blocks * BLK)
    lax.fori_loop(0, 4, head, 0)

    mix[c] = (nn(o_s[0], wo[0]) + nn(o_s[1], wo[1])).astype(BF16)
    to_sib = [
        remote(ref.at[c], ref.at[c], ms.at[n], mr.at[n], sib) for n, ref in enumerate((mix, gtb))
    ]
    to_sib[0].start()
    for part in range(3):
        cols = slice(part * BLK, (part + 1) * BLK)
        total = jnp.zeros((D, BLK), F32)
        for slot in range(2):
            total = total + nn(wk[slot], dkT_s[slot, :, :, cols].reshape(BLK, BLK))
            total = total + nn(wv[slot], dvT_s[slot, :, :, cols].reshape(BLK, BLK))
        if part == 0:
            ct_send[0] = total.astype(BF16)
        else:
            ct_own[part - 1] = total
    terms = [
        remote(ct_send.at[n], ct_recv.at[n], cs.at[n], cr.at[n], prev1) for n in range(2)
    ]

    next_scatter(0, 0)
    next_scatter(0, 1)
    next_scatter(1, 0)
    terms[0].start()
    gtq = nt(dq_s[0], wq[0]) + nt(dq_s[1], wq[1])
    next_scatter(0, 2)
    next_scatter(1, 1)
    terms[0].wait_recv()
    ct_send[1] = (ct_own[0] + ct_recv[0].astype(F32)).astype(BF16)
    terms[1].start()
    next_spread(0, 2)
    next_scatter(1, 2)
    terms[1].wait_recv()
    gtb[c] = (gtq + jnp.transpose(ct_own[1] + ct_recv[1].astype(F32))).astype(BF16)
    to_sib[1].start()
    next_spread(0, 1)
    next_spread(1, 2)
    next_spread(1, 1)
    arrived(to_sib)
    arrived(spreads[0][0])
    arrived(spreads[1][0])
    sent = mine + onward + times + [decays] + weights + psends + terms + to_sib
    for j in range(2):
        for stage in range(3):
            sent += scatters[j][stage] + spreads[j][stage]
    for copy in sent:
        copy.wait_send()


def finish(mix, gtb, red, mixed, gt, grad_q, grad_k, grad_v, grad_o, wide, rows, sem):
    copies = [
        pltpu.make_async_copy(mix, mixed, sem.at[0]),
        pltpu.make_async_copy(gtb, gt, sem.at[1]),
    ]
    copies[0].start()
    copies[1].start()
    for n, out in enumerate((grad_q, grad_k, grad_v, grad_o)):
        half = pl.ds((n % 2) * (D // 8), D // 8)
        for j in range(2):
            val = red[n // 2, j, half].astype(F32).reshape(D, HD)
            if n < 3:
                wide[n, :, j * HD : (j + 1) * HD] = val
            else:
                for k in range(4):
                    rows[j * HD : (j + 1) * HD, k * HD : (k + 1) * HD] = val[k * HD : (k + 1) * HD]
        copies.append(pltpu.make_async_copy(wide.at[n] if n < 3 else rows, out, sem.at[2 + n]))
        copies[-1].start()
    for copy in copies:
        copy.wait()


def shards(table, cotangent, stamps, starts, w_query, w_key, w_value, w_out, decay):
    tm_size = lax.axis_size("tm")
    hbm = pl.BlockSpec(memory_space=pltpu.HBM)
    vmem = pl.BlockSpec(memory_space=pltpu.VMEM)
    dma = pltpu.SemaphoreType.DMA
    V = pltpu.VMEM
    near = (
        V((2, BLK, D), BF16),
        V((2, BLK, D), BF16),
        V((2, 2, 128, 8, 128), BF16),
    )
    near = pl.pallas_call(
        functools.partial(kernel, tm_size),
        out_shape=near,
        in_specs=[hbm] * 9,
        out_specs=(vmem, vmem, vmem),
        scratch_shapes=[
            V((3, BLK, D), BF16),
            V((D, WIN), BF16),
            V((BLK, D), BF16),
            V((2, BLK), jnp.int32),
            V((2, BLK), jnp.int32),
            pltpu.SMEM((1, 2), F32),
            V((2, 2, BLK), jnp.int32),
            V((8, 128), F32),
            V((8, 128), F32),
            V((2, D, BLK), BF16),
            V((2, D, BLK), BF16),
            V((2, D, BLK), BF16),
            V((2, BLK, D), BF16),
            V((BLK, WIN), F32),
            V((4, 1, WIN), F32),
            V((4, BLK, HD), BF16),
            V((4, HD, BLK), BF16),
            V((4, WIN, HD), BF16),
            V((4, WIN, HD), BF16),
            V((4, BLK, HD), BF16),
            V((4, HD, BLK), BF16),
            V((2, BLK, BLK), BF16),
            V((2, BLK, BLK), BF16),
            V((2, 2, HD, WIN), BF16),
            V((2, 2, HD, WIN), BF16),
            V((2, 4, D, 128), F32),
            V((2, 4, D, 128), F32),
            V((4, D, 128), F32),
            V((2, 2, 2 * D, 128), BF16),
            V((2, 2, D // 2, 128), F32),
            V((2, 2, D // 8, 128), F32),
            V((2, 2, 3, D // 2, 128), BF16),
            V((2, 2, 3, D // 8, 128), F32),
            V((2, 2, 7, 8, 128), F32),
            V((2, D, BLK), BF16),
            V((2, D, BLK), BF16),
            V((2, D, BLK), F32),
            dma((9,)),
            dma((6,)),
            dma((6,)),
            dma((5,)),
            dma((5,)),
            dma((2,)),
            dma((2,)),
            dma((2, 3, 2, 7)),
            dma((2, 3, 2, 7)),
            dma((2, 3, 2, 7)),
            dma((2, 3, 2, 7)),
            dma((2,)),
            dma((2,)),
            dma((2,)),
            dma((2,)),
        ],
        compiler_params=pltpu.CompilerParams(
            collective_id=0, has_side_effects=True, vmem_limit_bytes=58 * 1024 * 1024
        ),
        name="history_attention",
    )(table, cotangent, stamps, starts, w_query, w_key, w_value, w_out, decay.reshape(1, 2))
    shapes = ((2, BLK, D), (2, BLK, D), (D, BLK), (D, BLK), (D, BLK), (BLK, D))
    return pl.pallas_call(
        finish,
        out_shape=tuple(
            jax.ShapeDtypeStruct(shape, BF16 if n < 2 else F32) for n, shape in enumerate(shapes)
        ),
        in_specs=[vmem] * 3,
        out_specs=(hbm,) * 6,
        scratch_shapes=[V((3, D, BLK), F32), V((BLK, D), F32), dma((6,))],
        compiler_params=pltpu.CompilerParams(vmem_limit_bytes=16 * 1024 * 1024),
        name="finish",
    )(*near)


def solution(mesh):
    return jax.shard_map(
        shards,
        mesh=mesh,
        in_specs=(
            P(None, "tm", None),
            P(None, "tm", None),
            P(None, "tm"),
            P(None, "tm"),
            P(None, "rep"),
            P(None, "rep"),
            P(None, "rep"),
            P("rep", None),
            P("rep"),
        ),
        out_specs=(
            P(None, "tm", None),
            P(None, "tm", None),
            P(None, "rep"),
            P(None, "rep"),
            P(None, "rep"),
            P("rep", None),
        ),
        check_vma=False,
    )
```

```python
import functools
import math

import jax
import jax.numpy as jnp
from jax import lax
from jax.experimental import pallas as pl
from jax.experimental.pallas import tpu as pltpu
from jax.sharding import PartitionSpec as P

HD = 128
BLK = 256
WIN = 3 * BLK
D = 512
NX, NY, NZ = 4, 4, 8
CHUNKS = 4
LOG2E = 1.4426950408889634
MESH = pl.DeviceIdType.MESH
F32 = jnp.float32
BF16 = jnp.bfloat16
ORDERS = (("x", "y", "z"), ("y", "x", "z"))
SIZES = {"x": NX, "y": NY, "z": NZ}
FARTHEST = {4: (2, 1, 3), 8: (4, 3, 5, 2, 6, 1, 7)}


def nt(a, b):
    return lax.dot_general(a, b, (((1,), (1,)), ((), ())), preferred_element_type=F32)


def nn(a, b):
    return jnp.dot(a, b, preferred_element_type=F32)


def kernel(
    tm_size,
    table,
    cot,
    stamps,
    starts,
    wq_in,
    wk_in,
    wv_in,
    wo_in,
    decay,
    mix,
    gtb,
    red,
    xw,
    xT,
    g_s,
    ts_own,
    st_own,
    dec_in,
    ts_near,
    dec_send,
    dec_recv,
    wq,
    wk,
    wv,
    wo,
    mb,
    brow,
    q_s,
    qT_s,
    k_s,
    v_s,
    do_s,
    doT_s,
    o_s,
    dq_s,
    kvT_s,
    psend,
    precv,
    pown,
    b0,
    b1,
    b2,
    rc0,
    rc1,
    rc2,
    ct_send,
    ct_recv,
    ct_own,
    lsem,
    hs,
    hr,
    ws,
    wr,
    ps,
    pr,
    rs_s,
    rs_r,
    ag_s,
    ag_r,
    cs,
    cr,
    ms,
    mr,
    met,
):
    tm = lax.axis_index("tm")
    c = lax.axis_index("rep")
    blocks = 2 * tm_size
    blk = c * (blocks - 1 - 2 * tm) + tm
    coord = {"x": tm // (NZ * NY), "z": (tm // NY) % NZ, "y": tm % NY}

    def holder(pos):
        side = pos // tm_size
        return (side * (blocks - 1 - 2 * pos) + pos, side)

    def partner(axis, d):
        at = dict(coord)
        at[axis] = (coord[axis] + SIZES[axis] + d) % SIZES[axis]
        return ((at["x"] * NZ + at["z"]) * NY + at["y"], c)

    next1 = holder((blk + 1) % blocks)
    pos1 = (blk + blocks - 1) % blocks
    pos2 = (blk + blocks - 2) % blocks
    prev1 = holder(pos1)
    sib = (tm, 1 - c)

    barrier = pltpu.get_barrier_semaphore()
    friends = [next1, prev1, sib]
    for axis in SIZES:
        friends += [partner(axis, 1), partner(axis, -1)]
    for friend in friends:
        pl.semaphore_signal(barrier, inc=1, device_id=friend, device_id_type=MESH)

    loads = [
        pltpu.make_async_copy(src, dst, lsem.at[n])
        for n, (src, dst) in enumerate(
            [
                (stamps, ts_own),
                (starts, st_own),
                (decay, dec_in),
                (table.at[c], xw.at[2]),
                (cot.at[c], g_s),
                (wq_in, wq.at[1]),
                (wk_in, wk.at[1]),
                (wv_in, wv.at[1]),
                (wo_in, wo.at[1]),
            ]
        )
    ]
    for copy in loads:
        copy.start()

    def remote(src, dst, send, recv, to):
        return pltpu.make_async_remote_copy(
            src_ref=src, dst_ref=dst, send_sem=send, recv_sem=recv, device_id=to, device_id_type=MESH
        )

    pl.semaphore_wait(barrier, len(friends))

    def tell(token):
        axis, d, n = token
        pl.semaphore_signal(met.at[n], inc=1, device_id=partner(axis, d), device_id_type=MESH)

    def hear(token):
        pl.semaphore_wait(met.at[token[2]], 1)

    tokens = ([("x", 1, 0), ("y", 1, 1), ("z", 1, 2), ("z", -1, 3)], [("z", 1, 4), ("z", -1, 5)], [("z", 1, 6)])

    chunk = BLK // CHUNKS
    pieces = [pl.ds(n * chunk, chunk) for n in range(CHUNKS)]
    mine = [
        remote(table.at[c, rows], xw.at[1, rows], hs.at[n], hr.at[n], next1)
        for n, rows in enumerate(pieces)
    ]
    onward = [
        remote(xw.at[1, rows], xw.at[0, rows], hs.at[CHUNKS + n], hr.at[CHUNKS + n], next1)
        for n, rows in enumerate(pieces)
    ]
    times = [
        remote(src, ts_near.at[n], hs.at[2 * CHUNKS + n], hr.at[2 * CHUNKS + n], next1)
        for n, src in enumerate((stamps, ts_near.at[0]))
    ]
    weights = [
        remote(src, dst.at[0], ws.at[n], wr.at[n], sib)
        for n, (src, dst) in enumerate(((wq_in, wq), (wk_in, wk), (wv_in, wv), (wo_in, wo)))
    ]
    decays = remote(dec_send, dec_recv, ws.at[4], wr.at[4], sib)
    for copy in times[:1] + mine + weights:
        copy.start()
    for token in tokens[0]:
        tell(token)
    for copy in loads[:3]:
        copy.wait()
    sub = lax.broadcasted_iota(jnp.int32, (8, 128), 0)
    dec_send[...] = jnp.where(sub == 0, dec_in[0, 0], dec_in[0, 1])
    decays.start()
    first_row = jnp.where(c == 0, st_own[0:1, :], st_own[1:2, :]) - (blk - 2) * BLK
    first_col = jnp.transpose(jnp.broadcast_to(first_row.astype(F32), (128, BLK)))
    row_id = lax.broadcasted_iota(jnp.int32, (BLK, 128), 0)
    col_id = lax.broadcasted_iota(jnp.int32, (BLK, 128), 1)
    for n in range(WIN // 128):
        key_id = col_id + n * 128
        ok = (key_id.astype(F32) >= first_col) & (key_id <= row_id + 2 * BLK)
        mb[:, n * 128 : (n + 1) * 128] = jnp.where(ok, 0.0, -1e30)


    def put_heads(dst, slot, rows, val):
        val = val.astype(BF16)
        for j in range(2):
            dst[2 * slot + j, rows, :] = val[:, j * HD : (j + 1) * HD]
        return val

    every = pl.ds(0, BLK)

    def own_rows(slot):
        x = xw[2]
        val = put_heads(q_s, slot, every, nn(x, wq[slot]))
        for j in range(2):
            qT_s[2 * slot + j] = jnp.transpose(val[:, j * HD : (j + 1) * HD])
        val = put_heads(do_s, slot, every, nt(g_s[...], wo[slot]))
        for j in range(2):
            doT_s[2 * slot + j] = jnp.transpose(val[:, j * HD : (j + 1) * HD])

    def keys_of(part, slot):
        rows = pl.ds(part * BLK, BLK)
        put_heads(k_s, slot, rows, nn(xw[part], wk[slot]))
        put_heads(v_s, slot, rows, nn(xw[part], wv[slot]))

    for copy in loads[3:]:
        copy.wait()
    own_rows(1)
    keys_of(2, 1)
    xT[:, 2 * BLK :] = jnp.transpose(xw[2])
    times[0].wait_recv()
    times[1].start()
    for token in tokens[0]:
        hear(token)
    for token in tokens[1]:
        tell(token)
    for n in range(CHUNKS):
        mine[n].wait_recv()
        onward[n].start()
    for token in tokens[1]:
        hear(token)
    for token in tokens[2]:
        tell(token)
    keys_of(1, 1)
    xT[:, BLK : 2 * BLK] = jnp.transpose(xw[1])
    for copy in weights:
        copy.wait_recv()
    own_rows(0)
    keys_of(2, 0)
    keys_of(1, 0)
    for token in tokens[2]:
        hear(token)
    for copy in (times[1], decays):
        copy.wait_recv()
    for copy in onward:
        copy.wait_recv()
    keys_of(0, 0)
    keys_of(0, 1)
    xT[:, :BLK] = jnp.transpose(xw[0])

    def side_row(ref, pos):
        return jnp.where(pos // tm_size == 0, ref[0:1, :], ref[1:2, :])

    own_times = side_row(ts_own, blk)
    base = jnp.max(own_times, axis=1, keepdims=True)
    rel = jnp.concatenate(
        [side_row(ts_near.at[1], pos2), side_row(ts_near.at[0], pos1), own_times], axis=1
    )
    rel = (rel - base).astype(F32) * LOG2E
    for j in range(2):
        brow[j] = rel * dec_recv[j : j + 1, 0:1]
        brow[2 + j] = rel * dec_send[j : j + 1, 0:1]

    inv_scale = 1.0 / math.sqrt(HD)
    psends = [
        remote(psend.at[j], precv.at[j], ps.at[j], pr.at[j], sib) for j in range(2)
    ]

    def products(t):
        return nt(q_s[t], k_s[t]), nt(do_s[t], v_s[t])

    def softmax(t, s, dp):
        s = s * (inv_scale * LOG2E) + (mb[...] + brow[t])
        p = jnp.exp2(s - jnp.max(s, axis=-1, keepdims=True))
        p = p * (1.0 / jnp.sum(p, axis=-1, keepdims=True))
        delta = jnp.sum(p * dp, axis=-1, keepdims=True)
        return p.astype(BF16), (p * (dp - delta)).astype(BF16)

    def attention(t, pb, ds):
        lanes = slice((t % 2) * HD, (t % 2 + 1) * HD)
        o_s[t // 2, :, lanes] = nn(pb, v_s[t]).astype(BF16)
        dq_s[t // 2, :, lanes] = (nn(ds, k_s[t]) * inv_scale).astype(BF16)
        kvT_s[t, :HD, :] = (nn(qT_s[t], ds) * inv_scale).astype(BF16)
        kvT_s[t, HD:, :] = nn(doT_s[t], pb).astype(BF16)

    def weight_grads(t):
        lanes = slice((t % 2) * HD, (t % 2 + 1) * HD)
        kv = nt(xT[...], kvT_s[t])
        go = nn(jnp.transpose(o_s[t // 2, :, lanes]), g_s[...])
        to = psend.at[t] if t < 2 else pown.at[t - 2]
        to[0] = nn(xT[:, 2 * BLK :], dq_s[t // 2, :, lanes]).astype(to.dtype)
        to[1] = kv[:, :HD].astype(to.dtype)
        to[2] = kv[:, HD:].astype(to.dtype)
        for n in range(4):
            to[3, n * HD : (n + 1) * HD, :] = go[:, n * HD : (n + 1) * HD].astype(to.dtype)

    def reduce_pair(j):
        psends[j].wait_recv()
        for n in range(4):
            b0[j, n // 2, (n % 2) * D : (n % 2 + 1) * D, :] = (pown[j, n] + precv[j, n].astype(F32)).astype(BF16)
        begin(scatters[j][0])

    def pass_on(step):
        if step in (0, 2):
            psends[step // 2].start()
        if step == 3:
            reduce_pair(1)
        if step in (1, 2):
            pl.when(c == step - 1)(lambda: reduce_pair(0))

    def begin(copies):
        for copy in copies:
            copy.start()

    sources = (b0, b1, b2)
    landing = (rc0, rc1, rc2)
    rows_at = (2 * D, D // 2, D // 8)

    def place(stage, col):
        axis = ORDERS[col][stage]
        return axis, SIZES[axis], rows_at[stage] // SIZES[axis]

    def scatter(j, stage):
        copies = []
        for col in range(2):
            axis, size, piece = place(stage, col)
            for d in FARTHEST[size]:
                there = (coord[axis] + d) % size
                copies.append(
                    remote(
                        sources[stage].at[j, col, pl.ds(pl.multiple_of(there * piece, piece), piece)],
                        landing[stage].at[j, col, d - 1],
                        rs_s.at[j, stage, col, d - 1],
                        rs_r.at[j, stage, col, d - 1],
                        partner(axis, d),
                    )
                )
        return copies

    def gathered(j, stage, col):
        axis, size, piece = place(stage, col)
        total = sources[stage][j, col, pl.ds(pl.multiple_of(coord[axis] * piece, piece), piece), :].astype(F32)
        for d in range(1, size):
            total = total + landing[stage][j, col, d - 1].astype(F32)
        return total

    def first_owner(stage, col):
        owner = 0
        for s in range(stage + 1):
            axis, _, piece = place(s, col)
            owner = owner + coord[axis] * (piece // 8)
        return owner

    def spread(j, stage):
        copies = []
        for col in range(2):
            axis, size, piece = place(stage, col)
            here = pl.ds(first_owner(stage, col), piece // 8)
            for d in FARTHEST[size]:
                copies.append(
                    remote(
                        red.at[col, j, here],
                        red.at[col, j, here],
                        ag_s.at[j, stage, col, d - 1],
                        ag_r.at[j, stage, col, d - 1],
                        partner(axis, d),
                    )
                )
        return copies

    scatters = [[scatter(j, stage) for stage in range(3)] for j in range(2)]
    spreads = [[spread(j, stage) for stage in range(3)] for j in range(2)]

    def arrived(copies):
        for copy in copies:
            copy.wait_recv()

    def next_scatter(j, stage):
        arrived(scatters[j][stage])
        for col in range(2):
            if stage < 2:
                sources[stage + 1][j, col] = gathered(j, stage, col).astype(sources[stage + 1].dtype)
            else:
                red[col, j, first_owner(2, col)] = (gathered(j, 2, col) * scale).astype(BF16)
        begin(scatters[j][stage + 1] if stage < 2 else spreads[j][2])

    def next_spread(j, stage):
        arrived(spreads[j][stage])
        begin(spreads[j][stage - 1])

    scale = 1.0 / math.sqrt(blocks * BLK)
    turn = (0, 2, 1, 3)
    now = products(turn[0])
    for step in range(4):
        later = products(turn[step + 1]) if step < 3 else None
        if step > 0:
            weight_grads(turn[step - 1])
        pb, ds = softmax(turn[step], *now)
        if step > 0:
            pass_on(step - 1)
        attention(turn[step], pb, ds)
        now = later
    weight_grads(turn[3])
    pass_on(3)

    mix[c] = (nn(o_s[0], wo[0]) + nn(o_s[1], wo[1])).astype(BF16)
    to_sib = [
        remote(ref.at[c], ref.at[c], ms.at[n], mr.at[n], sib) for n, ref in enumerate((mix, gtb))
    ]
    to_sib[0].start()
    for part in range(3):
        cols = slice(part * BLK, (part + 1) * BLK)
        total = jnp.zeros((D, BLK), F32)
        for t in range(4):
            lanes = slice((t % 2) * HD, (t % 2 + 1) * HD)
            both = jnp.concatenate([wk[t // 2, :, lanes], wv[t // 2, :, lanes]], axis=1)
            total = total + nn(both, kvT_s[t, :, cols])
        if part == 0:
            ct_send[0] = total.astype(BF16)
        else:
            ct_own[part - 1] = total
    terms = [
        [
            remote(ct_send.at[n, rows], ct_recv.at[n, rows], cs.at[n, h], cr.at[n, h], prev1)
            for h, rows in enumerate((every, pl.ds(BLK, BLK)))
        ]
        for n in range(2)
    ]

    next_scatter(0, 0)
    next_scatter(1, 0)
    gtq = nt(dq_s[0], wq[0]) + nt(dq_s[1], wq[1])
    next_scatter(0, 1)
    next_scatter(1, 1)
    begin(terms[0])
    next_scatter(0, 2)
    next_scatter(1, 2)
    for h in range(2):
        terms[0][h].wait_recv()
        rows = slice(h * BLK, (h + 1) * BLK)
        ct_send[1, rows, :] = (ct_own[0, rows, :] + ct_recv[0, rows, :].astype(F32)).astype(BF16)
        terms[1][h].start()
    next_spread(0, 2)
    next_spread(1, 2)
    next_spread(0, 1)
    arrived(terms[1])
    gtb[c] = (gtq + jnp.transpose(ct_own[1] + ct_recv[1].astype(F32))).astype(BF16)
    to_sib[1].start()
    next_spread(1, 1)
    arrived(to_sib)
    arrived(spreads[0][0])
    arrived(spreads[1][0])
    sent = mine + onward + times + [decays] + weights + psends + terms[0] + terms[1] + to_sib
    for j in range(2):
        for stage in range(3):
            sent += scatters[j][stage] + spreads[j][stage]
    for copy in sent:
        copy.wait_send()


def finish(mix, gtb, red, mixed, gt, grad_q, grad_k, grad_v, grad_o, wide, rows, sem):
    copies = [
        pltpu.make_async_copy(mix, mixed, sem.at[0]),
        pltpu.make_async_copy(gtb, gt, sem.at[1]),
    ]
    copies[0].start()
    copies[1].start()
    for n, out in enumerate((grad_q, grad_k, grad_v, grad_o)):
        half = pl.ds((n % 2) * (D // 8), D // 8)
        for j in range(2):
            val = red[n // 2, j, half].astype(F32).reshape(D, HD)
            if n < 3:
                wide[n, :, j * HD : (j + 1) * HD] = val
            else:
                for k in range(4):
                    rows[j * HD : (j + 1) * HD, k * HD : (k + 1) * HD] = val[k * HD : (k + 1) * HD]
        copies.append(pltpu.make_async_copy(wide.at[n] if n < 3 else rows, out, sem.at[2 + n]))
        copies[-1].start()
    for copy in copies:
        copy.wait()


def shards(table, cotangent, stamps, starts, w_query, w_key, w_value, w_out, decay):
    tm_size = lax.axis_size("tm")
    hbm = pl.BlockSpec(memory_space=pltpu.HBM)
    vmem = pl.BlockSpec(memory_space=pltpu.VMEM)
    dma = pltpu.SemaphoreType.DMA
    V = pltpu.VMEM
    near = (
        V((2, BLK, D), BF16),
        V((2, BLK, D), BF16),
        V((2, 2, 128, 8, 128), BF16),
    )
    near = pl.pallas_call(
        functools.partial(kernel, tm_size),
        out_shape=near,
        in_specs=[hbm] * 9,
        out_specs=(vmem, vmem, vmem),
        scratch_shapes=[
            V((3, BLK, D), BF16),
            V((D, WIN), BF16),
            V((BLK, D), BF16),
            V((2, BLK), jnp.int32),
            V((2, BLK), jnp.int32),
            pltpu.SMEM((1, 2), F32),
            V((2, 2, BLK), jnp.int32),
            V((8, 128), F32),
            V((8, 128), F32),
            V((2, D, BLK), BF16),
            V((2, D, BLK), BF16),
            V((2, D, BLK), BF16),
            V((2, BLK, D), BF16),
            V((BLK, WIN), F32),
            V((4, 1, WIN), F32),
            V((4, BLK, HD), BF16),
            V((4, HD, BLK), BF16),
            V((4, WIN, HD), BF16),
            V((4, WIN, HD), BF16),
            V((4, BLK, HD), BF16),
            V((4, HD, BLK), BF16),
            V((2, BLK, BLK), BF16),
            V((2, BLK, BLK), BF16),
            V((4, 2 * HD, WIN), BF16),
            V((2, 4, D, 128), BF16),
            V((2, 4, D, 128), BF16),
            V((2, 4, D, 128), F32),
            V((2, 2, 2 * D, 128), BF16),
            V((2, 2, D // 2, 128), BF16),
            V((2, 2, D // 8, 128), F32),
            V((2, 2, 3, D // 2, 128), BF16),
            V((2, 2, 3, D // 8, 128), BF16),
            V((2, 2, 7, 8, 128), F32),
            V((2, D, BLK), BF16),
            V((2, D, BLK), BF16),
            V((2, D, BLK), F32),
            dma((9,)),
            dma((2 * CHUNKS + 2,)),
            dma((2 * CHUNKS + 2,)),
            dma((5,)),
            dma((5,)),
            dma((2,)),
            dma((2,)),
            dma((2, 3, 2, 7)),
            dma((2, 3, 2, 7)),
            dma((2, 3, 2, 7)),
            dma((2, 3, 2, 7)),
            dma((2, 2)),
            dma((2, 2)),
            dma((2,)),
            dma((2,)),
            pltpu.SemaphoreType.REGULAR((7,)),
        ],
        compiler_params=pltpu.CompilerParams(
            collective_id=0, has_side_effects=True, vmem_limit_bytes=58 * 1024 * 1024
        ),
        name="history_attention",
    )(table, cotangent, stamps, starts, w_query, w_key, w_value, w_out, decay.reshape(1, 2))
    shapes = ((2, BLK, D), (2, BLK, D), (D, BLK), (D, BLK), (D, BLK), (BLK, D))
    return pl.pallas_call(
        finish,
        out_shape=tuple(
            jax.ShapeDtypeStruct(shape, BF16 if n < 2 else F32) for n, shape in enumerate(shapes)
        ),
        in_specs=[vmem] * 3,
        out_specs=(hbm,) * 6,
        scratch_shapes=[V((3, D, BLK), F32), V((BLK, D), F32), dma((6,))],
        compiler_params=pltpu.CompilerParams(vmem_limit_bytes=16 * 1024 * 1024),
        name="finish",
    )(*near)


def solution(mesh):
    return jax.shard_map(
        shards,
        mesh=mesh,
        in_specs=(
            P(None, "tm", None),
            P(None, "tm", None),
            P(None, "tm"),
            P(None, "tm"),
            P(None, "rep"),
            P(None, "rep"),
            P(None, "rep"),
            P("rep", None),
            P("rep"),
        ),
        out_specs=(
            P(None, "tm", None),
            P(None, "tm", None),
            P(None, "rep"),
            P(None, "rep"),
            P(None, "rep"),
            P("rep", None),
        ),
        check_vma=False,
    )
```

```python
import functools
import math

import jax
import jax.numpy as jnp
from jax import lax
from jax.experimental import pallas as pl
from jax.experimental.pallas import tpu as pltpu
from jax.sharding import PartitionSpec as P

HD = 128
BLK = 256
WIN = 3 * BLK
D = 512
NX, NY, NZ = 4, 4, 8
CHUNKS = 4
LOG2E = 1.4426950408889634
MESH = pl.DeviceIdType.MESH
F32 = jnp.float32
BF16 = jnp.bfloat16
ORDERS = (("x", "y", "z"), ("y", "x", "z"))
SIZES = {"x": NX, "y": NY, "z": NZ}
FARTHEST = {4: (2, 1, 3), 8: (4, 3, 5, 2, 6, 1, 7)}


def nt(a, b):
    return lax.dot_general(a, b, (((1,), (1,)), ((), ())), preferred_element_type=F32)


def nn(a, b):
    return jnp.dot(a, b, preferred_element_type=F32)


def kernel(
    tm_size,
    table,
    cot,
    stamps,
    starts,
    wq_in,
    wk_in,
    wv_in,
    wo_in,
    decay,
    mix,
    gtb,
    red,
    xw,
    xT,
    g_s,
    ts_own,
    st_own,
    dec_in,
    ts_near,
    dec_send,
    dec_recv,
    wq,
    wk,
    wv,
    wo,
    mb,
    brow,
    q_s,
    qT_s,
    k_s,
    v_s,
    do_s,
    doT_s,
    o_s,
    dq_s,
    kvT_s,
    psend,
    precv,
    pown,
    b0,
    b1,
    b2,
    rc0,
    rc1,
    rc2,
    ct_send,
    ct_recv,
    ct_own,
    lsem,
    hs,
    hr,
    ws,
    wr,
    ps,
    pr,
    rs_s,
    rs_r,
    ag_s,
    ag_r,
    cs,
    cr,
    ms,
    mr,
    met,
):
    tm = lax.axis_index("tm")
    c = lax.axis_index("rep")
    blocks = 2 * tm_size
    blk = c * (blocks - 1 - 2 * tm) + tm
    coord = {"x": tm // (NZ * NY), "z": (tm // NY) % NZ, "y": tm % NY}

    def holder(pos):
        side = pos // tm_size
        return (side * (blocks - 1 - 2 * pos) + pos, side)

    def partner(axis, d):
        at = dict(coord)
        at[axis] = (coord[axis] + SIZES[axis] + d) % SIZES[axis]
        return ((at["x"] * NZ + at["z"]) * NY + at["y"], c)

    next1 = holder((blk + 1) % blocks)
    pos1 = (blk + blocks - 1) % blocks
    pos2 = (blk + blocks - 2) % blocks
    prev1 = holder(pos1)
    sib = (tm, 1 - c)

    barrier = pltpu.get_barrier_semaphore()
    friends = [next1, prev1, sib]
    for axis in SIZES:
        friends += [partner(axis, 1), partner(axis, -1)]
    for friend in friends:
        pl.semaphore_signal(barrier, inc=1, device_id=friend, device_id_type=MESH)

    loads = [
        pltpu.make_async_copy(src, dst, lsem.at[n])
        for n, (src, dst) in enumerate(
            [
                (stamps, ts_own),
                (starts, st_own),
                (decay, dec_in),
                (table.at[c], xw.at[2]),
                (cot.at[c], g_s),
                (wq_in, wq.at[1]),
                (wk_in, wk.at[1]),
                (wv_in, wv.at[1]),
                (wo_in, wo.at[1]),
            ]
        )
    ]
    for copy in loads:
        copy.start()

    def remote(src, dst, send, recv, to):
        return pltpu.make_async_remote_copy(
            src_ref=src, dst_ref=dst, send_sem=send, recv_sem=recv, device_id=to, device_id_type=MESH
        )

    for copy in loads[:4]:
        copy.wait()
    pl.semaphore_wait(barrier, len(friends))

    def tell(token):
        axis, d, n = token
        pl.semaphore_signal(met.at[n], inc=1, device_id=partner(axis, d), device_id_type=MESH)

    def hear(token):
        pl.semaphore_wait(met.at[token[2]], 1)

    tokens = ([("x", 1, 0), ("y", 1, 1), ("z", 1, 2), ("z", -1, 3)], [("z", 1, 4), ("z", -1, 5)], [("z", 1, 6)])

    chunk = BLK // CHUNKS
    pieces = [pl.ds(n * chunk, chunk) for n in range(CHUNKS)]
    mine = [
        remote(xw.at[2, rows], xw.at[1, rows], hs.at[n], hr.at[n], next1)
        for n, rows in enumerate(pieces)
    ]
    onward = [
        remote(xw.at[1, rows], xw.at[0, rows], hs.at[CHUNKS + n], hr.at[CHUNKS + n], next1)
        for n, rows in enumerate(pieces)
    ]
    times = [
        remote(src, ts_near.at[n], hs.at[2 * CHUNKS + n], hr.at[2 * CHUNKS + n], next1)
        for n, src in enumerate((stamps, ts_near.at[0]))
    ]
    weights = [
        remote(src.at[1], dst.at[0], ws.at[n], wr.at[n], sib)
        for n, (src, dst) in enumerate(((wq, wq), (wk, wk), (wv, wv), (wo, wo)))
    ]
    decays = remote(dec_send, dec_recv, ws.at[4], wr.at[4], sib)
    for copy in times[:1] + mine:
        copy.start()
    for token in tokens[0]:
        tell(token)
    sub = lax.broadcasted_iota(jnp.int32, (8, 128), 0)
    dec_send[...] = jnp.where(sub == 0, dec_in[0, 0], dec_in[0, 1])
    decays.start()
    first_row = jnp.where(c == 0, st_own[0:1, :], st_own[1:2, :]) - (blk - 2) * BLK
    first_col = jnp.transpose(jnp.broadcast_to(first_row.astype(F32), (128, BLK)))
    row_id = lax.broadcasted_iota(jnp.int32, (BLK, 128), 0)
    col_id = lax.broadcasted_iota(jnp.int32, (BLK, 128), 1)
    for n in range(WIN // 128):
        key_id = col_id + n * 128
        ok = (key_id.astype(F32) >= first_col) & (key_id <= row_id + 2 * BLK)
        mb[:, n * 128 : (n + 1) * 128] = jnp.where(ok, 0.0, -1e30)


    def begin(copies):
        for copy in copies:
            copy.start()

    def put_heads(dst, slot, rows, val):
        val = val.astype(BF16)
        for j in range(2):
            dst[2 * slot + j, rows, :] = val[:, j * HD : (j + 1) * HD]
        return val

    every = pl.ds(0, BLK)

    def own_rows(slot):
        x = xw[2]
        val = put_heads(q_s, slot, every, nn(x, wq[slot]))
        for j in range(2):
            qT_s[2 * slot + j] = jnp.transpose(val[:, j * HD : (j + 1) * HD])
        val = put_heads(do_s, slot, every, nt(g_s[...], wo[slot]))
        for j in range(2):
            doT_s[2 * slot + j] = jnp.transpose(val[:, j * HD : (j + 1) * HD])

    def keys_of(part, slot):
        rows = pl.ds(part * BLK, BLK)
        put_heads(k_s, slot, rows, nn(xw[part], wk[slot]))
        put_heads(v_s, slot, rows, nn(xw[part], wv[slot]))

    for copy in loads[4:]:
        copy.wait()
    begin(weights)
    own_rows(1)
    keys_of(2, 1)
    xT[:, 2 * BLK :] = jnp.transpose(xw[2])
    times[0].wait_recv()
    times[1].start()
    for token in tokens[0]:
        hear(token)
    for token in tokens[1]:
        tell(token)
    for n in range(CHUNKS):
        mine[n].wait_recv()
        onward[n].start()
    for token in tokens[1]:
        hear(token)
    for token in tokens[2]:
        tell(token)
    keys_of(1, 1)
    xT[:, BLK : 2 * BLK] = jnp.transpose(xw[1])
    for copy in weights:
        copy.wait_recv()
    own_rows(0)
    keys_of(2, 0)
    keys_of(1, 0)
    for token in tokens[2]:
        hear(token)
    for copy in (times[1], decays):
        copy.wait_recv()
    for copy in onward:
        copy.wait_recv()
    keys_of(0, 0)
    keys_of(0, 1)
    xT[:, :BLK] = jnp.transpose(xw[0])

    def side_row(ref, pos):
        return jnp.where(pos // tm_size == 0, ref[0:1, :], ref[1:2, :])

    own_times = side_row(ts_own, blk)
    base = jnp.max(own_times, axis=1, keepdims=True)
    rel = jnp.concatenate(
        [side_row(ts_near.at[1], pos2), side_row(ts_near.at[0], pos1), own_times], axis=1
    )
    rel = (rel - base).astype(F32) * LOG2E
    for j in range(2):
        brow[j] = rel * dec_recv[j : j + 1, 0:1]
        brow[2 + j] = rel * dec_send[j : j + 1, 0:1]

    inv_scale = 1.0 / math.sqrt(HD)
    psends = [
        remote(psend.at[j], precv.at[j], ps.at[j], pr.at[j], sib) for j in range(2)
    ]

    def products(t):
        return nt(q_s[t], k_s[t]), nt(do_s[t], v_s[t])

    def softmax(t, s, dp):
        s = s * (inv_scale * LOG2E) + (mb[...] + brow[t])
        p = jnp.exp2(s - jnp.max(s, axis=-1, keepdims=True))
        p = p * (1.0 / jnp.sum(p, axis=-1, keepdims=True))
        delta = jnp.sum(p * dp, axis=-1, keepdims=True)
        return p.astype(BF16), (p * (dp - delta)).astype(BF16)

    def attention(t, pb, ds):
        lanes = slice((t % 2) * HD, (t % 2 + 1) * HD)
        o_s[t // 2, :, lanes] = nn(pb, v_s[t]).astype(BF16)
        dq_s[t // 2, :, lanes] = (nn(ds, k_s[t]) * inv_scale).astype(BF16)
        kvT_s[t, :HD, :] = (nn(qT_s[t], ds) * inv_scale).astype(BF16)
        kvT_s[t, HD:, :] = nn(doT_s[t], pb).astype(BF16)

    def weight_grads(t):
        lanes = slice((t % 2) * HD, (t % 2 + 1) * HD)
        kv = nt(xT[...], kvT_s[t])
        go = nn(jnp.transpose(o_s[t // 2, :, lanes]), g_s[...])
        to = psend.at[t] if t < 2 else pown.at[t - 2]
        to[0] = nn(xT[:, 2 * BLK :], dq_s[t // 2, :, lanes]).astype(to.dtype)
        to[1] = kv[:, :HD].astype(to.dtype)
        to[2] = kv[:, HD:].astype(to.dtype)
        for n in range(4):
            to[3, n * HD : (n + 1) * HD, :] = go[:, n * HD : (n + 1) * HD].astype(to.dtype)

    def reduce_pair(j):
        psends[j].wait_recv()
        for n in range(4):
            b0[j, n // 2, (n % 2) * D : (n % 2 + 1) * D, :] = (pown[j, n] + precv[j, n].astype(F32)).astype(BF16)
        begin(scatters[j][0])

    def pass_on(step):
        if step in (0, 2):
            psends[step // 2].start()
        if step == 3:
            reduce_pair(1)
        if step in (1, 2):
            pl.when(c == step - 1)(lambda: reduce_pair(0))

    sources = (b0, b1, b2)
    landing = (rc0, rc1, rc2)
    rows_at = (2 * D, D // 2, D // 8)

    def place(stage, col):
        axis = ORDERS[col][stage]
        return axis, SIZES[axis], rows_at[stage] // SIZES[axis]

    def scatter(j, stage):
        copies = []
        for col in range(2):
            axis, size, piece = place(stage, col)
            for d in FARTHEST[size]:
                there = (coord[axis] + d) % size
                copies.append(
                    remote(
                        sources[stage].at[j, col, pl.ds(pl.multiple_of(there * piece, piece), piece)],
                        landing[stage].at[j, col, d - 1],
                        rs_s.at[j, stage, col, d - 1],
                        rs_r.at[j, stage, col, d - 1],
                        partner(axis, d),
                    )
                )
        return copies

    def gathered(j, stage, col):
        axis, size, piece = place(stage, col)
        total = sources[stage][j, col, pl.ds(pl.multiple_of(coord[axis] * piece, piece), piece), :].astype(F32)
        for d in range(1, size):
            total = total + landing[stage][j, col, d - 1].astype(F32)
        return total

    def first_owner(stage, col):
        owner = 0
        for s in range(stage + 1):
            axis, _, piece = place(s, col)
            owner = owner + coord[axis] * (piece // 8)
        return owner

    def spread(j, stage):
        copies = []
        for col in range(2):
            axis, size, piece = place(stage, col)
            here = pl.ds(first_owner(stage, col), piece // 8)
            for d in FARTHEST[size]:
                copies.append(
                    remote(
                        red.at[col, j, here],
                        red.at[col, j, here],
                        ag_s.at[j, stage, col, d - 1],
                        ag_r.at[j, stage, col, d - 1],
                        partner(axis, d),
                    )
                )
        return copies

    scatters = [[scatter(j, stage) for stage in range(3)] for j in range(2)]
    spreads = [[spread(j, stage) for stage in range(3)] for j in range(2)]

    def arrived(copies):
        for copy in copies:
            copy.wait_recv()

    def next_scatter(j, stage):
        arrived(scatters[j][stage])
        for col in range(2):
            if stage < 2:
                sources[stage + 1][j, col] = gathered(j, stage, col).astype(sources[stage + 1].dtype)
            else:
                red[col, j, first_owner(2, col)] = (gathered(j, 2, col) * scale).astype(BF16)
        begin(scatters[j][stage + 1] if stage < 2 else spreads[j][2])

    def next_spread(j, stage):
        arrived(spreads[j][stage])
        begin(spreads[j][stage - 1])

    scale = 1.0 / math.sqrt(blocks * BLK)
    turn = (0, 2, 1, 3)
    now = products(turn[0])
    for step in range(4):
        later = products(turn[step + 1]) if step < 3 else None
        if step > 0:
            weight_grads(turn[step - 1])
        pb, ds = softmax(turn[step], *now)
        if step > 0:
            pass_on(step - 1)
        attention(turn[step], pb, ds)
        now = later
    weight_grads(turn[3])
    pass_on(3)

    mix[c] = (nn(o_s[0], wo[0]) + nn(o_s[1], wo[1])).astype(BF16)
    to_sib = [
        remote(ref.at[c], ref.at[c], ms.at[n], mr.at[n], sib) for n, ref in enumerate((mix, gtb))
    ]
    to_sib[0].start()
    for part in range(3):
        cols = slice(part * BLK, (part + 1) * BLK)
        total = jnp.zeros((D, BLK), F32)
        for t in range(4):
            lanes = slice((t % 2) * HD, (t % 2 + 1) * HD)
            both = jnp.concatenate([wk[t // 2, :, lanes], wv[t // 2, :, lanes]], axis=1)
            total = total + nn(both, kvT_s[t, :, cols])
        if part == 0:
            ct_send[0] = total.astype(BF16)
        else:
            ct_own[part - 1] = total
    terms = [
        [
            remote(ct_send.at[n, rows], ct_recv.at[n, rows], cs.at[n, h], cr.at[n, h], prev1)
            for h, rows in enumerate((every, pl.ds(BLK, BLK)))
        ]
        for n in range(2)
    ]

    next_scatter(0, 0)
    next_scatter(1, 0)
    gtq = nt(dq_s[0], wq[0]) + nt(dq_s[1], wq[1])
    next_scatter(0, 1)
    begin(terms[0])
    next_scatter(1, 1)
    next_scatter(0, 2)
    for h in range(2):
        terms[0][h].wait_recv()
        rows = slice(h * BLK, (h + 1) * BLK)
        ct_send[1, rows, :] = (ct_own[0, rows, :] + ct_recv[0, rows, :].astype(F32)).astype(BF16)
        terms[1][h].start()
    next_scatter(1, 2)
    next_spread(0, 2)
    next_spread(1, 2)
    next_spread(0, 1)
    arrived(terms[1])
    gtb[c] = (gtq + jnp.transpose(ct_own[1] + ct_recv[1].astype(F32))).astype(BF16)
    to_sib[1].start()
    next_spread(1, 1)
    arrived(to_sib)
    arrived(spreads[0][0])
    arrived(spreads[1][0])
    sent = mine + onward + times + [decays] + weights + psends + terms[0] + terms[1] + to_sib
    for j in range(2):
        for stage in range(3):
            sent += scatters[j][stage] + spreads[j][stage]
    for copy in sent:
        copy.wait_send()


def finish(mix, gtb, red, mixed, gt, grad_q, grad_k, grad_v, grad_o, wide, rows, sem):
    copies = [
        pltpu.make_async_copy(mix, mixed, sem.at[0]),
        pltpu.make_async_copy(gtb, gt, sem.at[1]),
    ]
    copies[0].start()
    copies[1].start()
    for n, out in enumerate((grad_q, grad_k, grad_v, grad_o)):
        half = pl.ds((n % 2) * (D // 8), D // 8)
        for j in range(2):
            val = red[n // 2, j, half].astype(F32).reshape(D, HD)
            if n < 3:
                wide[n, :, j * HD : (j + 1) * HD] = val
            else:
                for k in range(4):
                    rows[j * HD : (j + 1) * HD, k * HD : (k + 1) * HD] = val[k * HD : (k + 1) * HD]
        copies.append(pltpu.make_async_copy(wide.at[n] if n < 3 else rows, out, sem.at[2 + n]))
        copies[-1].start()
    for copy in copies:
        copy.wait()


def shards(table, cotangent, stamps, starts, w_query, w_key, w_value, w_out, decay):
    tm_size = lax.axis_size("tm")
    hbm = pl.BlockSpec(memory_space=pltpu.HBM)
    vmem = pl.BlockSpec(memory_space=pltpu.VMEM)
    dma = pltpu.SemaphoreType.DMA
    V = pltpu.VMEM
    near = (
        V((2, BLK, D), BF16),
        V((2, BLK, D), BF16),
        V((2, 2, 128, 8, 128), BF16),
    )
    near = pl.pallas_call(
        functools.partial(kernel, tm_size),
        out_shape=near,
        in_specs=[hbm] * 9,
        out_specs=(vmem, vmem, vmem),
        scratch_shapes=[
            V((3, BLK, D), BF16),
            V((D, WIN), BF16),
            V((BLK, D), BF16),
            V((2, BLK), jnp.int32),
            V((2, BLK), jnp.int32),
            pltpu.SMEM((1, 2), F32),
            V((2, 2, BLK), jnp.int32),
            V((8, 128), F32),
            V((8, 128), F32),
            V((2, D, BLK), BF16),
            V((2, D, BLK), BF16),
            V((2, D, BLK), BF16),
            V((2, BLK, D), BF16),
            V((BLK, WIN), F32),
            V((4, 1, WIN), F32),
            V((4, BLK, HD), BF16),
            V((4, HD, BLK), BF16),
            V((4, WIN, HD), BF16),
            V((4, WIN, HD), BF16),
            V((4, BLK, HD), BF16),
            V((4, HD, BLK), BF16),
            V((2, BLK, BLK), BF16),
            V((2, BLK, BLK), BF16),
            V((4, 2 * HD, WIN), BF16),
            V((2, 4, D, 128), BF16),
            V((2, 4, D, 128), BF16),
            V((2, 4, D, 128), F32),
            V((2, 2, 2 * D, 128), BF16),
            V((2, 2, D // 2, 128), BF16),
            V((2, 2, D // 8, 128), F32),
            V((2, 2, 3, D // 2, 128), BF16),
            V((2, 2, 3, D // 8, 128), BF16),
            V((2, 2, 7, 8, 128), F32),
            V((2, D, BLK), BF16),
            V((2, D, BLK), BF16),
            V((2, D, BLK), F32),
            dma((9,)),
            dma((2 * CHUNKS + 2,)),
            dma((2 * CHUNKS + 2,)),
            dma((5,)),
            dma((5,)),
            dma((2,)),
            dma((2,)),
            dma((2, 3, 2, 7)),
            dma((2, 3, 2, 7)),
            dma((2, 3, 2, 7)),
            dma((2, 3, 2, 7)),
            dma((2, 2)),
            dma((2, 2)),
            dma((2,)),
            dma((2,)),
            pltpu.SemaphoreType.REGULAR((7,)),
        ],
        compiler_params=pltpu.CompilerParams(
            collective_id=0, has_side_effects=True, vmem_limit_bytes=58 * 1024 * 1024
        ),
        name="history_attention",
    )(table, cotangent, stamps, starts, w_query, w_key, w_value, w_out, decay.reshape(1, 2))
    shapes = ((2, BLK, D), (2, BLK, D), (D, BLK), (D, BLK), (D, BLK), (BLK, D))
    return pl.pallas_call(
        finish,
        out_shape=tuple(
            jax.ShapeDtypeStruct(shape, BF16 if n < 2 else F32) for n, shape in enumerate(shapes)
        ),
        in_specs=[vmem] * 3,
        out_specs=(hbm,) * 6,
        scratch_shapes=[V((3, D, BLK), F32), V((BLK, D), F32), dma((6,))],
        compiler_params=pltpu.CompilerParams(vmem_limit_bytes=16 * 1024 * 1024),
        name="finish",
    )(*near)


def solution(mesh):
    return jax.shard_map(
        shards,
        mesh=mesh,
        in_specs=(
            P(None, "tm", None),
            P(None, "tm", None),
            P(None, "tm"),
            P(None, "tm"),
            P(None, "rep"),
            P(None, "rep"),
            P(None, "rep"),
            P("rep", None),
            P("rep"),
        ),
        out_specs=(
            P(None, "tm", None),
            P(None, "tm", None),
            P(None, "rep"),
            P(None, "rep"),
            P(None, "rep"),
            P("rep", None),
        ),
        check_vma=False,
    )
```

```python
import functools
import math

import jax
import jax.numpy as jnp
from jax import lax
from jax.experimental import pallas as pl
from jax.experimental.pallas import tpu as pltpu
from jax.sharding import PartitionSpec as P

HD = 128
BLK = 256
WIN = 3 * BLK
D = 512
NX, NY, NZ = 4, 4, 8
CHUNKS = 4
LOG2E = 1.4426950408889634
MESH = pl.DeviceIdType.MESH
F32 = jnp.float32
BF16 = jnp.bfloat16
ORDERS = (("x", "y", "z"), ("y", "x", "z"))
SIZES = {"x": NX, "y": NY, "z": NZ}
FARTHEST = {4: (2, 1, 3), 8: (4, 3, 5, 2, 6, 1, 7)}


def nt(a, b):
    return lax.dot_general(a, b, (((1,), (1,)), ((), ())), preferred_element_type=F32)


def nn(a, b):
    return jnp.dot(a, b, preferred_element_type=F32)


def kernel(
    tm_size,
    table,
    cot,
    stamps,
    starts,
    wq_in,
    wk_in,
    wv_in,
    wo_in,
    decay,
    mix,
    gtb,
    red,
    xw,
    xT,
    g_s,
    ts_own,
    st_own,
    dec_in,
    ts_near,
    dec_send,
    dec_recv,
    wq,
    wk,
    wv,
    wo,
    mb,
    brow,
    q_s,
    qT_s,
    k_s,
    v_s,
    do_s,
    doT_s,
    o_s,
    dq_s,
    kvT_s,
    psend,
    precv,
    pown,
    b0,
    b1,
    b2,
    rc0,
    rc1,
    rc2,
    ct_send,
    ct_recv,
    ct_own,
    lsem,
    hs,
    hr,
    ws,
    wr,
    ps,
    pr,
    rs_s,
    rs_r,
    ag_s,
    ag_r,
    cs,
    cr,
    ms,
    mr,
    met,
):
    tm = lax.axis_index("tm")
    c = lax.axis_index("rep")
    blocks = 2 * tm_size
    blk = c * (blocks - 1 - 2 * tm) + tm
    coord = {"x": tm // (NZ * NY), "z": (tm // NY) % NZ, "y": tm % NY}

    def holder(pos):
        side = pos // tm_size
        return (side * (blocks - 1 - 2 * pos) + pos, side)

    def partner(axis, d):
        at = dict(coord)
        at[axis] = (coord[axis] + SIZES[axis] + d) % SIZES[axis]
        return ((at["x"] * NZ + at["z"]) * NY + at["y"], c)

    next1 = holder((blk + 1) % blocks)
    pos1 = (blk + blocks - 1) % blocks
    pos2 = (blk + blocks - 2) % blocks
    prev1 = holder(pos1)
    sib = (tm, 1 - c)

    barrier = pltpu.get_barrier_semaphore()
    friends = [next1, prev1, sib]
    for axis in SIZES:
        friends += [partner(axis, 1), partner(axis, -1)]
    for friend in friends:
        pl.semaphore_signal(barrier, inc=1, device_id=friend, device_id_type=MESH)

    loads = [
        pltpu.make_async_copy(src, dst, lsem.at[n])
        for n, (src, dst) in enumerate(
            [
                (stamps, ts_own),
                (starts, st_own),
                (decay, dec_in),
                (table.at[c], xw.at[2]),
                (cot.at[c], g_s),
                (wq_in, wq.at[1]),
                (wk_in, wk.at[1]),
                (wv_in, wv.at[1]),
                (wo_in, wo.at[1]),
            ]
        )
    ]
    for copy in loads:
        copy.start()

    def remote(src, dst, send, recv, to):
        return pltpu.make_async_remote_copy(
            src_ref=src, dst_ref=dst, send_sem=send, recv_sem=recv, device_id=to, device_id_type=MESH
        )

    for copy in loads[:4]:
        copy.wait()
    pl.semaphore_wait(barrier, len(friends))

    def tell(token):
        axis, d, n = token
        pl.semaphore_signal(met.at[n], inc=1, device_id=partner(axis, d), device_id_type=MESH)

    def hear(token):
        pl.semaphore_wait(met.at[token[2]], 1)

    tokens = ([("x", 1, 0), ("y", 1, 1), ("z", 1, 2), ("z", -1, 3)], [("z", 1, 4), ("z", -1, 5)], [("z", 1, 6)])

    chunk = BLK // CHUNKS
    pieces = [pl.ds(n * chunk, chunk) for n in range(CHUNKS)]
    mine = [
        remote(xw.at[2, rows], xw.at[1, rows], hs.at[0], hr.at[n], next1)
        for n, rows in enumerate(pieces)
    ]
    onward = [
        remote(xw.at[1, rows], xw.at[0, rows], hs.at[1], hr.at[CHUNKS + n], next1)
        for n, rows in enumerate(pieces)
    ]
    times = [
        remote(src, ts_near.at[n], hs.at[2 + n], hr.at[2 * CHUNKS + n], next1)
        for n, src in enumerate((stamps, ts_near.at[0]))
    ]
    weights = [
        remote(src.at[1], dst.at[0], ws.at[n], wr.at[n], sib)
        for n, (src, dst) in enumerate(((wq, wq), (wk, wk), (wv, wv), (wo, wo)))
    ]
    decays = remote(dec_send, dec_recv, ws.at[4], wr.at[4], sib)
    for copy in times[:1] + mine:
        copy.start()
    for token in tokens[0]:
        tell(token)
    sub = lax.broadcasted_iota(jnp.int32, (8, 128), 0)
    dec_send[...] = jnp.where(sub == 0, dec_in[0, 0], dec_in[0, 1])
    decays.start()
    first_row = jnp.where(c == 0, st_own[0:1, :], st_own[1:2, :]) - (blk - 2) * BLK
    first_col = jnp.transpose(jnp.broadcast_to(first_row.astype(F32), (128, BLK)))
    row_id = lax.broadcasted_iota(jnp.int32, (BLK, 128), 0)
    col_id = lax.broadcasted_iota(jnp.int32, (BLK, 128), 1)
    for n in range(WIN // 128):
        key_id = col_id + n * 128
        ok = (key_id.astype(F32) >= first_col) & (key_id <= row_id + 2 * BLK)
        mb[:, n * 128 : (n + 1) * 128] = jnp.where(ok, 0.0, -1e30)


    def begin(copies):
        for copy in copies:
            copy.start()

    def put_heads(dst, slot, rows, val):
        val = val.astype(BF16)
        for j in range(2):
            dst[2 * slot + j, rows, :] = val[:, j * HD : (j + 1) * HD]
        return val

    every = pl.ds(0, BLK)

    def own_rows(slot):
        x = xw[2]
        val = put_heads(q_s, slot, every, nn(x, wq[slot]))
        for j in range(2):
            qT_s[2 * slot + j] = jnp.transpose(val[:, j * HD : (j + 1) * HD])
        val = put_heads(do_s, slot, every, nt(g_s[...], wo[slot]))
        for j in range(2):
            doT_s[2 * slot + j] = jnp.transpose(val[:, j * HD : (j + 1) * HD])

    def keys_of(part, slot):
        rows = pl.ds(part * BLK, BLK)
        put_heads(k_s, slot, rows, nn(xw[part], wk[slot]))
        put_heads(v_s, slot, rows, nn(xw[part], wv[slot]))

    for copy in loads[4:]:
        copy.wait()
    begin(weights)
    own_rows(1)
    keys_of(2, 1)
    xT[:, 2 * BLK :] = jnp.transpose(xw[2])
    times[0].wait_recv()
    times[1].start()
    for token in tokens[0]:
        hear(token)
    for token in tokens[1]:
        tell(token)
    for n in range(CHUNKS):
        mine[n].wait_recv()
        onward[n].start()
    for token in tokens[1]:
        hear(token)
    for token in tokens[2]:
        tell(token)
    keys_of(1, 1)
    xT[:, BLK : 2 * BLK] = jnp.transpose(xw[1])
    for copy in weights:
        copy.wait_recv()
    own_rows(0)
    keys_of(2, 0)
    keys_of(1, 0)
    for token in tokens[2]:
        hear(token)
    for copy in (times[1], decays):
        copy.wait_recv()
    for copy in onward:
        copy.wait_recv()
    keys_of(0, 0)
    keys_of(0, 1)
    xT[:, :BLK] = jnp.transpose(xw[0])

    def side_row(ref, pos):
        return jnp.where(pos // tm_size == 0, ref[0:1, :], ref[1:2, :])

    own_times = side_row(ts_own, blk)
    base = jnp.max(own_times, axis=1, keepdims=True)
    rel = jnp.concatenate(
        [side_row(ts_near.at[1], pos2), side_row(ts_near.at[0], pos1), own_times], axis=1
    )
    rel = (rel - base).astype(F32) * LOG2E
    for j in range(2):
        brow[j] = rel * dec_recv[j : j + 1, 0:1]
        brow[2 + j] = rel * dec_send[j : j + 1, 0:1]

    inv_scale = 1.0 / math.sqrt(HD)
    psends = [
        remote(psend.at[j], precv.at[j], ps.at[j], pr.at[j], sib) for j in range(2)
    ]

    def products(t):
        return nt(q_s[t], k_s[t]), nt(do_s[t], v_s[t])

    def softmax(t, s, dp):
        s = s * (inv_scale * LOG2E) + (mb[...] + brow[t])
        p = jnp.exp2(s - jnp.max(s, axis=-1, keepdims=True))
        p = p * (1.0 / jnp.sum(p, axis=-1, keepdims=True))
        delta = jnp.sum(p * dp, axis=-1, keepdims=True)
        return p.astype(BF16), (p * (dp - delta)).astype(BF16)

    def attention(t, pb, ds):
        lanes = slice((t % 2) * HD, (t % 2 + 1) * HD)
        o_s[t // 2, :, lanes] = nn(pb, v_s[t]).astype(BF16)
        dq_s[t // 2, :, lanes] = (nn(ds, k_s[t]) * inv_scale).astype(BF16)
        kvT_s[t, :HD, :] = (nn(qT_s[t], ds) * inv_scale).astype(BF16)
        kvT_s[t, HD:, :] = nn(doT_s[t], pb).astype(BF16)

    def weight_grads(t):
        lanes = slice((t % 2) * HD, (t % 2 + 1) * HD)
        kv = nt(xT[...], kvT_s[t])
        go = nn(jnp.transpose(o_s[t // 2, :, lanes]), g_s[...])
        to = psend.at[t] if t < 2 else pown.at[t - 2]
        to[0] = nn(xT[:, 2 * BLK :], dq_s[t // 2, :, lanes]).astype(to.dtype)
        to[1] = kv[:, :HD].astype(to.dtype)
        to[2] = kv[:, HD:].astype(to.dtype)
        for n in range(4):
            to[3, n * HD : (n + 1) * HD, :] = go[:, n * HD : (n + 1) * HD].astype(to.dtype)

    def reduce_pair(j):
        psends[j].wait_recv()
        for n in range(4):
            b0[j, n // 2, (n % 2) * D : (n % 2 + 1) * D, :] = (pown[j, n] + precv[j, n].astype(F32)).astype(BF16)
        begin(scatters[j][0])

    def pass_on(step):
        if step in (0, 2):
            psends[step // 2].start()
        if step == 3:
            reduce_pair(1)
        if step in (1, 2):
            pl.when(c == step - 1)(lambda: reduce_pair(0))

    sources = (b0, b1, b2)
    landing = (rc0, rc1, rc2)
    rows_at = (2 * D, D // 2, D // 8)

    def place(stage, col):
        axis = ORDERS[col][stage]
        return axis, SIZES[axis], rows_at[stage] // SIZES[axis]

    def scatter(j, stage):
        copies = []
        for col in range(2):
            axis, size, piece = place(stage, col)
            for d in FARTHEST[size]:
                there = (coord[axis] + d) % size
                copies.append(
                    remote(
                        sources[stage].at[j, col, pl.ds(pl.multiple_of(there * piece, piece), piece)],
                        landing[stage].at[j, col, d - 1],
                        rs_s.at[j, stage],
                        rs_r.at[j, stage],
                        partner(axis, d),
                    )
                )
        return copies

    def gathered(j, stage, col):
        axis, size, piece = place(stage, col)
        total = sources[stage][j, col, pl.ds(pl.multiple_of(coord[axis] * piece, piece), piece), :].astype(F32)
        for d in range(1, size):
            total = total + landing[stage][j, col, d - 1].astype(F32)
        return total

    def first_owner(stage, col):
        owner = 0
        for s in range(stage + 1):
            axis, _, piece = place(s, col)
            owner = owner + coord[axis] * (piece // 8)
        return owner

    def spread(j, stage):
        copies = []
        for col in range(2):
            axis, size, piece = place(stage, col)
            here = pl.ds(first_owner(stage, col), piece // 8)
            for d in FARTHEST[size]:
                copies.append(
                    remote(
                        red.at[col, j, here],
                        red.at[col, j, here],
                        ag_s.at[j, stage],
                        ag_r.at[j, stage],
                        partner(axis, d),
                    )
                )
        return copies

    def whole_scatter(j, stage):
        ref = landing[stage].at[j]
        return remote(ref, ref, rs_s.at[j, stage], rs_r.at[j, stage], sib)

    def whole_spread(j, stage):
        _, size, piece = place(stage, 0)
        ref = red.at[:, j, pl.ds(0, (size - 1) * (piece // 8))]
        return remote(ref, ref, ag_s.at[j, stage], ag_r.at[j, stage], sib)

    scatters = [[scatter(j, stage) for stage in range(3)] for j in range(2)]
    spreads = [[spread(j, stage) for stage in range(3)] for j in range(2)]

    def arrived(copies):
        for copy in copies:
            copy.wait_recv()

    def next_scatter(j, stage):
        whole_scatter(j, stage).wait_recv()
        for col in range(2):
            if stage < 2:
                sources[stage + 1][j, col] = gathered(j, stage, col).astype(sources[stage + 1].dtype)
            else:
                red[col, j, first_owner(2, col)] = (gathered(j, 2, col) * scale).astype(BF16)
        begin(scatters[j][stage + 1] if stage < 2 else spreads[j][2])

    def next_spread(j, stage):
        whole_spread(j, stage).wait_recv()
        begin(spreads[j][stage - 1])

    scale = 1.0 / math.sqrt(blocks * BLK)
    turn = (0, 2, 1, 3)
    now = products(turn[0])
    for step in range(4):
        later = products(turn[step + 1]) if step < 3 else None
        if step > 0:
            weight_grads(turn[step - 1])
        pb, ds = softmax(turn[step], *now)
        if step > 0:
            pass_on(step - 1)
        attention(turn[step], pb, ds)
        now = later
    weight_grads(turn[3])
    pass_on(3)

    mix[c] = (nn(o_s[0], wo[0]) + nn(o_s[1], wo[1])).astype(BF16)
    to_sib = [
        remote(ref.at[c], ref.at[c], ms.at[n], mr.at[n], sib) for n, ref in enumerate((mix, gtb))
    ]
    to_sib[0].start()
    for part in range(3):
        cols = slice(part * BLK, (part + 1) * BLK)
        total = jnp.zeros((D, BLK), F32)
        for t in range(4):
            lanes = slice((t % 2) * HD, (t % 2 + 1) * HD)
            both = jnp.concatenate([wk[t // 2, :, lanes], wv[t // 2, :, lanes]], axis=1)
            total = total + nn(both, kvT_s[t, :, cols])
        if part == 0:
            ct_send[0] = total.astype(BF16)
        else:
            ct_own[part - 1] = total
    terms = [
        [
            remote(ct_send.at[n, rows], ct_recv.at[n, rows], cs.at[n, h], cr.at[n, h], prev1)
            for h, rows in enumerate((every, pl.ds(BLK, BLK)))
        ]
        for n in range(2)
    ]

    next_scatter(0, 0)
    next_scatter(1, 0)
    gtq = nt(dq_s[0], wq[0]) + nt(dq_s[1], wq[1])
    next_scatter(0, 1)
    begin(terms[0])
    next_scatter(1, 1)
    next_scatter(0, 2)
    for h in range(2):
        terms[0][h].wait_recv()
        rows = slice(h * BLK, (h + 1) * BLK)
        ct_send[1, rows, :] = (ct_own[0, rows, :] + ct_recv[0, rows, :].astype(F32)).astype(BF16)
        terms[1][h].start()
    next_scatter(1, 2)
    next_spread(0, 2)
    next_spread(1, 2)
    next_spread(0, 1)
    arrived(terms[1])
    gtb[c] = (gtq + jnp.transpose(ct_own[1] + ct_recv[1].astype(F32))).astype(BF16)
    to_sib[1].start()
    next_spread(1, 1)
    arrived(to_sib)
    whole_spread(0, 0).wait_recv()
    whole_spread(1, 0).wait_recv()
    sent = [remote(xw.at[0], xw.at[0], hs.at[n], hr.at[n], next1) for n in range(2)]
    sent += times + [decays] + weights + psends + terms[0] + terms[1] + to_sib
    for j in range(2):
        for stage in range(3):
            sent += [whole_scatter(j, stage), whole_spread(j, stage)]
    for copy in sent:
        copy.wait_send()


def finish(mix, gtb, red, mixed, gt, grad_q, grad_k, grad_v, grad_o, wide, rows, sem):
    copies = [
        pltpu.make_async_copy(mix, mixed, sem.at[0]),
        pltpu.make_async_copy(gtb, gt, sem.at[1]),
    ]
    copies[0].start()
    copies[1].start()
    for n, out in enumerate((grad_q, grad_k, grad_v, grad_o)):
        half = pl.ds((n % 2) * (D // 8), D // 8)
        for j in range(2):
            val = red[n // 2, j, half].astype(F32).reshape(D, HD)
            if n < 3:
                wide[n, :, j * HD : (j + 1) * HD] = val
            else:
                for k in range(4):
                    rows[j * HD : (j + 1) * HD, k * HD : (k + 1) * HD] = val[k * HD : (k + 1) * HD]
        copies.append(pltpu.make_async_copy(wide.at[n] if n < 3 else rows, out, sem.at[2 + n]))
        copies[-1].start()
    for copy in copies:
        copy.wait()


def shards(table, cotangent, stamps, starts, w_query, w_key, w_value, w_out, decay):
    tm_size = lax.axis_size("tm")
    hbm = pl.BlockSpec(memory_space=pltpu.HBM)
    vmem = pl.BlockSpec(memory_space=pltpu.VMEM)
    dma = pltpu.SemaphoreType.DMA
    V = pltpu.VMEM
    near = (
        V((2, BLK, D), BF16),
        V((2, BLK, D), BF16),
        V((2, 2, 128, 8, 128), BF16),
    )
    near = pl.pallas_call(
        functools.partial(kernel, tm_size),
        out_shape=near,
        in_specs=[hbm] * 9,
        out_specs=(vmem, vmem, vmem),
        scratch_shapes=[
            V((3, BLK, D), BF16),
            V((D, WIN), BF16),
            V((BLK, D), BF16),
            V((2, BLK), jnp.int32),
            V((2, BLK), jnp.int32),
            pltpu.SMEM((1, 2), F32),
            V((2, 2, BLK), jnp.int32),
            V((8, 128), F32),
            V((8, 128), F32),
            V((2, D, BLK), BF16),
            V((2, D, BLK), BF16),
            V((2, D, BLK), BF16),
            V((2, BLK, D), BF16),
            V((BLK, WIN), F32),
            V((4, 1, WIN), F32),
            V((4, BLK, HD), BF16),
            V((4, HD, BLK), BF16),
            V((4, WIN, HD), BF16),
            V((4, WIN, HD), BF16),
            V((4, BLK, HD), BF16),
            V((4, HD, BLK), BF16),
            V((2, BLK, BLK), BF16),
            V((2, BLK, BLK), BF16),
            V((4, 2 * HD, WIN), BF16),
            V((2, 4, D, 128), BF16),
            V((2, 4, D, 128), BF16),
            V((2, 4, D, 128), F32),
            V((2, 2, 2 * D, 128), BF16),
            V((2, 2, D // 2, 128), BF16),
            V((2, 2, D // 8, 128), F32),
            V((2, 2, 3, D // 2, 128), BF16),
            V((2, 2, 3, D // 8, 128), BF16),
            V((2, 2, 7, 8, 128), F32),
            V((2, D, BLK), BF16),
            V((2, D, BLK), BF16),
            V((2, D, BLK), F32),
            dma((9,)),
            dma((4,)),
            dma((2 * CHUNKS + 2,)),
            dma((5,)),
            dma((5,)),
            dma((2,)),
            dma((2,)),
            dma((2, 3)),
            dma((2, 3)),
            dma((2, 3)),
            dma((2, 3)),
            dma((2, 2)),
            dma((2, 2)),
            dma((2,)),
            dma((2,)),
            pltpu.SemaphoreType.REGULAR((7,)),
        ],
        compiler_params=pltpu.CompilerParams(
            collective_id=0, has_side_effects=True, vmem_limit_bytes=58 * 1024 * 1024
        ),
        name="history_attention",
    )(table, cotangent, stamps, starts, w_query, w_key, w_value, w_out, decay.reshape(1, 2))
    shapes = ((2, BLK, D), (2, BLK, D), (D, BLK), (D, BLK), (D, BLK), (BLK, D))
    return pl.pallas_call(
        finish,
        out_shape=tuple(
            jax.ShapeDtypeStruct(shape, BF16 if n < 2 else F32) for n, shape in enumerate(shapes)
        ),
        in_specs=[vmem] * 3,
        out_specs=(hbm,) * 6,
        scratch_shapes=[V((3, D, BLK), F32), V((BLK, D), F32), dma((6,))],
        compiler_params=pltpu.CompilerParams(vmem_limit_bytes=16 * 1024 * 1024),
        name="finish",
    )(*near)


def solution(mesh):
    return jax.shard_map(
        shards,
        mesh=mesh,
        in_specs=(
            P(None, "tm", None),
            P(None, "tm", None),
            P(None, "tm"),
            P(None, "tm"),
            P(None, "rep"),
            P(None, "rep"),
            P(None, "rep"),
            P("rep", None),
            P("rep"),
        ),
        out_specs=(
            P(None, "tm", None),
            P(None, "tm", None),
            P(None, "rep"),
            P(None, "rep"),
            P(None, "rep"),
            P("rep", None),
        ),
        check_vma=False,
    )
```

```python
import functools
import math

import jax
import jax.numpy as jnp
from jax import lax
from jax.experimental import pallas as pl
from jax.experimental.pallas import tpu as pltpu
from jax.sharding import PartitionSpec as P

HD = 128
BLK = 256
WIN = 3 * BLK
D = 512
NX, NY, NZ = 4, 4, 8
CHUNKS = 4
LOG2E = 1.4426950408889634
MESH = pl.DeviceIdType.MESH
F32 = jnp.float32
BF16 = jnp.bfloat16
ORDERS = (("x", "y", "z"), ("y", "x", "z"))
SIZES = {"x": NX, "y": NY, "z": NZ}
FARTHEST = {4: (2, 1, 3), 8: (4, 3, 5, 2, 6, 1, 7)}


def nt(a, b):
    return lax.dot_general(a, b, (((1,), (1,)), ((), ())), preferred_element_type=F32)


def nn(a, b):
    return jnp.dot(a, b, preferred_element_type=F32)


def kernel(
    tm_size,
    table,
    cot,
    stamps,
    starts,
    wq_in,
    wk_in,
    wv_in,
    wo_in,
    decay,
    mix,
    gtb,
    red,
    xw,
    xT,
    g_s,
    ts_own,
    st_own,
    dec_in,
    ts_near,
    dec_send,
    dec_recv,
    wq,
    wk,
    wv,
    wo,
    mb,
    brow,
    s_pre,
    dp_pre,
    q_s,
    qT_s,
    k_s,
    v_s,
    do_s,
    doT_s,
    o_s,
    dq_s,
    kvT_s,
    psend,
    precv,
    pown,
    b0,
    b1,
    b2,
    rc0,
    rc1,
    rc2,
    ct_send,
    ct_recv,
    ct_own,
    lsem,
    hs,
    hr,
    ws,
    wr,
    ps,
    pr,
    rs_s,
    rs_r,
    ag_s,
    ag_r,
    cs,
    cr,
    ms,
    mr,
    met,
):
    tm = lax.axis_index("tm")
    c = lax.axis_index("rep")
    blocks = 2 * tm_size
    blk = c * (blocks - 1 - 2 * tm) + tm
    coord = {"x": tm // (NZ * NY), "z": (tm // NY) % NZ, "y": tm % NY}

    def holder(pos):
        side = pos // tm_size
        return (side * (blocks - 1 - 2 * pos) + pos, side)

    def partner(axis, d):
        at = dict(coord)
        at[axis] = (coord[axis] + SIZES[axis] + d) % SIZES[axis]
        return ((at["x"] * NZ + at["z"]) * NY + at["y"], c)

    next1 = holder((blk + 1) % blocks)
    pos1 = (blk + blocks - 1) % blocks
    pos2 = (blk + blocks - 2) % blocks
    prev1 = holder(pos1)
    sib = (tm, 1 - c)

    barrier = pltpu.get_barrier_semaphore()
    friends = [next1, prev1, sib]
    for axis in SIZES:
        friends += [partner(axis, 1), partner(axis, -1)]
    for friend in friends:
        pl.semaphore_signal(barrier, inc=1, device_id=friend, device_id_type=MESH)

    loads = [
        pltpu.make_async_copy(src, dst, lsem.at[n])
        for n, (src, dst) in enumerate(
            [
                (stamps, ts_own),
                (starts, st_own),
                (decay, dec_in),
                (table.at[c], xw.at[2]),
                (cot.at[c], g_s),
                (wq_in, wq.at[1]),
                (wk_in, wk.at[1]),
                (wv_in, wv.at[1]),
                (wo_in, wo.at[1]),
            ]
        )
    ]
    for copy in loads:
        copy.start()

    def remote(src, dst, send, recv, to):
        return pltpu.make_async_remote_copy(
            src_ref=src, dst_ref=dst, send_sem=send, recv_sem=recv, device_id=to, device_id_type=MESH
        )

    for copy in loads[:4]:
        copy.wait()
    pl.semaphore_wait(barrier, len(friends))

    def tell(token):
        axis, d, n = token
        pl.semaphore_signal(met.at[n], inc=1, device_id=partner(axis, d), device_id_type=MESH)

    tokens = ([("x", 1, 0), ("y", 1, 0), ("z", 1, 0), ("z", -1, 0)], [("z", 1, 1), ("z", -1, 1)], [("z", 1, 2)])

    def hear(n):
        pl.semaphore_wait(met.at[n], len(tokens[n]))

    chunk = BLK // CHUNKS
    pieces = [pl.ds(n * chunk, chunk) for n in range(CHUNKS)]
    mine = [
        remote(xw.at[2, rows], xw.at[1, rows], hs.at[0], hr.at[n], next1)
        for n, rows in enumerate(pieces)
    ]
    onward = [
        remote(xw.at[1, rows], xw.at[0, rows], hs.at[1], hr.at[CHUNKS + n], next1)
        for n, rows in enumerate(pieces)
    ]
    times = [
        remote(src, ts_near.at[n], hs.at[2 + n], hr.at[2 * CHUNKS + n], next1)
        for n, src in enumerate((stamps, ts_near.at[0]))
    ]
    weights = [
        remote(src.at[1], dst.at[0], ws.at[0], wr.at[0], sib)
        for n, (src, dst) in enumerate(((wq, wq), (wk, wk), (wv, wv), (wo, wo)))
    ]
    decays = remote(dec_send, dec_recv, ws.at[1], wr.at[1], sib)
    for copy in times[:1] + mine:
        copy.start()
    for token in tokens[0]:
        tell(token)
    sub = lax.broadcasted_iota(jnp.int32, (8, 128), 0)
    dec_send[...] = jnp.where(sub == 0, dec_in[0, 0], dec_in[0, 1])
    decays.start()
    first_row = jnp.where(c == 0, st_own[0:1, :], st_own[1:2, :]) - (blk - 2) * BLK
    first_col = jnp.transpose(jnp.broadcast_to(first_row.astype(F32), (128, BLK)))
    row_id = lax.broadcasted_iota(jnp.int32, (BLK, 128), 0)
    col_id = lax.broadcasted_iota(jnp.int32, (BLK, 128), 1)
    for n in range(WIN // 128):
        key_id = col_id + n * 128
        ok = (key_id.astype(F32) >= first_col) & (key_id <= row_id + 2 * BLK)
        mb[:, n * 128 : (n + 1) * 128] = jnp.where(ok, 0.0, -1e30)


    def begin(copies):
        for copy in copies:
            copy.start()

    def put_heads(dst, slot, rows, val):
        val = val.astype(BF16)
        for j in range(2):
            dst[2 * slot + j, rows, :] = val[:, j * HD : (j + 1) * HD]
        return val

    every = pl.ds(0, BLK)

    def own_rows(slot):
        x = xw[2]
        val = put_heads(q_s, slot, every, nn(x, wq[slot]))
        for j in range(2):
            qT_s[2 * slot + j] = jnp.transpose(val[:, j * HD : (j + 1) * HD])
        val = put_heads(do_s, slot, every, nt(g_s[...], wo[slot]))
        for j in range(2):
            doT_s[2 * slot + j] = jnp.transpose(val[:, j * HD : (j + 1) * HD])

    def keys_of(part, slot):
        rows = pl.ds(part * BLK, BLK)
        put_heads(k_s, slot, rows, nn(xw[part], wk[slot]))
        put_heads(v_s, slot, rows, nn(xw[part], wv[slot]))

    for copy in loads[4:]:
        copy.wait()
    begin(weights)
    own_rows(1)
    keys_of(2, 1)
    xT[:, 2 * BLK :] = jnp.transpose(xw[2])

    def side_row(ref, pos):
        return jnp.where(pos // tm_size == 0, ref[0:1, :], ref[1:2, :])

    own_times = side_row(ts_own, blk)
    base = jnp.max(own_times, axis=1, keepdims=True)
    inv_scale = 1.0 / math.sqrt(HD)

    def columns(part):
        return slice(part * BLK, (part + 1) * BLK)

    def decay_terms(part, times_row):
        rel = (times_row - base).astype(F32) * LOG2E
        for h in range(4):
            rate = (dec_recv, dec_send)[h // 2][h % 2 : h % 2 + 1, 0:1]
            brow[h, :, columns(part)] = rel * rate

    def scores(h, part):
        raw = nt(q_s[h], k_s[h, columns(part), :]) * (inv_scale * LOG2E)
        return raw + (mb[:, columns(part)] + brow[h, :, columns(part)])

    def early(h, part):
        s_pre[h, :, columns(part - 1)] = scores(h, part)
        dp_pre[h, :, columns(part - 1)] = nt(do_s[h], v_s[h, columns(part), :])

    all_weights = remote(psend, psend, ws.at[0], wr.at[0], sib)
    all_weights.wait_recv()
    decays.wait_recv()
    own_rows(0)
    keys_of(2, 0)
    decay_terms(2, own_times)
    times[0].wait_recv()
    times[1].start()
    hear(0)
    for token in tokens[1]:
        tell(token)
    for n in range(CHUNKS):
        mine[n].wait_recv()
        onward[n].start()
        early(n, 2)
    hear(1)
    for token in tokens[2]:
        tell(token)
    keys_of(1, 1)
    keys_of(1, 0)
    xT[:, BLK : 2 * BLK] = jnp.transpose(xw[1])
    decay_terms(1, side_row(ts_near.at[0], pos1))
    for h in range(4):
        early(h, 1)
    hear(2)
    times[1].wait_recv()
    decay_terms(0, side_row(ts_near.at[1], pos2))
    for copy in onward:
        copy.wait_recv()
    keys_of(0, 0)
    keys_of(0, 1)
    xT[:, :BLK] = jnp.transpose(xw[0])

    psends = [
        remote(psend.at[j], precv.at[j], ps.at[0], pr.at[j], sib) for j in range(2)
    ]

    def products(t):
        return scores(t, 0), nt(do_s[t], v_s[t, :BLK, :])

    def softmax(t, s, dp):
        s = jnp.concatenate([s, s_pre[t]], axis=1)
        dp = jnp.concatenate([dp, dp_pre[t]], axis=1)
        p = jnp.exp2(s - jnp.max(s, axis=-1, keepdims=True))
        p = p * (1.0 / jnp.sum(p, axis=-1, keepdims=True))
        delta = jnp.sum(p * dp, axis=-1, keepdims=True)
        return p.astype(BF16), (p * (dp - delta)).astype(BF16)

    def attention(t, pb, ds):
        lanes = slice((t % 2) * HD, (t % 2 + 1) * HD)
        o_s[t // 2, :, lanes] = nn(pb, v_s[t]).astype(BF16)
        dq_s[t // 2, :, lanes] = (nn(ds, k_s[t]) * inv_scale).astype(BF16)
        kvT_s[t, :HD, :] = (nn(qT_s[t], ds) * inv_scale).astype(BF16)
        kvT_s[t, HD:, :] = nn(doT_s[t], pb).astype(BF16)

    def weight_grads(t):
        lanes = slice((t % 2) * HD, (t % 2 + 1) * HD)
        kv = nt(xT[...], kvT_s[t])
        go = nn(jnp.transpose(o_s[t // 2, :, lanes]), g_s[...])
        to = psend.at[t] if t < 2 else pown.at[t - 2]
        to[0] = nn(xT[:, 2 * BLK :], dq_s[t // 2, :, lanes]).astype(to.dtype)
        to[1] = kv[:, :HD].astype(to.dtype)
        to[2] = kv[:, HD:].astype(to.dtype)
        for n in range(4):
            to[3, n * HD : (n + 1) * HD, :] = go[:, n * HD : (n + 1) * HD].astype(to.dtype)

    def reduce_pair(j):
        psends[j].wait_recv()
        for n in range(4):
            b0[j, n // 2, (n % 2) * D : (n % 2 + 1) * D, :] = (pown[j, n] + precv[j, n].astype(F32)).astype(BF16)
        begin(scatters[j][0])

    def pass_on(step):
        if step in (0, 2):
            psends[step // 2].start()
        if step == 3:
            reduce_pair(1)
        if step in (1, 2):
            pl.when(c == step - 1)(lambda: reduce_pair(0))

    sources = (b0, b1, b2)
    landing = (rc0, rc1, rc2)
    rows_at = (2 * D, D // 2, D // 8)

    def place(stage, col):
        axis = ORDERS[col][stage]
        return axis, SIZES[axis], rows_at[stage] // SIZES[axis]

    def scatter(j, stage):
        copies = []
        for col in range(2):
            axis, size, piece = place(stage, col)
            for d in FARTHEST[size]:
                there = (coord[axis] + d) % size
                copies.append(
                    remote(
                        sources[stage].at[j, col, pl.ds(pl.multiple_of(there * piece, piece), piece)],
                        landing[stage].at[j, col, d - 1],
                        rs_s.at[j, stage],
                        rs_r.at[j, stage],
                        partner(axis, d),
                    )
                )
        return copies

    def gathered(j, stage, col):
        axis, size, piece = place(stage, col)
        total = sources[stage][j, col, pl.ds(pl.multiple_of(coord[axis] * piece, piece), piece), :].astype(F32)
        for d in range(1, size):
            total = total + landing[stage][j, col, d - 1].astype(F32)
        return total

    def first_owner(stage, col):
        owner = 0
        for s in range(stage + 1):
            axis, _, piece = place(s, col)
            owner = owner + coord[axis] * (piece // 8)
        return owner

    def spread(j, stage):
        copies = []
        for col in range(2):
            axis, size, piece = place(stage, col)
            here = pl.ds(first_owner(stage, col), piece // 8)
            for d in FARTHEST[size]:
                copies.append(
                    remote(
                        red.at[col, j, here],
                        red.at[col, j, here],
                        ag_s.at[j, stage],
                        ag_r.at[j, stage],
                        partner(axis, d),
                    )
                )
        return copies

    def spread_last(j):
        own, others = [], []
        for col in range(2):
            axis, size, _ = place(0, col)
            second, count, piece = place(1, col)
            base = coord[axis] * count
            for e in range(count):
                here = pl.ds((base + (coord[second] + e) % count) * (piece // 8), piece // 8)
                for d in FARTHEST[size]:
                    (others if e else own).append(
                        remote(
                            red.at[col, j, here],
                            red.at[col, j, here],
                            ag_s.at[j, 0],
                            ag_r.at[j, 0],
                            partner(axis, d),
                        )
                    )
        return own, others

    def whole_scatter(j, stage):
        ref = landing[stage].at[j]
        return remote(ref, ref, rs_s.at[j, stage], rs_r.at[j, stage], sib)

    def whole_spread(j, stage):
        _, size, piece = place(stage, 0)
        ref = red.at[:, j, pl.ds(0, (size - 1) * (piece // 8))]
        return remote(ref, ref, ag_s.at[j, stage], ag_r.at[j, stage], sib)

    scatters = [[scatter(j, stage) for stage in range(3)] for j in range(2)]
    spreads = [[None, spread(j, 1), spread(j, 2)] for j in range(2)]
    lasts = [spread_last(j) for j in range(2)]

    def arrived(copies):
        for copy in copies:
            copy.wait_recv()

    def next_scatter(j, stage):
        whole_scatter(j, stage).wait_recv()
        for col in range(2):
            if stage < 2:
                sources[stage + 1][j, col] = gathered(j, stage, col).astype(sources[stage + 1].dtype)
            else:
                red[col, j, first_owner(2, col)] = (gathered(j, 2, col) * scale).astype(BF16)
        begin(scatters[j][stage + 1] if stage < 2 else spreads[j][2])

    def next_spread(j, stage):
        whole_spread(j, stage).wait_recv()
        if stage == 2:
            begin(spreads[j][1])
        begin(lasts[j][2 - stage])

    scale = 1.0 / math.sqrt(blocks * BLK)
    turn = (0, 2, 1, 3)
    now = products(turn[0])
    for step in range(4):
        later = products(turn[step + 1]) if step < 3 else None
        if step > 0:
            weight_grads(turn[step - 1])
        pb, ds = softmax(turn[step], *now)
        if step > 0:
            pass_on(step - 1)
        attention(turn[step], pb, ds)
        now = later
    weight_grads(turn[3])
    pass_on(3)

    mix[c] = (nn(o_s[0], wo[0]) + nn(o_s[1], wo[1])).astype(BF16)
    to_sib = [
        remote(ref.at[c], ref.at[c], ms.at[0], mr.at[0], sib) for n, ref in enumerate((mix, gtb))
    ]
    to_sib[0].start()
    for part in range(3):
        cols = slice(part * BLK, (part + 1) * BLK)
        total = jnp.zeros((D, BLK), F32)
        for t in range(4):
            lanes = slice((t % 2) * HD, (t % 2 + 1) * HD)
            both = jnp.concatenate([wk[t // 2, :, lanes], wv[t // 2, :, lanes]], axis=1)
            total = total + nn(both, kvT_s[t, :, cols])
        if part == 0:
            ct_send[0] = total.astype(BF16)
        else:
            ct_own[part - 1] = total
    terms = [
        [
            remote(ct_send.at[n, rows], ct_recv.at[n, rows], cs.at[0], cr.at[n, h], prev1)
            for h, rows in enumerate((every, pl.ds(BLK, BLK)))
        ]
        for n in range(2)
    ]

    next_scatter(0, 0)
    next_scatter(1, 0)
    gtq = nt(dq_s[0], wq[0]) + nt(dq_s[1], wq[1])
    next_scatter(0, 1)
    begin(terms[0])
    next_scatter(1, 1)
    next_scatter(0, 2)
    for h in range(2):
        terms[0][h].wait_recv()
        rows = slice(h * BLK, (h + 1) * BLK)
        ct_send[1, rows, :] = (ct_own[0, rows, :] + ct_recv[0, rows, :].astype(F32)).astype(BF16)
        terms[1][h].start()
    next_scatter(1, 2)
    next_spread(0, 2)
    next_spread(1, 2)
    next_spread(0, 1)
    arrived(terms[1])
    gtb[c] = (gtq + jnp.transpose(ct_own[1] + ct_recv[1].astype(F32))).astype(BF16)
    to_sib[1].start()
    next_spread(1, 1)
    both = remote(mix, mix, ms.at[0], mr.at[0], sib)
    both.wait_recv()
    whole_spread(0, 0).wait_recv()
    whole_spread(1, 0).wait_recv()
    sent = [remote(xw.at[0], xw.at[0], hs.at[n], hr.at[n], next1) for n in range(2)]
    sent += times + [decays, all_weights, both]
    sent += [remote(psend, psend, ps.at[0], pr.at[0], sib)]
    sent += [remote(ct_send, ct_send, cs.at[0], cr.at[0, 0], prev1)]
    for j in range(2):
        for stage in range(3):
            sent += [whole_scatter(j, stage), whole_spread(j, stage)]
    for copy in sent:
        copy.wait_send()


def finish(mix, gtb, red, mixed, gt, grad_q, grad_k, grad_v, grad_o, wide, rows, sem):
    copies = [
        pltpu.make_async_copy(mix, mixed, sem.at[0]),
        pltpu.make_async_copy(gtb, gt, sem.at[1]),
    ]
    copies[0].start()
    copies[1].start()
    for n, out in enumerate((grad_q, grad_k, grad_v, grad_o)):
        half = pl.ds((n % 2) * (D // 8), D // 8)
        for j in range(2):
            val = red[n // 2, j, half].astype(F32).reshape(D, HD)
            if n < 3:
                wide[n, :, j * HD : (j + 1) * HD] = val
            else:
                for k in range(4):
                    rows[j * HD : (j + 1) * HD, k * HD : (k + 1) * HD] = val[k * HD : (k + 1) * HD]
        copies.append(pltpu.make_async_copy(wide.at[n] if n < 3 else rows, out, sem.at[2 + n]))
        copies[-1].start()
    for copy in copies:
        copy.wait()


def shards(table, cotangent, stamps, starts, w_query, w_key, w_value, w_out, decay):
    tm_size = lax.axis_size("tm")
    hbm = pl.BlockSpec(memory_space=pltpu.HBM)
    vmem = pl.BlockSpec(memory_space=pltpu.VMEM)
    dma = pltpu.SemaphoreType.DMA
    V = pltpu.VMEM
    near = (
        V((2, BLK, D), BF16),
        V((2, BLK, D), BF16),
        V((2, 2, 128, 8, 128), BF16),
    )
    near = pl.pallas_call(
        functools.partial(kernel, tm_size),
        out_shape=near,
        in_specs=[hbm] * 9,
        out_specs=(vmem, vmem, vmem),
        scratch_shapes=[
            V((3, BLK, D), BF16),
            V((D, WIN), BF16),
            V((BLK, D), BF16),
            V((2, BLK), jnp.int32),
            V((2, BLK), jnp.int32),
            pltpu.SMEM((1, 2), F32),
            V((2, 2, BLK), jnp.int32),
            V((8, 128), F32),
            V((8, 128), F32),
            V((2, D, BLK), BF16),
            V((2, D, BLK), BF16),
            V((2, D, BLK), BF16),
            V((2, BLK, D), BF16),
            V((BLK, WIN), F32),
            V((4, 1, WIN), F32),
            V((4, BLK, 2 * BLK), F32),
            V((4, BLK, 2 * BLK), F32),
            V((4, BLK, HD), BF16),
            V((4, HD, BLK), BF16),
            V((4, WIN, HD), BF16),
            V((4, WIN, HD), BF16),
            V((4, BLK, HD), BF16),
            V((4, HD, BLK), BF16),
            V((2, BLK, BLK), BF16),
            V((2, BLK, BLK), BF16),
            V((4, 2 * HD, WIN), BF16),
            V((2, 4, D, 128), BF16),
            V((2, 4, D, 128), BF16),
            V((2, 4, D, 128), F32),
            V((2, 2, 2 * D, 128), BF16),
            V((2, 2, D // 2, 128), BF16),
            V((2, 2, D // 8, 128), F32),
            V((2, 2, 3, D // 2, 128), BF16),
            V((2, 2, 3, D // 8, 128), BF16),
            V((2, 2, 7, 8, 128), F32),
            V((2, D, BLK), BF16),
            V((2, D, BLK), BF16),
            V((2, D, BLK), F32),
            dma((9,)),
            dma((4,)),
            dma((2 * CHUNKS + 2,)),
            dma((2,)),
            dma((2,)),
            dma((1,)),
            dma((2,)),
            dma((2, 3)),
            dma((2, 3)),
            dma((2, 3)),
            dma((2, 3)),
            dma((1,)),
            dma((2, 2)),
            dma((1,)),
            dma((1,)),
            pltpu.SemaphoreType.REGULAR((3,)),
        ],
        compiler_params=pltpu.CompilerParams(
            collective_id=0, has_side_effects=True, vmem_limit_bytes=58 * 1024 * 1024
        ),
        name="history_attention",
    )(table, cotangent, stamps, starts, w_query, w_key, w_value, w_out, decay.reshape(1, 2))
    shapes = ((2, BLK, D), (2, BLK, D), (D, BLK), (D, BLK), (D, BLK), (BLK, D))
    return pl.pallas_call(
        finish,
        out_shape=tuple(
            jax.ShapeDtypeStruct(shape, BF16 if n < 2 else F32) for n, shape in enumerate(shapes)
        ),
        in_specs=[vmem] * 3,
        out_specs=(hbm,) * 6,
        scratch_shapes=[V((3, D, BLK), F32), V((BLK, D), F32), dma((6,))],
        compiler_params=pltpu.CompilerParams(vmem_limit_bytes=16 * 1024 * 1024),
        name="finish",
    )(*near)


def solution(mesh):
    return jax.shard_map(
        shards,
        mesh=mesh,
        in_specs=(
            P(None, "tm", None),
            P(None, "tm", None),
            P(None, "tm"),
            P(None, "tm"),
            P(None, "rep"),
            P(None, "rep"),
            P(None, "rep"),
            P("rep", None),
            P("rep"),
        ),
        out_specs=(
            P(None, "tm", None),
            P(None, "tm", None),
            P(None, "rep"),
            P(None, "rep"),
            P(None, "rep"),
            P("rep", None),
        ),
        check_vma=False,
    )
```

```python
import functools
import math

import jax
import jax.numpy as jnp
from jax import lax
from jax.experimental import pallas as pl
from jax.experimental.pallas import tpu as pltpu
from jax.sharding import PartitionSpec as P

HD = 128
BLK = 256
WIN = 3 * BLK
D = 512
NX, NY, NZ = 4, 4, 8
CHUNKS = 4
LOG2E = 1.4426950408889634
MESH = pl.DeviceIdType.MESH
F32 = jnp.float32
BF16 = jnp.bfloat16
ORDERS = (("x", "y", "z"), ("y", "x", "z"))
SIZES = {"x": NX, "y": NY, "z": NZ}
FARTHEST = {4: (2, 1, 3), 8: (4, 3, 5, 2, 6, 1, 7)}


def nt(a, b):
    return lax.dot_general(a, b, (((1,), (1,)), ((), ())), preferred_element_type=F32)


def nn(a, b):
    return jnp.dot(a, b, preferred_element_type=F32)


def kernel(
    tm_size,
    table,
    cot,
    stamps,
    starts,
    wq_in,
    wk_in,
    wv_in,
    wo_in,
    decay,
    mix,
    gtb,
    red,
    xw,
    xT,
    g_s,
    ts_own,
    st_own,
    dec_in,
    ts_near,
    dec_send,
    dec_recv,
    wq,
    wk,
    wv,
    wo,
    mb,
    brow,
    s_pre,
    dp_pre,
    q_s,
    qT_s,
    k_s,
    v_s,
    do_s,
    doT_s,
    o_s,
    dq_s,
    kvT_s,
    psend,
    precv,
    pown,
    b0,
    b1,
    b2,
    b1_exact,
    b2_exact,
    rc0,
    rc1,
    rc2,
    ct_send,
    ct_recv,
    ct_own,
    lsem,
    hs,
    hr,
    ws,
    wr,
    ps,
    pr,
    rs_s,
    rs_r,
    ag_s,
    ag_r,
    cs,
    cr,
    ms,
    mr,
    met,
):
    tm = lax.axis_index("tm")
    c = lax.axis_index("rep")
    blocks = 2 * tm_size
    blk = c * (blocks - 1 - 2 * tm) + tm
    coord = {"x": tm // (NZ * NY), "z": (tm // NY) % NZ, "y": tm % NY}

    def holder(pos):
        side = pos // tm_size
        return (side * (blocks - 1 - 2 * pos) + pos, side)

    def partner(axis, d):
        at = dict(coord)
        at[axis] = (coord[axis] + SIZES[axis] + d) % SIZES[axis]
        return ((at["x"] * NZ + at["z"]) * NY + at["y"], c)

    next1 = holder((blk + 1) % blocks)
    pos1 = (blk + blocks - 1) % blocks
    pos2 = (blk + blocks - 2) % blocks
    prev1 = holder(pos1)
    sib = (tm, 1 - c)

    barrier = pltpu.get_barrier_semaphore()
    friends = [next1, prev1, sib]
    for axis in SIZES:
        friends += [partner(axis, 1), partner(axis, -1)]
    for friend in friends:
        pl.semaphore_signal(barrier, inc=1, device_id=friend, device_id_type=MESH)

    loads = [
        pltpu.make_async_copy(src, dst, lsem.at[n])
        for n, (src, dst) in enumerate(
            [
                (stamps, ts_own),
                (starts, st_own),
                (decay, dec_in),
                (table.at[c], xw.at[2]),
                (cot.at[c], g_s),
                (wq_in, wq.at[1]),
                (wk_in, wk.at[1]),
                (wv_in, wv.at[1]),
                (wo_in, wo.at[1]),
            ]
        )
    ]
    for copy in loads:
        copy.start()

    def remote(src, dst, send, recv, to):
        return pltpu.make_async_remote_copy(
            src_ref=src, dst_ref=dst, send_sem=send, recv_sem=recv, device_id=to, device_id_type=MESH
        )

    for copy in loads[:4]:
        copy.wait()
    pl.semaphore_wait(barrier, len(friends))

    def tell(token):
        axis, d, n = token
        pl.semaphore_signal(met.at[n], inc=1, device_id=partner(axis, d), device_id_type=MESH)

    tokens = ([("x", 1, 0), ("y", 1, 0), ("z", 1, 0), ("z", -1, 0)], [("z", 1, 1), ("z", -1, 1)], [("z", 1, 2)])

    def hear(n):
        pl.semaphore_wait(met.at[n], len(tokens[n]))

    chunk = BLK // CHUNKS
    pieces = [pl.ds(n * chunk, chunk) for n in range(CHUNKS)]
    mine = [
        remote(xw.at[2, rows], xw.at[1, rows], hs.at[0], hr.at[n], next1)
        for n, rows in enumerate(pieces)
    ]
    onward = [
        remote(xw.at[1, rows], xw.at[0, rows], hs.at[1], hr.at[CHUNKS + n], next1)
        for n, rows in enumerate(pieces)
    ]
    times = [
        remote(src, ts_near.at[n], hs.at[2 + n], hr.at[2 * CHUNKS + n], next1)
        for n, src in enumerate((stamps, ts_near.at[0]))
    ]
    weights = [
        remote(src.at[1], dst.at[0], ws.at[0], wr.at[0], sib)
        for n, (src, dst) in enumerate(((wq, wq), (wk, wk), (wv, wv), (wo, wo)))
    ]
    decays = remote(dec_send, dec_recv, ws.at[1], wr.at[1], sib)
    for copy in times[:1] + mine:
        copy.start()
    for token in tokens[0]:
        tell(token)
    sub = lax.broadcasted_iota(jnp.int32, (8, 128), 0)
    dec_send[...] = jnp.where(sub == 0, dec_in[0, 0], dec_in[0, 1])
    decays.start()
    first_row = jnp.where(c == 0, st_own[0:1, :], st_own[1:2, :]) - (blk - 2) * BLK
    first_col = jnp.transpose(jnp.broadcast_to(first_row.astype(F32), (128, BLK)))
    row_id = lax.broadcasted_iota(jnp.int32, (BLK, 128), 0)
    col_id = lax.broadcasted_iota(jnp.int32, (BLK, 128), 1)
    for n in range(WIN // 128):
        key_id = col_id + n * 128
        ok = (key_id.astype(F32) >= first_col) & (key_id <= row_id + 2 * BLK)
        mb[:, n * 128 : (n + 1) * 128] = jnp.where(ok, 0.0, -1e30)


    def begin(copies):
        for copy in copies:
            copy.start()

    def put_heads(dst, slot, rows, val):
        val = val.astype(BF16)
        for j in range(2):
            dst[2 * slot + j, rows, :] = val[:, j * HD : (j + 1) * HD]
        return val

    every = pl.ds(0, BLK)

    def own_rows(slot):
        x = xw[2]
        val = put_heads(q_s, slot, every, nn(x, wq[slot]))
        for j in range(2):
            qT_s[2 * slot + j] = jnp.transpose(val[:, j * HD : (j + 1) * HD])
        val = put_heads(do_s, slot, every, nt(g_s[...], wo[slot]))
        for j in range(2):
            doT_s[2 * slot + j] = jnp.transpose(val[:, j * HD : (j + 1) * HD])

    def keys_of(part, slot):
        rows = pl.ds(part * BLK, BLK)
        put_heads(k_s, slot, rows, nn(xw[part], wk[slot]))
        put_heads(v_s, slot, rows, nn(xw[part], wv[slot]))

    for copy in loads[4:]:
        copy.wait()
    begin(weights)
    own_rows(1)
    keys_of(2, 1)
    xT[:, 2 * BLK :] = jnp.transpose(xw[2])

    def side_row(ref, pos):
        return jnp.where(pos // tm_size == 0, ref[0:1, :], ref[1:2, :])

    own_times = side_row(ts_own, blk)
    base = jnp.max(own_times, axis=1, keepdims=True)
    inv_scale = 1.0 / math.sqrt(HD)

    def columns(part):
        return slice(part * BLK, (part + 1) * BLK)

    def decay_terms(part, times_row):
        rel = (times_row - base).astype(F32) * LOG2E
        for h in range(4):
            rate = (dec_recv, dec_send)[h // 2][h % 2 : h % 2 + 1, 0:1]
            brow[h, :, columns(part)] = rel * rate

    def scores(h, part):
        raw = nt(q_s[h], k_s[h, columns(part), :]) * (inv_scale * LOG2E)
        return raw + (mb[:, columns(part)] + brow[h, :, columns(part)])

    def early(h, part):
        s_pre[h, :, columns(part - 1)] = scores(h, part)
        dp_pre[h, :, columns(part - 1)] = nt(do_s[h], v_s[h, columns(part), :])

    all_weights = remote(psend, psend, ws.at[0], wr.at[0], sib)
    all_weights.wait_recv()
    decays.wait_recv()
    own_rows(0)
    keys_of(2, 0)
    decay_terms(2, own_times)
    times[0].wait_recv()
    times[1].start()
    hear(0)
    for token in tokens[1]:
        tell(token)
    for n in range(CHUNKS):
        mine[n].wait_recv()
        onward[n].start()
        early(n, 2)
    hear(1)
    for token in tokens[2]:
        tell(token)
    keys_of(1, 1)
    keys_of(1, 0)
    xT[:, BLK : 2 * BLK] = jnp.transpose(xw[1])
    decay_terms(1, side_row(ts_near.at[0], pos1))
    for h in range(4):
        early(h, 1)
    hear(2)
    times[1].wait_recv()
    decay_terms(0, side_row(ts_near.at[1], pos2))
    for copy in onward:
        copy.wait_recv()
    keys_of(0, 0)
    keys_of(0, 1)
    xT[:, :BLK] = jnp.transpose(xw[0])

    psends = [
        remote(psend.at[j], precv.at[j], ps.at[0], pr.at[j], sib) for j in range(2)
    ]

    def products(t):
        return scores(t, 0), nt(do_s[t], v_s[t, :BLK, :])

    def softmax(t, s, dp):
        s = jnp.concatenate([s, s_pre[t]], axis=1)
        dp = jnp.concatenate([dp, dp_pre[t]], axis=1)
        p = jnp.exp2(s - jnp.max(s, axis=-1, keepdims=True))
        p = p * (1.0 / jnp.sum(p, axis=-1, keepdims=True))
        delta = jnp.sum(p * dp, axis=-1, keepdims=True)
        return p.astype(BF16), (p * (dp - delta)).astype(BF16)

    def attention(t, pb, ds):
        lanes = slice((t % 2) * HD, (t % 2 + 1) * HD)
        o_s[t // 2, :, lanes] = nn(pb, v_s[t]).astype(BF16)
        dq_s[t // 2, :, lanes] = (nn(ds, k_s[t]) * inv_scale).astype(BF16)
        kvT_s[t, :HD, :] = (nn(qT_s[t], ds) * inv_scale).astype(BF16)
        kvT_s[t, HD:, :] = nn(doT_s[t], pb).astype(BF16)

    def weight_grads(t):
        lanes = slice((t % 2) * HD, (t % 2 + 1) * HD)
        kv = nt(xT[...], kvT_s[t])
        go = nn(jnp.transpose(o_s[t // 2, :, lanes]), g_s[...])
        to = psend.at[t] if t < 2 else pown.at[t - 2]
        to[0] = nn(xT[:, 2 * BLK :], dq_s[t // 2, :, lanes]).astype(to.dtype)
        to[1] = kv[:, :HD].astype(to.dtype)
        to[2] = kv[:, HD:].astype(to.dtype)
        for n in range(4):
            to[3, n * HD : (n + 1) * HD, :] = go[:, n * HD : (n + 1) * HD].astype(to.dtype)

    def reduce_pair(j):
        psends[j].wait_recv()
        for n in range(4):
            b0[j, n // 2, (n % 2) * D : (n % 2 + 1) * D, :] = (pown[j, n] + precv[j, n].astype(F32)).astype(BF16)
        begin(scatters[j][0])

    def pass_on(step):
        if step in (0, 2):
            psends[step // 2].start()
        if step == 3:
            reduce_pair(1)
        if step in (1, 2):
            pl.when(c == step - 1)(lambda: reduce_pair(0))

    sources = (b0, b1, b2)
    landing = (rc0, rc1, rc2)
    exact = (b1_exact, b2_exact)
    rows_at = (2 * D, D // 2, D // 8)

    def place(stage, col):
        axis = ORDERS[col][stage]
        return axis, SIZES[axis], rows_at[stage] // SIZES[axis]

    def scatter(j, stage):
        copies = []
        for col in range(2):
            axis, size, piece = place(stage, col)
            for d in FARTHEST[size]:
                there = (coord[axis] + d) % size
                rows = there if stage == 2 else pl.ds(pl.multiple_of(there * piece, piece), piece)
                copies.append(
                    remote(
                        sources[stage].at[j, col, rows],
                        landing[stage].at[j, col, d - 1],
                        rs_s.at[j, stage],
                        rs_r.at[j, stage],
                        partner(axis, d),
                    )
                )
        return copies

    def gathered(j, stage, col):
        axis, size, piece = place(stage, col)
        if stage == 0:
            here = (2 * col + coord[axis] // 2, pl.ds(pl.multiple_of(coord[axis] % 2 * piece, piece), piece))
            total = pown[j, here[0], here[1], :] + precv[j, here[0], here[1], :].astype(F32)
        else:
            total = exact[stage - 1][j, col, pl.ds(pl.multiple_of(coord[axis] * piece, piece), piece), :]
        for d in range(1, size):
            total = total + landing[stage][j, col, d - 1].astype(F32)
        return total

    def first_owner(stage, col):
        owner = 0
        for s in range(stage + 1):
            axis, _, piece = place(s, col)
            owner = owner + coord[axis] * (piece // 8)
        return owner

    def spread(j, stage):
        copies = []
        for col in range(2):
            axis, size, piece = place(stage, col)
            here = pl.ds(first_owner(stage, col), piece // 8)
            for d in FARTHEST[size]:
                copies.append(
                    remote(
                        red.at[col, j, here],
                        red.at[col, j, here],
                        ag_s.at[j, stage],
                        ag_r.at[j, stage],
                        partner(axis, d),
                    )
                )
        return copies

    def spread_last(j):
        own, others = [], []
        for col in range(2):
            axis, size, _ = place(0, col)
            second, count, piece = place(1, col)
            base = coord[axis] * count
            for e in range(count):
                here = pl.ds((base + (coord[second] + e) % count) * (piece // 8), piece // 8)
                for d in FARTHEST[size]:
                    (others if e else own).append(
                        remote(
                            red.at[col, j, here],
                            red.at[col, j, here],
                            ag_s.at[j, 0],
                            ag_r.at[j, 0],
                            partner(axis, d),
                        )
                    )
        return own, others

    def whole_scatter(j, stage):
        ref = landing[stage].at[j]
        return remote(ref, ref, rs_s.at[j, stage], rs_r.at[j, stage], sib)

    def whole_spread(j, stage):
        _, size, piece = place(stage, 0)
        ref = red.at[:, j, pl.ds(0, (size - 1) * (piece // 8))]
        return remote(ref, ref, ag_s.at[j, stage], ag_r.at[j, stage], sib)

    scatters = [[scatter(j, stage) for stage in range(3)] for j in range(2)]
    spreads = [[None, spread(j, 1), spread(j, 2)] for j in range(2)]
    lasts = [spread_last(j) for j in range(2)]

    def arrived(copies):
        for copy in copies:
            copy.wait_recv()

    def next_scatter(j, stage):
        whole_scatter(j, stage).wait_recv()
        for col in range(2):
            if stage < 2:
                total = gathered(j, stage, col)
                exact[stage][j, col] = total
                if stage == 1:
                    total = total.reshape(NZ, 8, 128)
                sources[stage + 1][j, col] = total.astype(BF16)
            else:
                red[col, j, first_owner(2, col)] = (gathered(j, 2, col) * scale).astype(BF16)
        begin(scatters[j][stage + 1] if stage < 2 else spreads[j][2])

    def next_spread(j, stage):
        whole_spread(j, stage).wait_recv()
        if stage == 2:
            begin(spreads[j][1])
        begin(lasts[j][2 - stage])

    scale = 1.0 / math.sqrt(blocks * BLK)
    turn = (0, 2, 1, 3)
    now = products(turn[0])
    for step in range(4):
        later = products(turn[step + 1]) if step < 3 else None
        if step > 0:
            weight_grads(turn[step - 1])
        pb, ds = softmax(turn[step], *now)
        if step > 0:
            pass_on(step - 1)
        attention(turn[step], pb, ds)
        now = later
    weight_grads(turn[3])
    pass_on(3)

    mix[c] = (nn(o_s[0], wo[0]) + nn(o_s[1], wo[1])).astype(BF16)
    to_sib = [
        remote(ref.at[c], ref.at[c], ms.at[0], mr.at[0], sib) for n, ref in enumerate((mix, gtb))
    ]
    to_sib[0].start()
    for part in range(3):
        cols = slice(part * BLK, (part + 1) * BLK)
        total = jnp.zeros((D, BLK), F32)
        for t in range(4):
            lanes = slice((t % 2) * HD, (t % 2 + 1) * HD)
            both = jnp.concatenate([wk[t // 2, :, lanes], wv[t // 2, :, lanes]], axis=1)
            total = total + nn(both, kvT_s[t, :, cols])
        if part == 0:
            ct_send[0] = total.astype(BF16)
        else:
            ct_own[part - 1] = total
    terms = [
        [
            remote(ct_send.at[n, rows], ct_recv.at[n, rows], cs.at[0], cr.at[n, h], prev1)
            for h, rows in enumerate((every, pl.ds(BLK, BLK)))
        ]
        for n in range(2)
    ]

    next_scatter(0, 0)
    next_scatter(1, 0)
    gtq = nt(dq_s[0], wq[0]) + nt(dq_s[1], wq[1])
    next_scatter(0, 1)
    begin(terms[0])
    next_scatter(1, 1)
    next_scatter(0, 2)
    for h in range(2):
        terms[0][h].wait_recv()
        rows = slice(h * BLK, (h + 1) * BLK)
        ct_send[1, rows, :] = (ct_own[0, rows, :] + ct_recv[0, rows, :].astype(F32)).astype(BF16)
        terms[1][h].start()
    next_scatter(1, 2)
    next_spread(0, 2)
    next_spread(1, 2)
    next_spread(0, 1)
    arrived(terms[1])
    gtb[c] = (gtq + jnp.transpose(ct_own[1] + ct_recv[1].astype(F32))).astype(BF16)
    to_sib[1].start()
    next_spread(1, 1)
    both = remote(mix, mix, ms.at[0], mr.at[0], sib)
    both.wait_recv()
    whole_spread(0, 0).wait_recv()
    whole_spread(1, 0).wait_recv()
    sent = [remote(xw.at[0], xw.at[0], hs.at[n], hr.at[n], next1) for n in range(2)]
    sent += times + [decays, all_weights, both]
    sent += [remote(psend, psend, ps.at[0], pr.at[0], sib)]
    sent += [remote(ct_send, ct_send, cs.at[0], cr.at[0, 0], prev1)]
    for j in range(2):
        for stage in range(3):
            sent += [whole_scatter(j, stage), whole_spread(j, stage)]
    for copy in sent:
        copy.wait_send()


def finish(mix, gtb, red, mixed, gt, grad_q, grad_k, grad_v, grad_o, wide, rows, sem):
    copies = [
        pltpu.make_async_copy(mix, mixed, sem.at[0]),
        pltpu.make_async_copy(gtb, gt, sem.at[1]),
    ]
    copies[0].start()
    copies[1].start()
    for n, out in enumerate((grad_q, grad_k, grad_v, grad_o)):
        half = pl.ds((n % 2) * (D // 8), D // 8)
        for j in range(2):
            val = red[n // 2, j, half].astype(F32).reshape(D, HD)
            if n < 3:
                wide[n, :, j * HD : (j + 1) * HD] = val
            else:
                for k in range(4):
                    rows[j * HD : (j + 1) * HD, k * HD : (k + 1) * HD] = val[k * HD : (k + 1) * HD]
        copies.append(pltpu.make_async_copy(wide.at[n] if n < 3 else rows, out, sem.at[2 + n]))
        copies[-1].start()
    for copy in copies:
        copy.wait()


def shards(table, cotangent, stamps, starts, w_query, w_key, w_value, w_out, decay):
    tm_size = lax.axis_size("tm")
    hbm = pl.BlockSpec(memory_space=pltpu.HBM)
    vmem = pl.BlockSpec(memory_space=pltpu.VMEM)
    dma = pltpu.SemaphoreType.DMA
    V = pltpu.VMEM
    near = (
        V((2, BLK, D), BF16),
        V((2, BLK, D), BF16),
        V((2, 2, 128, 8, 128), BF16),
    )
    near = pl.pallas_call(
        functools.partial(kernel, tm_size),
        out_shape=near,
        in_specs=[hbm] * 9,
        out_specs=(vmem, vmem, vmem),
        scratch_shapes=[
            V((3, BLK, D), BF16),
            V((D, WIN), BF16),
            V((BLK, D), BF16),
            V((2, BLK), jnp.int32),
            V((2, BLK), jnp.int32),
            pltpu.SMEM((1, 2), F32),
            V((2, 2, BLK), jnp.int32),
            V((8, 128), F32),
            V((8, 128), F32),
            V((2, D, BLK), BF16),
            V((2, D, BLK), BF16),
            V((2, D, BLK), BF16),
            V((2, BLK, D), BF16),
            V((BLK, WIN), F32),
            V((4, 1, WIN), F32),
            V((4, BLK, 2 * BLK), F32),
            V((4, BLK, 2 * BLK), F32),
            V((4, BLK, HD), BF16),
            V((4, HD, BLK), BF16),
            V((4, WIN, HD), BF16),
            V((4, WIN, HD), BF16),
            V((4, BLK, HD), BF16),
            V((4, HD, BLK), BF16),
            V((2, BLK, BLK), BF16),
            V((2, BLK, BLK), BF16),
            V((4, 2 * HD, WIN), BF16),
            V((2, 4, D, 128), BF16),
            V((2, 4, D, 128), BF16),
            V((2, 4, D, 128), F32),
            V((2, 2, 2 * D, 128), BF16),
            V((2, 2, D // 2, 128), BF16),
            V((2, 2, NZ, 8, 128), BF16),
            V((2, 2, D // 2, 128), F32),
            V((2, 2, D // 8, 128), F32),
            V((2, 2, 3, D // 2, 128), BF16),
            V((2, 2, 3, D // 8, 128), BF16),
            V((2, 2, 7, 8, 128), BF16),
            V((2, D, BLK), BF16),
            V((2, D, BLK), BF16),
            V((2, D, BLK), F32),
            dma((9,)),
            dma((4,)),
            dma((2 * CHUNKS + 2,)),
            dma((2,)),
            dma((2,)),
            dma((1,)),
            dma((2,)),
            dma((2, 3)),
            dma((2, 3)),
            dma((2, 3)),
            dma((2, 3)),
            dma((1,)),
            dma((2, 2)),
            dma((1,)),
            dma((1,)),
            pltpu.SemaphoreType.REGULAR((3,)),
        ],
        compiler_params=pltpu.CompilerParams(
            collective_id=0, has_side_effects=True, vmem_limit_bytes=58 * 1024 * 1024
        ),
        name="history_attention",
    )(table, cotangent, stamps, starts, w_query, w_key, w_value, w_out, decay.reshape(1, 2))
    shapes = ((2, BLK, D), (2, BLK, D), (D, BLK), (D, BLK), (D, BLK), (BLK, D))
    return pl.pallas_call(
        finish,
        out_shape=tuple(
            jax.ShapeDtypeStruct(shape, BF16 if n < 2 else F32) for n, shape in enumerate(shapes)
        ),
        in_specs=[vmem] * 3,
        out_specs=(hbm,) * 6,
        scratch_shapes=[V((3, D, BLK), F32), V((BLK, D), F32), dma((6,))],
        compiler_params=pltpu.CompilerParams(vmem_limit_bytes=16 * 1024 * 1024),
        name="finish",
    )(*near)


def solution(mesh):
    return jax.shard_map(
        shards,
        mesh=mesh,
        in_specs=(
            P(None, "tm", None),
            P(None, "tm", None),
            P(None, "tm"),
            P(None, "tm"),
            P(None, "rep"),
            P(None, "rep"),
            P(None, "rep"),
            P("rep", None),
            P("rep"),
        ),
        out_specs=(
            P(None, "tm", None),
            P(None, "tm", None),
            P(None, "rep"),
            P(None, "rep"),
            P(None, "rep"),
            P("rep", None),
        ),
        check_vma=False,
    )
```

```python
import functools
import math

import jax
import jax.numpy as jnp
from jax import lax
from jax.experimental import pallas as pl
from jax.experimental.pallas import tpu as pltpu
from jax.sharding import PartitionSpec as P

HD = 128
BLK = 256
WIN = 3 * BLK
D = 512
NX, NY, NZ = 4, 4, 8
CHUNKS = 8
LOG2E = 1.4426950408889634
MESH = pl.DeviceIdType.MESH
F32 = jnp.float32
BF16 = jnp.bfloat16
ORDERS = (("x", "y", "z"), ("y", "x", "z"))
SIZES = {"x": NX, "y": NY, "z": NZ}
FARTHEST = {4: (2, 1, 3), 8: (4, 3, 5, 2, 6, 1, 7)}


def nt(a, b):
    return lax.dot_general(a, b, (((1,), (1,)), ((), ())), preferred_element_type=F32)


def nn(a, b):
    return jnp.dot(a, b, preferred_element_type=F32)


def kernel(
    tm_size,
    table,
    cot,
    stamps,
    starts,
    wq_in,
    wk_in,
    wv_in,
    wo_in,
    decay,
    mix,
    gtb,
    red,
    xw,
    xT,
    g_s,
    ts_own,
    st_own,
    dec_in,
    ts_near,
    dec_send,
    dec_recv,
    wq,
    wk,
    wv,
    wo,
    mb,
    brow,
    s_pre,
    dp_pre,
    q_s,
    qT_s,
    k_s,
    v_s,
    do_s,
    doT_s,
    o_s,
    dq_s,
    kvT_s,
    psend,
    precv,
    pown,
    b0,
    b1,
    b2,
    b1_exact,
    b2_exact,
    rc0,
    rc1,
    rc2,
    ct_send,
    ct_recv,
    ct_own,
    lsem,
    hs,
    hr,
    ws,
    wr,
    ps,
    pr,
    rs_s,
    rs_r,
    ag_s,
    ag_r,
    cs,
    cr,
    ms,
    mr,
    met,
):
    tm = lax.axis_index("tm")
    c = lax.axis_index("rep")
    blocks = 2 * tm_size
    blk = c * (blocks - 1 - 2 * tm) + tm
    coord = {"x": tm // (NZ * NY), "z": (tm // NY) % NZ, "y": tm % NY}

    def holder(pos):
        side = pos // tm_size
        return (side * (blocks - 1 - 2 * pos) + pos, side)

    def partner(axis, d):
        at = dict(coord)
        at[axis] = (coord[axis] + SIZES[axis] + d) % SIZES[axis]
        return ((at["x"] * NZ + at["z"]) * NY + at["y"], c)

    next1 = holder((blk + 1) % blocks)
    pos1 = (blk + blocks - 1) % blocks
    pos2 = (blk + blocks - 2) % blocks
    prev1 = holder(pos1)
    sib = (tm, 1 - c)

    barrier = pltpu.get_barrier_semaphore()
    friends = [next1, prev1, sib]
    for axis in SIZES:
        friends += [partner(axis, 1), partner(axis, -1)]
    for friend in friends:
        pl.semaphore_signal(barrier, inc=1, device_id=friend, device_id_type=MESH)

    loads = [
        pltpu.make_async_copy(src, dst, lsem.at[n])
        for n, (src, dst) in enumerate(
            [
                (stamps, ts_own),
                (starts, st_own),
                (decay, dec_in),
                (table.at[c], xw.at[2]),
                (cot.at[c], g_s),
                (wq_in, wq.at[1]),
                (wk_in, wk.at[1]),
                (wv_in, wv.at[1]),
                (wo_in, wo.at[1]),
            ]
        )
    ]
    for copy in loads:
        copy.start()

    def remote(src, dst, send, recv, to):
        return pltpu.make_async_remote_copy(
            src_ref=src, dst_ref=dst, send_sem=send, recv_sem=recv, device_id=to, device_id_type=MESH
        )

    for copy in loads[:4]:
        copy.wait()
    pl.semaphore_wait(barrier, len(friends))

    def tell(token):
        axis, d, n = token
        pl.semaphore_signal(met.at[n], inc=1, device_id=partner(axis, d), device_id_type=MESH)

    tokens = ([("x", 1, 0), ("y", 1, 0), ("z", 1, 0), ("z", -1, 0)], [("z", 1, 1), ("z", -1, 1)], [("z", 1, 2)])

    def hear(n):
        pl.semaphore_wait(met.at[n], len(tokens[n]))

    chunk = BLK // CHUNKS
    pieces = [pl.ds(n * chunk, chunk) for n in range(CHUNKS)]
    mine = [
        remote(xw.at[2, rows], xw.at[1, rows], hs.at[0], hr.at[n], next1)
        for n, rows in enumerate(pieces)
    ]
    onward = [
        remote(xw.at[1, rows], xw.at[0, rows], hs.at[1], hr.at[CHUNKS + n], next1)
        for n, rows in enumerate(pieces)
    ]
    times = [
        remote(src, ts_near.at[n], hs.at[2 + n], hr.at[2 * CHUNKS + n], next1)
        for n, src in enumerate((stamps, ts_near.at[0]))
    ]
    weights = [
        remote(src.at[1], dst.at[0], ws.at[0], wr.at[0], sib)
        for n, (src, dst) in enumerate(((wq, wq), (wk, wk), (wv, wv), (wo, wo)))
    ]
    decays = remote(dec_send, dec_recv, ws.at[1], wr.at[1], sib)
    for copy in times[:1] + mine:
        copy.start()
    for token in tokens[0]:
        tell(token)
    sub = lax.broadcasted_iota(jnp.int32, (8, 128), 0)
    dec_send[...] = jnp.where(sub == 0, dec_in[0, 0], dec_in[0, 1])
    decays.start()
    first_row = jnp.where(c == 0, st_own[0:1, :], st_own[1:2, :]) - (blk - 2) * BLK
    first_col = jnp.transpose(jnp.broadcast_to(first_row.astype(F32), (128, BLK)))
    row_id = lax.broadcasted_iota(jnp.int32, (BLK, 128), 0)
    col_id = lax.broadcasted_iota(jnp.int32, (BLK, 128), 1)
    for n in range(WIN // 128):
        key_id = col_id + n * 128
        ok = (key_id.astype(F32) >= first_col) & (key_id <= row_id + 2 * BLK)
        mb[:, n * 128 : (n + 1) * 128] = jnp.where(ok, 0.0, -1e30)


    def begin(copies):
        for copy in copies:
            copy.start()

    def put_heads(dst, slot, rows, val):
        val = val.astype(BF16)
        for j in range(2):
            dst[2 * slot + j, rows, :] = val[:, j * HD : (j + 1) * HD]
        return val

    every = pl.ds(0, BLK)

    def own_rows(slot):
        x = xw[2]
        val = put_heads(q_s, slot, every, nn(x, wq[slot]))
        for j in range(2):
            qT_s[2 * slot + j] = jnp.transpose(val[:, j * HD : (j + 1) * HD])
        val = put_heads(do_s, slot, every, nt(g_s[...], wo[slot]))
        for j in range(2):
            doT_s[2 * slot + j] = jnp.transpose(val[:, j * HD : (j + 1) * HD])

    def keys_of(part, slot):
        rows = pl.ds(part * BLK, BLK)
        put_heads(k_s, slot, rows, nn(xw[part], wk[slot]))
        put_heads(v_s, slot, rows, nn(xw[part], wv[slot]))

    for copy in loads[4:]:
        copy.wait()
    begin(weights)
    own_rows(1)
    keys_of(2, 1)
    xT[:, 2 * BLK :] = jnp.transpose(xw[2])

    def side_row(ref, pos):
        return jnp.where(pos // tm_size == 0, ref[0:1, :], ref[1:2, :])

    own_times = side_row(ts_own, blk)
    base = jnp.max(own_times, axis=1, keepdims=True)
    inv_scale = 1.0 / math.sqrt(HD)

    def columns(part):
        return slice(part * BLK, (part + 1) * BLK)

    def decay_terms(part, times_row):
        rel = (times_row - base).astype(F32) * LOG2E
        for h in range(4):
            rate = (dec_recv, dec_send)[h // 2][h % 2 : h % 2 + 1, 0:1]
            brow[h, :, columns(part)] = rel * rate

    def scores(h, part):
        raw = nt(q_s[h], k_s[h, columns(part), :]) * (inv_scale * LOG2E)
        return raw + (mb[:, columns(part)] + brow[h, :, columns(part)])

    def early(h, part):
        s_pre[h, :, columns(part - 1)] = scores(h, part)
        dp_pre[h, :, columns(part - 1)] = nt(do_s[h], v_s[h, columns(part), :])

    all_weights = remote(psend, psend, ws.at[0], wr.at[0], sib)
    all_weights.wait_recv()
    decays.wait_recv()
    own_rows(0)
    keys_of(2, 0)
    decay_terms(2, own_times)
    times[0].wait_recv()
    times[1].start()
    hear(0)
    for token in tokens[1]:
        tell(token)
    for n in range(CHUNKS):
        mine[n].wait_recv()
        onward[n].start()
        if n % 2:
            early(n // 2, 2)
    hear(1)
    for token in tokens[2]:
        tell(token)
    keys_of(1, 1)
    keys_of(1, 0)
    xT[:, BLK : 2 * BLK] = jnp.transpose(xw[1])
    decay_terms(1, side_row(ts_near.at[0], pos1))
    for h in range(4):
        early(h, 1)
    hear(2)
    times[1].wait_recv()
    decay_terms(0, side_row(ts_near.at[1], pos2))
    for copy in onward:
        copy.wait_recv()
    keys_of(0, 0)
    keys_of(0, 1)
    xT[:, :BLK] = jnp.transpose(xw[0])

    psends = [
        remote(psend.at[j], precv.at[j], ps.at[0], pr.at[j], sib) for j in range(2)
    ]

    def products(t):
        return scores(t, 0), nt(do_s[t], v_s[t, :BLK, :])

    def softmax(t, s, dp):
        s = jnp.concatenate([s, s_pre[t]], axis=1)
        dp = jnp.concatenate([dp, dp_pre[t]], axis=1)
        p = jnp.exp2(s - jnp.max(s, axis=-1, keepdims=True))
        p = p * (1.0 / jnp.sum(p, axis=-1, keepdims=True))
        delta = jnp.sum(p * dp, axis=-1, keepdims=True)
        return p.astype(BF16), (p * (dp - delta)).astype(BF16)

    def attention(t, pb, ds):
        lanes = slice((t % 2) * HD, (t % 2 + 1) * HD)
        o_s[t // 2, :, lanes] = nn(pb, v_s[t]).astype(BF16)
        dq_s[t // 2, :, lanes] = (nn(ds, k_s[t]) * inv_scale).astype(BF16)
        kvT_s[t, :HD, :] = (nn(qT_s[t], ds) * inv_scale).astype(BF16)
        kvT_s[t, HD:, :] = nn(doT_s[t], pb).astype(BF16)

    def weight_grads(t):
        lanes = slice((t % 2) * HD, (t % 2 + 1) * HD)
        kv = nt(xT[...], kvT_s[t])
        go = nn(jnp.transpose(o_s[t // 2, :, lanes]), g_s[...])
        to = psend.at[t] if t < 2 else pown.at[t - 2]
        to[0] = nn(xT[:, 2 * BLK :], dq_s[t // 2, :, lanes]).astype(to.dtype)
        to[1] = kv[:, :HD].astype(to.dtype)
        to[2] = kv[:, HD:].astype(to.dtype)
        for n in range(4):
            to[3, n * HD : (n + 1) * HD, :] = go[:, n * HD : (n + 1) * HD].astype(to.dtype)

    def reduce_pair(j):
        psends[j].wait_recv()
        for n in range(4):
            b0[j, n // 2, (n % 2) * D : (n % 2 + 1) * D, :] = (pown[j, n] + precv[j, n].astype(F32)).astype(BF16)
        begin(scatters[j][0])

    def pass_on(step):
        if step in (0, 2):
            psends[step // 2].start()
        if step == 3:
            reduce_pair(1)
        if step in (1, 2):
            pl.when(c == step - 1)(lambda: reduce_pair(0))

    sources = (b0, b1, b2)
    landing = (rc0, rc1, rc2)
    exact = (b1_exact, b2_exact)
    rows_at = (2 * D, D // 2, D // 8)

    def place(stage, col):
        axis = ORDERS[col][stage]
        return axis, SIZES[axis], rows_at[stage] // SIZES[axis]

    def scatter(j, stage):
        copies = []
        for col in range(2):
            axis, size, piece = place(stage, col)
            for d in FARTHEST[size]:
                there = (coord[axis] + d) % size
                rows = there if stage == 2 else pl.ds(pl.multiple_of(there * piece, piece), piece)
                copies.append(
                    remote(
                        sources[stage].at[j, col, rows],
                        landing[stage].at[j, col, d - 1],
                        rs_s.at[j, stage],
                        rs_r.at[j, stage],
                        partner(axis, d),
                    )
                )
        return copies

    def gathered(j, stage, col):
        axis, size, piece = place(stage, col)
        if stage == 0:
            here = (2 * col + coord[axis] // 2, pl.ds(pl.multiple_of(coord[axis] % 2 * piece, piece), piece))
            total = pown[j, here[0], here[1], :] + precv[j, here[0], here[1], :].astype(F32)
        else:
            total = exact[stage - 1][j, col, pl.ds(pl.multiple_of(coord[axis] * piece, piece), piece), :]
        for d in range(1, size):
            total = total + landing[stage][j, col, d - 1].astype(F32)
        return total

    def first_owner(stage, col):
        owner = 0
        for s in range(stage + 1):
            axis, _, piece = place(s, col)
            owner = owner + coord[axis] * (piece // 8)
        return owner

    def spread(j, stage):
        copies = []
        for col in range(2):
            axis, size, piece = place(stage, col)
            here = pl.ds(first_owner(stage, col), piece // 8)
            for d in FARTHEST[size]:
                copies.append(
                    remote(
                        red.at[col, j, here],
                        red.at[col, j, here],
                        ag_s.at[j, stage],
                        ag_r.at[j, stage],
                        partner(axis, d),
                    )
                )
        return copies

    def spread_last(j):
        own, others = [], []
        for col in range(2):
            axis, size, _ = place(0, col)
            second, count, piece = place(1, col)
            base = coord[axis] * count
            for e in range(count):
                here = pl.ds((base + (coord[second] + e) % count) * (piece // 8), piece // 8)
                for d in FARTHEST[size]:
                    (others if e else own).append(
                        remote(
                            red.at[col, j, here],
                            red.at[col, j, here],
                            ag_s.at[j, 0],
                            ag_r.at[j, 0],
                            partner(axis, d),
                        )
                    )
        return own, others

    def whole_scatter(j, stage):
        ref = landing[stage].at[j]
        return remote(ref, ref, rs_s.at[j, stage], rs_r.at[j, stage], sib)

    def whole_spread(j, stage):
        _, size, piece = place(stage, 0)
        ref = red.at[:, j, pl.ds(0, (size - 1) * (piece // 8))]
        return remote(ref, ref, ag_s.at[j, stage], ag_r.at[j, stage], sib)

    scatters = [[scatter(j, stage) for stage in range(3)] for j in range(2)]
    spreads = [[None, spread(j, 1), spread(j, 2)] for j in range(2)]
    lasts = [spread_last(j) for j in range(2)]

    def arrived(copies):
        for copy in copies:
            copy.wait_recv()

    def next_scatter(j, stage):
        whole_scatter(j, stage).wait_recv()
        for col in range(2):
            if stage < 2:
                total = gathered(j, stage, col)
                exact[stage][j, col] = total
                if stage == 1:
                    total = total.reshape(NZ, 8, 128)
                sources[stage + 1][j, col] = total.astype(BF16)
            else:
                red[col, j, first_owner(2, col)] = (gathered(j, 2, col) * scale).astype(BF16)
        begin(scatters[j][stage + 1] if stage < 2 else spreads[j][2])

    def next_spread(j, stage):
        whole_spread(j, stage).wait_recv()
        if stage == 2:
            begin(spreads[j][1])
        begin(lasts[j][2 - stage])

    scale = 1.0 / math.sqrt(blocks * BLK)
    turn = (0, 2, 1, 3)
    now = products(turn[0])
    for step in range(4):
        later = products(turn[step + 1]) if step < 3 else None
        if step > 0:
            weight_grads(turn[step - 1])
        pb, ds = softmax(turn[step], *now)
        if step > 0:
            pass_on(step - 1)
        attention(turn[step], pb, ds)
        now = later
    weight_grads(turn[3])
    pass_on(3)

    mix[c] = (nn(o_s[0], wo[0]) + nn(o_s[1], wo[1])).astype(BF16)
    to_sib = [
        remote(ref.at[c], ref.at[c], ms.at[0], mr.at[0], sib) for n, ref in enumerate((mix, gtb))
    ]
    to_sib[0].start()
    for part in range(3):
        cols = slice(part * BLK, (part + 1) * BLK)
        total = jnp.zeros((D, BLK), F32)
        for t in range(4):
            lanes = slice((t % 2) * HD, (t % 2 + 1) * HD)
            both = jnp.concatenate([wk[t // 2, :, lanes], wv[t // 2, :, lanes]], axis=1)
            total = total + nn(both, kvT_s[t, :, cols])
        if part == 0:
            ct_send[0] = total.astype(BF16)
        else:
            ct_own[part - 1] = total
    terms = [
        [
            remote(ct_send.at[n, rows], ct_recv.at[n, rows], cs.at[0], cr.at[n, h], prev1)
            for h, rows in enumerate((every, pl.ds(BLK, BLK)))
        ]
        for n in range(2)
    ]

    next_scatter(0, 0)
    next_scatter(1, 0)
    gtq = nt(dq_s[0], wq[0]) + nt(dq_s[1], wq[1])
    next_scatter(0, 1)
    begin(terms[0])
    next_scatter(1, 1)
    next_scatter(0, 2)
    late = coord["y"] == (1 - c) * (NY - 1)

    def relay_terms():
        for h in range(2):
            terms[0][h].wait_recv()
            rows = slice(h * BLK, (h + 1) * BLK)
            ct_send[1, rows, :] = (ct_own[0, rows, :] + ct_recv[0, rows, :].astype(F32)).astype(BF16)
            terms[1][h].start()

    pl.when(jnp.logical_not(late))(relay_terms)
    next_scatter(1, 2)
    pl.when(late)(relay_terms)
    next_spread(0, 2)
    next_spread(1, 2)
    next_spread(0, 1)
    arrived(terms[1])
    gtb[c] = (gtq + jnp.transpose(ct_own[1] + ct_recv[1].astype(F32))).astype(BF16)
    to_sib[1].start()
    next_spread(1, 1)
    both = remote(mix, mix, ms.at[0], mr.at[0], sib)
    both.wait_recv()
    whole_spread(0, 0).wait_recv()
    whole_spread(1, 0).wait_recv()
    sent = [remote(xw.at[0], xw.at[0], hs.at[n], hr.at[n], next1) for n in range(2)]
    sent += times + [decays, all_weights, both]
    sent += [remote(psend, psend, ps.at[0], pr.at[0], sib)]
    sent += [remote(ct_send, ct_send, cs.at[0], cr.at[0, 0], prev1)]
    for j in range(2):
        for stage in range(3):
            sent += [whole_scatter(j, stage), whole_spread(j, stage)]
    for copy in sent:
        copy.wait_send()


def finish(mix, gtb, red, mixed, gt, grad_q, grad_k, grad_v, grad_o, wide, rows, sem):
    copies = [
        pltpu.make_async_copy(mix, mixed, sem.at[0]),
        pltpu.make_async_copy(gtb, gt, sem.at[1]),
    ]
    copies[0].start()
    copies[1].start()
    for n, out in enumerate((grad_q, grad_k, grad_v, grad_o)):
        half = pl.ds((n % 2) * (D // 8), D // 8)
        for j in range(2):
            val = red[n // 2, j, half].astype(F32).reshape(D, HD)
            if n < 3:
                wide[n, :, j * HD : (j + 1) * HD] = val
            else:
                for k in range(4):
                    rows[j * HD : (j + 1) * HD, k * HD : (k + 1) * HD] = val[k * HD : (k + 1) * HD]
        copies.append(pltpu.make_async_copy(wide.at[n] if n < 3 else rows, out, sem.at[2 + n]))
        copies[-1].start()
    for copy in copies:
        copy.wait()


def shards(table, cotangent, stamps, starts, w_query, w_key, w_value, w_out, decay):
    tm_size = lax.axis_size("tm")
    hbm = pl.BlockSpec(memory_space=pltpu.HBM)
    vmem = pl.BlockSpec(memory_space=pltpu.VMEM)
    dma = pltpu.SemaphoreType.DMA
    V = pltpu.VMEM
    near = (
        V((2, BLK, D), BF16),
        V((2, BLK, D), BF16),
        V((2, 2, 128, 8, 128), BF16),
    )
    near = pl.pallas_call(
        functools.partial(kernel, tm_size),
        out_shape=near,
        in_specs=[hbm] * 9,
        out_specs=(vmem, vmem, vmem),
        scratch_shapes=[
            V((3, BLK, D), BF16),
            V((D, WIN), BF16),
            V((BLK, D), BF16),
            V((2, BLK), jnp.int32),
            V((2, BLK), jnp.int32),
            pltpu.SMEM((1, 2), F32),
            V((2, 2, BLK), jnp.int32),
            V((8, 128), F32),
            V((8, 128), F32),
            V((2, D, BLK), BF16),
            V((2, D, BLK), BF16),
            V((2, D, BLK), BF16),
            V((2, BLK, D), BF16),
            V((BLK, WIN), F32),
            V((4, 1, WIN), F32),
            V((4, BLK, 2 * BLK), F32),
            V((4, BLK, 2 * BLK), F32),
            V((4, BLK, HD), BF16),
            V((4, HD, BLK), BF16),
            V((4, WIN, HD), BF16),
            V((4, WIN, HD), BF16),
            V((4, BLK, HD), BF16),
            V((4, HD, BLK), BF16),
            V((2, BLK, BLK), BF16),
            V((2, BLK, BLK), BF16),
            V((4, 2 * HD, WIN), BF16),
            V((2, 4, D, 128), BF16),
            V((2, 4, D, 128), BF16),
            V((2, 4, D, 128), F32),
            V((2, 2, 2 * D, 128), BF16),
            V((2, 2, D // 2, 128), BF16),
            V((2, 2, NZ, 8, 128), BF16),
            V((2, 2, D // 2, 128), F32),
            V((2, 2, D // 8, 128), F32),
            V((2, 2, 3, D // 2, 128), BF16),
            V((2, 2, 3, D // 8, 128), BF16),
            V((2, 2, 7, 8, 128), BF16),
            V((2, D, BLK), BF16),
            V((2, D, BLK), BF16),
            V((2, D, BLK), F32),
            dma((9,)),
            dma((4,)),
            dma((2 * CHUNKS + 2,)),
            dma((2,)),
            dma((2,)),
            dma((1,)),
            dma((2,)),
            dma((2, 3)),
            dma((2, 3)),
            dma((2, 3)),
            dma((2, 3)),
            dma((1,)),
            dma((2, 2)),
            dma((1,)),
            dma((1,)),
            pltpu.SemaphoreType.REGULAR((3,)),
        ],
        compiler_params=pltpu.CompilerParams(
            collective_id=0, has_side_effects=True, vmem_limit_bytes=58 * 1024 * 1024
        ),
        name="history_attention",
    )(table, cotangent, stamps, starts, w_query, w_key, w_value, w_out, decay.reshape(1, 2))
    shapes = ((2, BLK, D), (2, BLK, D), (D, BLK), (D, BLK), (D, BLK), (BLK, D))
    return pl.pallas_call(
        finish,
        out_shape=tuple(
            jax.ShapeDtypeStruct(shape, BF16 if n < 2 else F32) for n, shape in enumerate(shapes)
        ),
        in_specs=[vmem] * 3,
        out_specs=(hbm,) * 6,
        scratch_shapes=[V((3, D, BLK), F32), V((BLK, D), F32), dma((6,))],
        compiler_params=pltpu.CompilerParams(vmem_limit_bytes=16 * 1024 * 1024),
        name="finish",
    )(*near)


def solution(mesh):
    return jax.shard_map(
        shards,
        mesh=mesh,
        in_specs=(
            P(None, "tm", None),
            P(None, "tm", None),
            P(None, "tm"),
            P(None, "tm"),
            P(None, "rep"),
            P(None, "rep"),
            P(None, "rep"),
            P("rep", None),
            P("rep"),
        ),
        out_specs=(
            P(None, "tm", None),
            P(None, "tm", None),
            P(None, "rep"),
            P(None, "rep"),
            P(None, "rep"),
            P("rep", None),
        ),
        check_vma=False,
    )
```

```python
import functools
import math

import jax
import jax.numpy as jnp
from jax import lax
from jax.experimental import pallas as pl
from jax.experimental.pallas import tpu as pltpu
from jax.sharding import PartitionSpec as P

HD = 128
BLK = 256
WIN = 3 * BLK
D = 512
NX, NY, NZ = 4, 4, 8
CHUNKS = 8
LOG2E = 1.4426950408889634
MESH = pl.DeviceIdType.MESH
F32 = jnp.float32
BF16 = jnp.bfloat16
ORDERS = (("x", "y", "z"), ("y", "x", "z"))
SIZES = {"x": NX, "y": NY, "z": NZ}
FARTHEST = {4: (2, 1, 3), 8: (4, 3, 5, 2, 6, 1, 7)}


def nt(a, b):
    return lax.dot_general(a, b, (((1,), (1,)), ((), ())), preferred_element_type=F32)


def nn(a, b):
    return jnp.dot(a, b, preferred_element_type=F32)


def kernel(
    tm_size,
    table,
    cot,
    stamps,
    starts,
    wq_in,
    wk_in,
    wv_in,
    wo_in,
    decay,
    mix,
    gtb,
    red,
    xw,
    xT,
    g_s,
    ts_own,
    st_own,
    dec_in,
    ts_near,
    dec_send,
    dec_recv,
    wq,
    wk,
    wv,
    wo,
    mb,
    brow,
    s_pre,
    dp_pre,
    q_s,
    qT_s,
    k_s,
    v_s,
    do_s,
    doT_s,
    o_s,
    dq_s,
    kvT_s,
    psend,
    precv,
    pown,
    b0,
    b1,
    b2,
    b1_exact,
    b2_exact,
    rc0,
    rc1,
    rc2,
    ct_send,
    ct_recv,
    ct_own,
    lsem,
    hs,
    hr,
    ws,
    wr,
    ps,
    pr,
    rs_s,
    rs_r,
    ag_s,
    ag_r,
    cs,
    cr,
    ms,
    mr,
    met,
):
    tm = lax.axis_index("tm")
    c = lax.axis_index("rep")
    blocks = 2 * tm_size
    blk = c * (blocks - 1 - 2 * tm) + tm
    coord = {"x": tm // (NZ * NY), "z": (tm // NY) % NZ, "y": tm % NY}

    def holder(pos):
        side = pos // tm_size
        return (side * (blocks - 1 - 2 * pos) + pos, side)

    def partner(axis, d):
        at = dict(coord)
        at[axis] = (coord[axis] + SIZES[axis] + d) % SIZES[axis]
        return ((at["x"] * NZ + at["z"]) * NY + at["y"], c)

    next1 = holder((blk + 1) % blocks)
    pos1 = (blk + blocks - 1) % blocks
    pos2 = (blk + blocks - 2) % blocks
    prev1 = holder(pos1)
    sib = (tm, 1 - c)

    barrier = pltpu.get_barrier_semaphore()
    friends = [next1, prev1, sib]
    for axis in SIZES:
        friends += [partner(axis, 1), partner(axis, -1)]
    for friend in friends:
        pl.semaphore_signal(barrier, inc=1, device_id=friend, device_id_type=MESH)

    loads = [
        pltpu.make_async_copy(src, dst, lsem.at[n])
        for n, (src, dst) in enumerate(
            [
                (stamps, ts_own),
                (starts, st_own),
                (decay, dec_in),
                (table.at[c], xw.at[2]),
                (cot.at[c], g_s),
                (wq_in, wq.at[1]),
                (wk_in, wk.at[1]),
                (wv_in, wv.at[1]),
                (wo_in, wo.at[1]),
            ]
        )
    ]
    for copy in loads:
        copy.start()

    def remote(src, dst, send, recv, to):
        return pltpu.make_async_remote_copy(
            src_ref=src, dst_ref=dst, send_sem=send, recv_sem=recv, device_id=to, device_id_type=MESH
        )

    for copy in loads[:4]:
        copy.wait()
    pl.semaphore_wait(barrier, len(friends))

    def tell(token):
        axis, d, n = token
        pl.semaphore_signal(met.at[n], inc=1, device_id=partner(axis, d), device_id_type=MESH)

    tokens = ([("x", 1, 0), ("y", 1, 0), ("z", 1, 0), ("z", -1, 0)], [("z", 1, 1), ("z", -1, 1)], [("z", 1, 2)])

    def hear(n):
        pl.semaphore_wait(met.at[n], len(tokens[n]))

    chunk = BLK // CHUNKS
    pieces = [pl.ds(n * chunk, chunk) for n in range(CHUNKS)]
    mine = [
        remote(xw.at[2, rows], xw.at[1, rows], hs.at[0], hr.at[n], next1)
        for n, rows in enumerate(pieces)
    ]
    onward = [
        remote(xw.at[1, rows], xw.at[0, rows], hs.at[1], hr.at[CHUNKS + n], next1)
        for n, rows in enumerate(pieces)
    ]
    times = [
        remote(src, ts_near.at[n], hs.at[2 + n], hr.at[2 * CHUNKS + n], next1)
        for n, src in enumerate((stamps, ts_near.at[0]))
    ]
    weights = [
        remote(src.at[1], dst.at[0], ws.at[0], wr.at[0], sib)
        for n, (src, dst) in enumerate(((wq, wq), (wk, wk), (wv, wv), (wo, wo)))
    ]
    decays = remote(dec_send, dec_recv, ws.at[1], wr.at[1], sib)
    for copy in times[:1] + mine:
        copy.start()
    for token in tokens[0]:
        tell(token)
    sub = lax.broadcasted_iota(jnp.int32, (8, 128), 0)
    dec_send[...] = jnp.where(sub == 0, dec_in[0, 0], dec_in[0, 1])
    decays.start()
    first_row = jnp.where(c == 0, st_own[0:1, :], st_own[1:2, :]) - (blk - 2) * BLK
    first_col = jnp.transpose(jnp.broadcast_to(first_row.astype(F32), (128, BLK)))
    row_id = lax.broadcasted_iota(jnp.int32, (BLK, 128), 0)
    col_id = lax.broadcasted_iota(jnp.int32, (BLK, 128), 1)
    for n in range(WIN // 128):
        key_id = col_id + n * 128
        ok = (key_id.astype(F32) >= first_col) & (key_id <= row_id + 2 * BLK)
        mb[:, n * 128 : (n + 1) * 128] = jnp.where(ok, 0.0, -1e30)


    def begin(copies):
        for copy in copies:
            copy.start()

    def put_heads(dst, slot, rows, val):
        val = val.astype(BF16)
        for j in range(2):
            dst[2 * slot + j, rows, :] = val[:, j * HD : (j + 1) * HD]
        return val

    every = pl.ds(0, BLK)

    def own_rows(slot):
        x = xw[2]
        val = put_heads(q_s, slot, every, nn(x, wq[slot]))
        for j in range(2):
            qT_s[2 * slot + j] = jnp.transpose(val[:, j * HD : (j + 1) * HD])
        val = put_heads(do_s, slot, every, nt(g_s[...], wo[slot]))
        for j in range(2):
            doT_s[2 * slot + j] = jnp.transpose(val[:, j * HD : (j + 1) * HD])

    def keys_of(part, slot):
        rows = pl.ds(part * BLK, BLK)
        put_heads(k_s, slot, rows, nn(xw[part], wk[slot]))
        put_heads(v_s, slot, rows, nn(xw[part], wv[slot]))

    for copy in loads[4:]:
        copy.wait()
    begin(weights)
    own_rows(1)
    keys_of(2, 1)
    xT[:, 2 * BLK :] = jnp.transpose(xw[2])

    def side_row(ref, pos):
        return jnp.where(pos // tm_size == 0, ref[0:1, :], ref[1:2, :])

    own_times = side_row(ts_own, blk)
    base = jnp.max(own_times, axis=1, keepdims=True)
    inv_scale = 1.0 / math.sqrt(HD)

    def columns(part):
        return slice(part * BLK, (part + 1) * BLK)

    def decay_terms(part, times_row):
        rel = (times_row - base).astype(F32) * LOG2E
        for h in range(4):
            rate = (dec_recv, dec_send)[h // 2][h % 2 : h % 2 + 1, 0:1]
            brow[h, :, columns(part)] = rel * rate

    def scores(h, part):
        raw = nt(q_s[h], k_s[h, columns(part), :]) * (inv_scale * LOG2E)
        return raw + (mb[:, columns(part)] + brow[h, :, columns(part)])

    def early(h, part):
        s_pre[h, :, columns(part - 1)] = scores(h, part)
        dp_pre[h, :, columns(part - 1)] = nt(do_s[h], v_s[h, columns(part), :])

    all_weights = remote(psend, psend, ws.at[0], wr.at[0], sib)
    all_weights.wait_recv()
    decays.wait_recv()
    own_rows(0)
    keys_of(2, 0)
    decay_terms(2, own_times)
    times[0].wait_recv()
    times[1].start()
    hear(0)
    for token in tokens[1]:
        tell(token)
    for n in range(CHUNKS):
        mine[n].wait_recv()
        onward[n].start()
        if n % 2:
            early(n // 2, 2)
    hear(1)
    for token in tokens[2]:
        tell(token)
    keys_of(1, 1)
    keys_of(1, 0)
    xT[:, BLK : 2 * BLK] = jnp.transpose(xw[1])
    decay_terms(1, side_row(ts_near.at[0], pos1))
    for h in range(4):
        early(h, 1)
    hear(2)
    times[1].wait_recv()
    decay_terms(0, side_row(ts_near.at[1], pos2))
    for copy in onward:
        copy.wait_recv()
    keys_of(0, 0)
    keys_of(0, 1)
    xT[:, :BLK] = jnp.transpose(xw[0])

    psends = [
        remote(psend.at[j], precv.at[j], ps.at[0], pr.at[j], sib) for j in range(2)
    ]

    def products(t):
        return scores(t, 0), nt(do_s[t], v_s[t, :BLK, :])

    def softmax(t, s, dp):
        s = jnp.concatenate([s, s_pre[t]], axis=1)
        dp = jnp.concatenate([dp, dp_pre[t]], axis=1)
        p = jnp.exp2(s - jnp.max(s, axis=-1, keepdims=True))
        p = p * (1.0 / jnp.sum(p, axis=-1, keepdims=True))
        delta = jnp.sum(p * dp, axis=-1, keepdims=True)
        return p.astype(BF16), (p * (dp - delta)).astype(BF16)

    def attention(t, pb, ds):
        lanes = slice((t % 2) * HD, (t % 2 + 1) * HD)
        o_s[t // 2, :, lanes] = nn(pb, v_s[t]).astype(BF16)
        dq_s[t // 2, :, lanes] = (nn(ds, k_s[t]) * inv_scale).astype(BF16)
        kvT_s[t, :HD, :] = (nn(qT_s[t], ds) * inv_scale).astype(BF16)
        kvT_s[t, HD:, :] = nn(doT_s[t], pb).astype(BF16)

    def weight_grads(t):
        lanes = slice((t % 2) * HD, (t % 2 + 1) * HD)
        kv = nt(xT[...], kvT_s[t])
        go = nn(jnp.transpose(o_s[t // 2, :, lanes]), g_s[...])
        to = psend.at[t] if t < 2 else pown.at[t - 2]
        to[0] = nn(xT[:, 2 * BLK :], dq_s[t // 2, :, lanes]).astype(to.dtype)
        to[1] = kv[:, :HD].astype(to.dtype)
        to[2] = kv[:, HD:].astype(to.dtype)
        for n in range(4):
            to[3, n * HD : (n + 1) * HD, :] = go[:, n * HD : (n + 1) * HD].astype(to.dtype)

    def reduce_pair(j):
        psends[j].wait_recv()
        for n in range(4):
            b0[j, n // 2, (n % 2) * D : (n % 2 + 1) * D, :] = (pown[j, n] + precv[j, n].astype(F32)).astype(BF16)
        begin(scatters[j][0])

    def pass_on(step):
        if step in (0, 2):
            psends[step // 2].start()
        if step == 3:
            reduce_pair(1)
        if step in (1, 2):
            pl.when(c == step - 1)(lambda: reduce_pair(0))

    sources = (b0, b1, b2)
    landing = (rc0, rc1, rc2)
    exact = (b1_exact, b2_exact)
    rows_at = (2 * D, D // 2, D // 8)

    def place(stage, col):
        axis = ORDERS[col][stage]
        return axis, SIZES[axis], rows_at[stage] // SIZES[axis]

    def scatter(j, stage):
        copies = []
        for col in range(2):
            axis, size, piece = place(stage, col)
            for d in FARTHEST[size]:
                there = (coord[axis] + d) % size
                rows = there if stage == 2 else pl.ds(pl.multiple_of(there * piece, piece), piece)
                copies.append(
                    remote(
                        sources[stage].at[j, col, rows],
                        landing[stage].at[j, col, d - 1],
                        rs_s.at[j, stage],
                        rs_r.at[j, stage],
                        partner(axis, d),
                    )
                )
        return copies

    def gathered(j, stage, col):
        axis, size, piece = place(stage, col)
        if stage == 0:
            here = (2 * col + coord[axis] // 2, pl.ds(pl.multiple_of(coord[axis] % 2 * piece, piece), piece))
            total = pown[j, here[0], here[1], :] + precv[j, here[0], here[1], :].astype(F32)
        else:
            total = exact[stage - 1][j, col, pl.ds(pl.multiple_of(coord[axis] * piece, piece), piece), :]
        for d in range(1, size):
            total = total + landing[stage][j, col, d - 1].astype(F32)
        return total

    def first_owner(stage, col):
        owner = 0
        for s in range(stage + 1):
            axis, _, piece = place(s, col)
            owner = owner + coord[axis] * (piece // 8)
        return owner

    def spread(j, stage):
        copies = []
        for col in range(2):
            axis, size, piece = place(stage, col)
            here = pl.ds(first_owner(stage, col), piece // 8)
            for d in FARTHEST[size]:
                copies.append(
                    remote(
                        red.at[col, j, here],
                        red.at[col, j, here],
                        ag_s.at[j, stage],
                        ag_r.at[j, stage],
                        partner(axis, d),
                    )
                )
        return copies

    def spread_last(j):
        own, others = [], []
        for col in range(2):
            axis, size, _ = place(0, col)
            second, count, piece = place(1, col)
            base = coord[axis] * count
            for e in range(count):
                here = pl.ds((base + (coord[second] + e) % count) * (piece // 8), piece // 8)
                for d in FARTHEST[size]:
                    (others if e else own).append(
                        remote(
                            red.at[col, j, here],
                            red.at[col, j, here],
                            ag_s.at[j, 0],
                            ag_r.at[j, 0],
                            partner(axis, d),
                        )
                    )
        return own, others

    def whole_scatter(j, stage):
        ref = landing[stage].at[j]
        return remote(ref, ref, rs_s.at[j, stage], rs_r.at[j, stage], sib)

    def whole_spread(j, stage):
        _, size, piece = place(stage, 0)
        ref = red.at[:, j, pl.ds(0, (size - 1) * (piece // 8))]
        return remote(ref, ref, ag_s.at[j, stage], ag_r.at[j, stage], sib)

    scatters = [[scatter(j, stage) for stage in range(3)] for j in range(2)]
    spreads = [[None, spread(j, 1), spread(j, 2)] for j in range(2)]
    lasts = [spread_last(j) for j in range(2)]

    def arrived(copies):
        for copy in copies:
            copy.wait_recv()

    def next_scatter(j, stage):
        whole_scatter(j, stage).wait_recv()
        for col in range(2):
            if stage < 2:
                total = gathered(j, stage, col)
                exact[stage][j, col] = total
                if stage == 1:
                    total = total.reshape(NZ, 8, 128)
                sources[stage + 1][j, col] = total.astype(BF16)
            else:
                red[col, j, first_owner(2, col)] = (gathered(j, 2, col) * scale).astype(BF16)
        begin(scatters[j][stage + 1] if stage < 2 else spreads[j][2])

    def next_spread(j, stage):
        whole_spread(j, stage).wait_recv()
        if stage == 2:
            begin(spreads[j][1])
        begin(lasts[j][2 - stage])

    scale = 1.0 / math.sqrt(blocks * BLK)
    turn = (0, 2, 1, 3)
    now = products(turn[0])
    for step in range(4):
        later = products(turn[step + 1]) if step < 3 else None
        if step > 0:
            weight_grads(turn[step - 1])
        if step > 0:
            pass_on(step - 1)
        pb, ds = softmax(turn[step], *now)
        attention(turn[step], pb, ds)
        now = later
    weight_grads(turn[3])
    pass_on(3)

    mix[c] = (nn(o_s[0], wo[0]) + nn(o_s[1], wo[1])).astype(BF16)
    to_sib = [
        remote(ref.at[c], ref.at[c], ms.at[0], mr.at[0], sib) for n, ref in enumerate((mix, gtb))
    ]
    to_sib[0].start()
    for part in range(3):
        cols = slice(part * BLK, (part + 1) * BLK)
        total = jnp.zeros((D, BLK), F32)
        for t in range(4):
            lanes = slice((t % 2) * HD, (t % 2 + 1) * HD)
            both = jnp.concatenate([wk[t // 2, :, lanes], wv[t // 2, :, lanes]], axis=1)
            total = total + nn(both, kvT_s[t, :, cols])
        if part == 0:
            ct_send[0] = total.astype(BF16)
        else:
            ct_own[part - 1] = total
    terms = [
        [
            remote(ct_send.at[n, rows], ct_recv.at[n, rows], cs.at[0], cr.at[n, h], prev1)
            for h, rows in enumerate((every, pl.ds(BLK, BLK)))
        ]
        for n in range(2)
    ]

    next_scatter(0, 0)
    next_scatter(1, 0)
    gtq = nt(dq_s[0], wq[0]) + nt(dq_s[1], wq[1])
    next_scatter(0, 1)
    begin(terms[0])
    next_scatter(1, 1)
    next_scatter(0, 2)
    late = coord["y"] == (1 - c) * (NY - 1)

    def relay_terms():
        for h in range(2):
            terms[0][h].wait_recv()
            rows = slice(h * BLK, (h + 1) * BLK)
            ct_send[1, rows, :] = (ct_own[0, rows, :] + ct_recv[0, rows, :].astype(F32)).astype(BF16)
            terms[1][h].start()

    pl.when(jnp.logical_not(late))(relay_terms)
    next_scatter(1, 2)
    pl.when(late)(relay_terms)
    next_spread(0, 2)
    next_spread(1, 2)
    next_spread(0, 1)
    arrived(terms[1])
    gtb[c] = (gtq + jnp.transpose(ct_own[1] + ct_recv[1].astype(F32))).astype(BF16)
    to_sib[1].start()
    next_spread(1, 1)
    both = remote(mix, mix, ms.at[0], mr.at[0], sib)
    both.wait_recv()
    whole_spread(0, 0).wait_recv()
    whole_spread(1, 0).wait_recv()
    sent = [remote(xw.at[0], xw.at[0], hs.at[n], hr.at[n], next1) for n in range(2)]
    sent += times + [decays, all_weights, both]
    sent += [remote(psend, psend, ps.at[0], pr.at[0], sib)]
    sent += [remote(ct_send, ct_send, cs.at[0], cr.at[0, 0], prev1)]
    for j in range(2):
        for stage in range(3):
            sent += [whole_scatter(j, stage), whole_spread(j, stage)]
    for copy in sent:
        copy.wait_send()


def finish(mix, gtb, red, mixed, gt, grad_q, grad_k, grad_v, grad_o, wide, rows, sem):
    copies = [
        pltpu.make_async_copy(mix, mixed, sem.at[0]),
        pltpu.make_async_copy(gtb, gt, sem.at[1]),
    ]
    copies[0].start()
    copies[1].start()
    for n, out in enumerate((grad_q, grad_k, grad_v, grad_o)):
        half = pl.ds((n % 2) * (D // 8), D // 8)
        for j in range(2):
            val = red[n // 2, j, half].astype(F32).reshape(D, HD)
            if n < 3:
                wide[n, :, j * HD : (j + 1) * HD] = val
            else:
                for k in range(4):
                    rows[j * HD : (j + 1) * HD, k * HD : (k + 1) * HD] = val[k * HD : (k + 1) * HD]
        copies.append(pltpu.make_async_copy(wide.at[n] if n < 3 else rows, out, sem.at[2 + n]))
        copies[-1].start()
    for copy in copies:
        copy.wait()


def shards(table, cotangent, stamps, starts, w_query, w_key, w_value, w_out, decay):
    tm_size = lax.axis_size("tm")
    hbm = pl.BlockSpec(memory_space=pltpu.HBM)
    vmem = pl.BlockSpec(memory_space=pltpu.VMEM)
    dma = pltpu.SemaphoreType.DMA
    V = pltpu.VMEM
    near = (
        V((2, BLK, D), BF16),
        V((2, BLK, D), BF16),
        V((2, 2, 128, 8, 128), BF16),
    )
    near = pl.pallas_call(
        functools.partial(kernel, tm_size),
        out_shape=near,
        in_specs=[hbm] * 9,
        out_specs=(vmem, vmem, vmem),
        scratch_shapes=[
            V((3, BLK, D), BF16),
            V((D, WIN), BF16),
            V((BLK, D), BF16),
            V((2, BLK), jnp.int32),
            V((2, BLK), jnp.int32),
            pltpu.SMEM((1, 2), F32),
            V((2, 2, BLK), jnp.int32),
            V((8, 128), F32),
            V((8, 128), F32),
            V((2, D, BLK), BF16),
            V((2, D, BLK), BF16),
            V((2, D, BLK), BF16),
            V((2, BLK, D), BF16),
            V((BLK, WIN), F32),
            V((4, 1, WIN), F32),
            V((4, BLK, 2 * BLK), F32),
            V((4, BLK, 2 * BLK), F32),
            V((4, BLK, HD), BF16),
            V((4, HD, BLK), BF16),
            V((4, WIN, HD), BF16),
            V((4, WIN, HD), BF16),
            V((4, BLK, HD), BF16),
            V((4, HD, BLK), BF16),
            V((2, BLK, BLK), BF16),
            V((2, BLK, BLK), BF16),
            V((4, 2 * HD, WIN), BF16),
            V((2, 4, D, 128), BF16),
            V((2, 4, D, 128), BF16),
            V((2, 4, D, 128), F32),
            V((2, 2, 2 * D, 128), BF16),
            V((2, 2, D // 2, 128), BF16),
            V((2, 2, NZ, 8, 128), BF16),
            V((2, 2, D // 2, 128), F32),
            V((2, 2, D // 8, 128), F32),
            V((2, 2, 3, D // 2, 128), BF16),
            V((2, 2, 3, D // 8, 128), BF16),
            V((2, 2, 7, 8, 128), BF16),
            V((2, D, BLK), BF16),
            V((2, D, BLK), BF16),
            V((2, D, BLK), F32),
            dma((9,)),
            dma((4,)),
            dma((2 * CHUNKS + 2,)),
            dma((2,)),
            dma((2,)),
            dma((1,)),
            dma((2,)),
            dma((2, 3)),
            dma((2, 3)),
            dma((2, 3)),
            dma((2, 3)),
            dma((1,)),
            dma((2, 2)),
            dma((1,)),
            dma((1,)),
            pltpu.SemaphoreType.REGULAR((3,)),
        ],
        compiler_params=pltpu.CompilerParams(
            collective_id=0, has_side_effects=True, vmem_limit_bytes=58 * 1024 * 1024
        ),
        name="history_attention",
    )(table, cotangent, stamps, starts, w_query, w_key, w_value, w_out, decay.reshape(1, 2))
    shapes = ((2, BLK, D), (2, BLK, D), (D, BLK), (D, BLK), (D, BLK), (BLK, D))
    return pl.pallas_call(
        finish,
        out_shape=tuple(
            jax.ShapeDtypeStruct(shape, BF16 if n < 2 else F32) for n, shape in enumerate(shapes)
        ),
        in_specs=[vmem] * 3,
        out_specs=(hbm,) * 6,
        scratch_shapes=[V((3, D, BLK), F32), V((BLK, D), F32), dma((6,))],
        compiler_params=pltpu.CompilerParams(vmem_limit_bytes=16 * 1024 * 1024),
        name="finish",
    )(*near)


def solution(mesh):
    return jax.shard_map(
        shards,
        mesh=mesh,
        in_specs=(
            P(None, "tm", None),
            P(None, "tm", None),
            P(None, "tm"),
            P(None, "tm"),
            P(None, "rep"),
            P(None, "rep"),
            P(None, "rep"),
            P("rep", None),
            P("rep"),
        ),
        out_specs=(
            P(None, "tm", None),
            P(None, "tm", None),
            P(None, "rep"),
            P(None, "rep"),
            P(None, "rep"),
            P("rep", None),
        ),
        check_vma=False,
    )
```
